128 devices in a mesh: depth: 32 (over y, z, core), lat: 4 (over x).
Axes of the slice: x: 4, y: 4, z: 4, core: 2. Of those that a mesh axis runs over, the one named last changes fastest.
Arguments:
- density: bfloat16 [32, 16, 512, 2048], P('depth', None, None, 'lat'), may hold values from 0 to 1
- occupancy: int32 [32, 4, 16], P('depth', None, 'lat'), may hold values from 0 to 1, as said below
- shear_offsets: int32 [32, 16], P('depth'), may hold values from 0 to 127, as said below
- frac_lateral: float32 [32, 16], P('depth'), may hold values from 0.05 to 0.95
- frac_vertical: float32 [32, 16], P('depth'), may hold values from 0.05 to 0.95
- extinction: float32 [32, 16], P('depth'), may hold values from 2 to 32
- slab_gain: float32 [32], P('depth'), may hold values from 0.05 to 1
- view_rank: int32 [32], replicated, may hold values from 0 to 31, as said below
Outputs:
- image_color: float32 [512, 2048], P('depth', 'lat')
- image_alpha: float32 [512, 2048], P('depth', 'lat')
The draws below stay inside these ranges and needn't reach their ends.
Inputs may be any that keep to these rules, and one draw needn't show every extreme that they name: `occupancy`: A block is 1 if occupied; the share of occupied blocks differs from slab to slab. `shear_offsets`: some slice has the offset 128 - 1. `view_rank`: A permutation of the slabs in which every aligned group of a power of two of slabs holds consecutive ranks.
All inputs are finite; a program needn't handle non-finite values.
Results may differ from the reference program's by a relative error of at most 0.00077.
Values may be sent and summed in bfloat16 or wider, within the bound.
No kernel may reach another device: no remote copies, remote signals or barrier semaphores. Data moves between devices by JAX's collectives and lax.ppermute only.
A program may use at most 128 MiB of HBM per device.

```python
import math
import jax
import jax.numpy as jnp
from jax import lax

SL = 16
ROWS = 512
WID = 512
SHIFT = 128
BLK = 128
SLABS = 32
NBR = 4
IMGW = 2048
N_LAT = 4


def draw_occupancy(key, part):
    level_key = jax.random.fold_in(key, 11)
    cell_key = jax.random.fold_in(key, 12)
    fill_level = jax.random.randint(level_key, (SLABS, 1, 1), 1, 9)
    cells = jax.random.randint(cell_key, (SLABS, NBR, IMGW // BLK), 0, 8)
    return (cells < fill_level).astype(jnp.int32)


def draw_shear_offsets(key, part):
    value_key = jax.random.fold_in(key, 21)
    place_key = jax.random.fold_in(key, 22)
    values = jax.random.randint(value_key, (SLABS * SL,), 0, SHIFT)
    where_max = jax.random.randint(place_key, (), 0, SLABS * SL)
    values = values.at[where_max].set(SHIFT - 1)
    return values.reshape(SLABS, SL).astype(jnp.int32)


def draw_view_rank(key, part):
    flip_key = jax.random.fold_in(key, 31)
    level_count = SLABS.bit_length() - 1
    flip_table = jax.random.randint(flip_key, (level_count, SLABS), 0, 2).astype(jnp.int32)
    slab_index = jnp.arange(SLABS, dtype=jnp.int32)
    ranks = jnp.zeros((SLABS,), jnp.int32)
    for level in range(level_count):
        node = jnp.right_shift(slab_index, level + 1)
        flip_bit = flip_table[level][node]
        own_bit = jnp.bitwise_and(jnp.right_shift(slab_index, level), 1)
        ranks = ranks + jnp.left_shift(jnp.bitwise_xor(own_bit, flip_bit), level)
    return ranks.astype(jnp.int32)


def level_of(rng, shape, pieces, low, high):
    def one(position, shards_of):
        steps = jax.random.uniform(jax.random.fold_in(jax.random.fold_in(rng, 6), position), (shards_of,), jnp.float32, low / len(pieces), high / len(pieces))
        return jnp.repeat(jnp.exp(steps), shape[position] // shards_of).reshape((-1,) + (1,) * (len(shape) - position - 1))

    level = one(*pieces[0])
    for cut in pieces[1:]:
        level = level * one(*cut)
    return level


def setup_inputs(seed: int = 0) -> dict:
    arg_keys = jax.random.split(jax.random.key(seed), 9)
    density = jnp.clip(1.0 * jax.random.uniform(arg_keys[0], (SLABS, SL, ROWS, IMGW), jnp.float32) ** level_of(arg_keys[0], (SLABS, SL, ROWS, IMGW), ((0, 32), (3, 4)), -0.2, 0.2), 0.0, 1.0).astype(jnp.bfloat16)
    occupancy = draw_occupancy(jax.random.fold_in(arg_keys[8], 71), 0)
    shear_offsets = draw_shear_offsets(jax.random.fold_in(arg_keys[8], 71), 0)
    frac_lateral = jnp.clip(0.05 + 0.9 * jax.random.uniform(arg_keys[3], (SLABS, SL), jnp.float32) ** level_of(arg_keys[3], (SLABS, SL), ((0, 32),), -0.2, 0.2), 0.05, 0.95)
    frac_vertical = jnp.clip(0.05 + 0.9 * jax.random.uniform(arg_keys[4], (SLABS, SL), jnp.float32) ** level_of(arg_keys[4], (SLABS, SL), ((0, 32),), -0.2, 0.2), 0.05, 0.95)
    extinction = jnp.clip(jnp.exp(math.log(32.0) - 2.7725887 * jax.random.uniform(arg_keys[5], (SLABS, SL), jnp.float32) ** level_of(arg_keys[5], (SLABS, SL), ((0, 32),), -0.2, 0.2)), 2.0, 32.0)
    slab_gain = jnp.clip(jnp.exp(math.log(1.0) - 2.9957323 * jax.random.uniform(arg_keys[6], (SLABS,), jnp.float32) ** level_of(arg_keys[6], (SLABS,), ((0, 32),), -0.2, 0.2)), 0.05, 1.0)
    view_rank = draw_view_rank(jax.random.fold_in(arg_keys[8], 71), 0)
    return {"density": density, "occupancy": occupancy, "shear_offsets": shear_offsets, "frac_lateral": frac_lateral, "frac_vertical": frac_vertical, "extinction": extinction, "slab_gain": slab_gain, "view_rank": view_rank}


def lateral_weights(offsets, fraction, in_count, out_count):
    source = jnp.arange(in_count, dtype=jnp.int32)[None, :, None]
    target = jnp.arange(out_count, dtype=jnp.int32)[None, None, :]
    shifted = target - offsets[:, None, None]
    first_term = jnp.where(shifted == source, (1.0 - fraction)[:, None, None], 0.0)
    second = jnp.where(shifted - 1 == source, fraction[:, None, None], 0.0)
    return (first_term + second).astype(jnp.bfloat16)


def vertical_weights(fraction, row_count):
    target = jnp.arange(row_count, dtype=jnp.int32)[None, :, None]
    source = jnp.arange(row_count, dtype=jnp.int32)[None, None, :]
    first_term = jnp.where(target == source, (1.0 - fraction)[:, None, None], 0.0)
    second = jnp.where(target - 1 == source, fraction[:, None, None], 0.0)
    return (first_term + second).astype(jnp.bfloat16)


def shade_slices(density_sum, extinction, gain, slice_total):
    row_above = jnp.pad(density_sum, ((0, 0), (1, 0), (0, 0)))[:, :-1, :]
    shading = 0.3 + 0.7 * jax.nn.sigmoid(4.0 * (density_sum - row_above))
    opacity = 1.0 - jnp.exp(-extinction[:, None, None] * density_sum / slice_total)
    emission = opacity * shading * gain
    through = jnp.cumprod(1.0 - opacity, axis=0)
    before = jnp.concatenate([jnp.ones_like(through[:1]), through[:-1]], axis=0)
    return jnp.sum(emission * before, axis=0), 1.0 - through[-1]


def reference(density, occupancy, shear_offsets, frac_lateral, frac_vertical, extinction, slab_gain, view_rank):
    def one_slab(slab_items):
        slab_voxels, occ_blocks, offsets, lateral_frac, vertical_frac, slab_ext, gain = slab_items
        block_mask = jnp.repeat(jnp.repeat(occ_blocks, BLK, axis=0), BLK, axis=1).astype(jnp.bfloat16)
        masked = (slab_voxels * block_mask[None]).reshape(SL, ROWS, N_LAT, WID)
        lateral_matrix = lateral_weights(offsets, lateral_frac, WID, WID + SHIFT)
        across = jnp.einsum('srbw,swq->srbq', masked.astype(jnp.float32), lateral_matrix.astype(jnp.float32)).astype(jnp.bfloat16)
        vertical_matrix = vertical_weights(vertical_frac, ROWS)
        resampled = jnp.einsum('sij,sjbq->sibq', vertical_matrix.astype(jnp.float32), across.astype(jnp.float32)).astype(jnp.bfloat16)
        local_part = resampled[..., :WID].astype(jnp.float32)
        edge_spill = resampled[..., WID:].astype(jnp.float32)
        incoming = jnp.concatenate([jnp.zeros_like(edge_spill[:, :, :1]), edge_spill[:, :, :-1]], axis=2)
        incoming = jnp.pad(incoming, ((0, 0), (0, 0), (0, 0), (0, WID - SHIFT)))
        density_sum = (local_part + incoming).reshape(SL, ROWS, N_LAT * WID)
        return shade_slices(density_sum, slab_ext, gain, SLABS * SL)

    slab_colors, slab_alphas = lax.map(one_slab, (density, occupancy, shear_offsets, frac_lateral, frac_vertical, extinction, slab_gain))
    view_order = jnp.argsort(view_rank)
    slab_colors = slab_colors[view_order]
    slab_alphas = slab_alphas[view_order]

    def composite(running, slab_pair):
        run_color, run_alpha = running
        next_color, next_alpha = slab_pair
        return (run_color + (1.0 - run_alpha) * next_color, run_alpha + (1.0 - run_alpha) * next_alpha), None

    start = (jnp.zeros(slab_colors.shape[1:], slab_colors.dtype), jnp.zeros(slab_alphas.shape[1:], slab_alphas.dtype))
    (image_color, image_alpha), _ = lax.scan(composite, start, (slab_colors, slab_alphas))
    return image_color, image_alpha
```

```python
import functools
import math

import jax
import jax.numpy as jnp
from jax import lax
from jax.experimental import pallas as pl
from jax.experimental.pallas import tpu as pltpu
from jax.sharding import PartitionSpec as P

SHIFT = 128
BLK = 128
HALF = SHIFT // 2
LANES = 128
PIECE = 16
WIRE = jnp.float32
LOG2E = math.log2(math.e)
SMEM = pltpu.SMEM
F32 = jnp.float32
BF16 = jnp.bfloat16


def rounded(scalar, shape):
    return jnp.full(shape, scalar, F32).astype(BF16).astype(F32)


def tap(distance, offset, fraction):
    second = jnp.where(distance == offset + 1, fraction, 0.0)
    return jnp.where(distance == offset, 1.0 - fraction, second)


def strips_kernel(occ, x_first, x_last, to_left, to_right):
    chunk = pl.program_id(0)
    half = x_first.shape[2] // 2
    k = lax.broadcasted_iota(jnp.int32, (2 * LANES, LANES), 0)
    n = lax.broadcasted_iota(jnp.int32, (2 * LANES, LANES), 1)
    take = jnp.where(n < HALF, n, n + HALF)
    for ref, out, first, column in (
        (x_first, to_left, 0, 0),
        (x_last, to_right, HALF, occ.shape[2] - 1),
    ):
        low = occ[0, 2 * chunk, column].astype(F32)
        high = occ[0, 2 * chunk + 1, column].astype(F32)
        if first == 0:
            source = take
            pick = jnp.where(k == source, jnp.where(n < HALF, low, high), 0.0)
        else:
            source = jnp.where(n < HALF, n + LANES + HALF, n)
            pick = jnp.where(k == source, jnp.where(n < HALF, high, low), 0.0)
        pick = pick.astype(BF16)
        for s in range(ref.shape[1]):
            rows = jnp.concatenate([ref[0, s, :half], ref[0, s, half:]], axis=1)
            out[0, s] = jnp.dot(rows, pick, preferred_element_type=F32).astype(BF16)


def edge_strips(density, occupancy, chunks):
    _, slices, rows, cols = density.shape
    step = rows // chunks
    shape = jax.ShapeDtypeStruct((chunks, slices, step // 2, LANES), BF16)
    last = cols // LANES - 1
    return pl.pallas_call(
        strips_kernel,
        grid=(chunks,),
        in_specs=[
            pl.BlockSpec(memory_space=SMEM),
            pl.BlockSpec((1, slices, step, LANES), lambda c: (0, 0, c, 0)),
            pl.BlockSpec((1, slices, step, LANES), lambda c: (0, 0, c, last)),
        ],
        out_specs=[pl.BlockSpec((1, slices, step // 2, LANES), lambda c: (c, 0, 0, 0))] * 2,
        out_shape=[shape, shape],
        name="edge_strips",
    )(occupancy, density, density)


def shade(s, x, base, state, refs, first_row):
    frac_vertical, extinction, slice_total = refs
    through_ref, sum_ref = state
    rows = x.shape[0]
    v0 = 2.0 * rounded(1.0 - frac_vertical[0, s], (1, LANES))
    v1 = 2.0 * rounded(frac_vertical[0, s], (1, LANES))
    density = v0 * x + v1 * pltpu.roll(x, 1, 0)
    above = pltpu.roll(density, 1, 0)
    density, above = density[8:], above[8:]
    rate = extinction[0, s] * (-LOG2E / (2.0 * slice_total))
    kept = jnp.exp2(rate * density)
    slope = jnp.tanh(density - above)
    through = through_ref[base : base + rows - 8]
    after = through * kept
    through_ref[base : base + rows - 8] = after
    sum_ref[base : base + rows - 8] += (through - after) * slope


def finish(state, gain, swap, out_keep, out_send, tile):
    through_ref, sum_ref = state
    rows = out_keep.shape[1] * 2
    base = tile * rows
    alphas, colors = [], []
    for p in range(rows // PIECE):
        at = slice(base + p * PIECE, base + (p + 1) * PIECE)
        alpha = 1.0 - through_ref[at]
        alphas.append(alpha)
        colors.append(gain * (0.65 * alpha + 0.35 * sum_ref[at]))
    lanes = slice(tile * LANES, (tile + 1) * LANES)
    for q in range(rows // PIECE // 2):
        at = slice(q * PIECE, (q + 1) * PIECE)
        for i, values in enumerate((colors, alphas)):
            even, odd = values[2 * q], values[2 * q + 1]
            out_keep[i, at, lanes] = jnp.where(swap, odd, even)
            out_send[i, at, lanes] = jnp.where(swap, even, odd).astype(out_send.dtype)


def interior_kernel(
    slice_total, occ, offset, frac_lateral, frac_vertical, extinction, gain,
    x_ref, lead_ref, out_keep, out_send, weights, through_ref, sum_ref,
):
    block = pl.program_id(0)
    slices, rows = x_ref.shape[1], x_ref.shape[2]
    tiles = x_ref.shape[3] // LANES

    @pl.when(block == 0)
    def _():
        k = lax.broadcasted_iota(jnp.int32, (2 * LANES, LANES), 0)
        n = lax.broadcasted_iota(jnp.int32, (2 * LANES, LANES), 1)

        def build(s, _):
            weights[s] = tap(LANES + n - k, offset[0, s], frac_lateral[0, s]).astype(BF16)
            return 0

        lax.fori_loop(0, slices, build, 0)

    through_ref[...] = jnp.ones_like(through_ref)
    sum_ref[...] = jnp.zeros_like(sum_ref)
    inside = jnp.where(block > 0, 1, 0)
    above = jnp.maximum(block - 1, 0)
    mask = [jnp.full((1, LANES), occ[0, block, t], F32).astype(BF16) for t in range(tiles)]
    lead_mask = [
        jnp.full((1, LANES), occ[0, above, t] * inside, F32).astype(BF16) for t in range(tiles)
    ]
    state = (through_ref, sum_ref)

    def one(s, _):
        parts = []
        for t in range(tiles):
            lanes = slice(t * LANES, (t + 1) * LANES)
            parts.append(
                jnp.concatenate(
                    [lead_ref[0, s, :, lanes] * lead_mask[t], x_ref[0, s, :, lanes] * mask[t]],
                    axis=0,
                )
            )
        for t in range(1, tiles):
            pair = jnp.concatenate([parts[t - 1], parts[t]], axis=1)
            x = jnp.dot(pair, weights[s], preferred_element_type=F32)
            shade(
                s, x[8:], (t - 1) * rows, state,
                (frac_vertical, extinction, slice_total), rows,
            )
        return 0

    lax.fori_loop(0, slices, one, 0)
    swap = lax.axis_index("depth") % 2 == 1
    for t in range(tiles - 1):
        finish(state, gain[0], swap, out_keep, out_send, t)


def small_specs():
    return [pl.BlockSpec(memory_space=SMEM)] * 6


def interior(density, small, slice_total):
    _, slices, rows, cols = density.shape
    step = BLK
    width = cols - LANES
    return pl.pallas_call(
        functools.partial(interior_kernel, slice_total),
        grid=(rows // step,),
        in_specs=small_specs()
        + [
            pl.BlockSpec((1, slices, step, cols), lambda b: (0, 0, b, 0)),
            pl.BlockSpec(
                (1, slices, 16, cols), lambda b: (0, 0, jnp.maximum(b * (step // 16) - 1, 0), 0)
            ),
        ],
        out_specs=[pl.BlockSpec((2, step // 2, width), lambda b: (0, b, 0))] * 2,
        out_shape=[
            jax.ShapeDtypeStruct((2, rows // 2, width), F32),
            jax.ShapeDtypeStruct((2, rows // 2, width), F32),
        ],
        scratch_shapes=[
            pltpu.VMEM((slices, 2 * LANES, LANES), BF16),
            pltpu.VMEM((step * (cols // LANES - 1), LANES), F32),
            pltpu.VMEM((step * (cols // LANES - 1), LANES), F32),
        ],
        compiler_params=pltpu.CompilerParams(vmem_limit_bytes=40 * 2**20),
        name="interior",
    )(*small, density, density)


def border_kernel(
    chunk, slice_total, occ, offset, frac_lateral, frac_vertical, extinction, gain,
    first_ref, last_ref, first_lead, last_lead, right_ref, left_ref, right_lead, left_lead,
    out_keep, out_send, weights, through_ref, sum_ref,
):
    half = pl.program_id(0)
    block = 2 * chunk + half
    slices, rows = first_ref.shape[1], first_ref.shape[2]
    last_tile = occ.shape[2] - 1
    follows = jnp.where(lax.axis_index("lat") < lax.axis_size("lat") - 1, 1, 0)

    @pl.when(half == 0)
    def _():
        k = lax.broadcasted_iota(jnp.int32, (LANES, LANES), 0)
        n = lax.broadcasted_iota(jnp.int32, (LANES, LANES), 1)
        far = 1 << 20
        own = jnp.where(n >= HALF, n - k, far)
        before = jnp.where(n < HALF, LANES + n - k, far)
        swapped = jnp.where(k < HALF, k + HALF, k - HALF)

        def build(s, _):
            o, f = offset[0, s], frac_lateral[0, s]
            w_own = tap(own, o, f)
            w_before = tap(before, o, f)
            for v, kk in enumerate((k, swapped)):
                right = jnp.where((kk < HALF) & (n < HALF), n - kk, far)
                left = jnp.where((kk >= HALF) & (n >= HALF), LANES + n - kk, far)
                weights[v, s, 0:LANES] = w_own.astype(BF16)
                weights[v, s, LANES : 2 * LANES] = w_before.astype(BF16)
                weights[v, s, 2 * LANES : 3 * LANES] = tap(right, o, f).astype(BF16)
                weights[v, s, 3 * LANES :] = tap(left, o, f).astype(BF16)
            return 0

        lax.fori_loop(0, slices, build, 0)

    through_ref[...] = jnp.ones_like(through_ref)
    sum_ref[...] = jnp.zeros_like(sum_ref)
    inside = jnp.where(block > 0, 1, 0)
    above = jnp.maximum(block - 1, 0)

    def splat(value):
        return jnp.full((1, LANES), value, F32).astype(BF16)

    mask_first = splat(occ[0, block, 0])
    mask_last = splat(occ[0, block, last_tile] * follows)
    lead_first = splat(occ[0, above, 0] * inside)
    lead_last = splat(occ[0, above, last_tile] * follows * inside)
    lead_halo = splat(inside)
    state = (through_ref, sum_ref)

    def one(s, _):
        lead = jnp.concatenate(
            [
                first_lead[0, s] * lead_first,
                last_lead[0, s] * lead_last,
                right_lead[0, s] * lead_halo,
                left_lead[0, s] * lead_halo,
            ],
            axis=1,
        )
        main = jnp.concatenate(
            [first_ref[0, s] * mask_first, last_ref[0, s] * mask_last, right_ref[0, s], left_ref[0, s]],
            axis=1,
        )
        x_lead = jnp.dot(lead, weights[1 - half, s], preferred_element_type=F32)
        x_main = jnp.dot(main, weights[half, s], preferred_element_type=F32)
        x = jnp.concatenate([x_lead[8:], x_main], axis=0)
        shade(s, x, 0, state, (frac_vertical, extinction, slice_total), rows)
        return 0

    lax.fori_loop(0, slices, one, 0)
    swap = lax.axis_index("depth") % 2 == 1
    finish(state, gain[0], swap, out_keep, out_send, 0)


def border(density, small, halos, previous, chunk, chunks, slice_total):
    _, slices, rows, cols = density.shape
    step = BLK
    last = cols // LANES - 1
    first_block = 2 * chunk
    per = step // 16

    def body(column):
        return pl.BlockSpec((1, slices, step, LANES), lambda b: (0, 0, first_block + b, column))

    def lead(column):
        return pl.BlockSpec(
            (1, slices, 16, LANES),
            lambda b: (0, 0, jnp.maximum((first_block + b) * per - 1, 0), column),
        )

    halo = pl.BlockSpec((1, slices, step, LANES), lambda b: (0, 0, 0, 0))
    halo_lead = pl.BlockSpec((1, slices, 16, LANES), lambda b: (b, 0, 0, 0))
    right, left = halos
    leads = [
        jnp.concatenate([p[:, :, -16:], h[:, :, -16:]], axis=0) for p, h in zip(previous, halos)
    ]
    return pl.pallas_call(
        functools.partial(border_kernel, chunk, slice_total),
        grid=(2,),
        in_specs=small_specs()
        + [body(0), body(last), lead(0), lead(last), halo, halo, halo_lead, halo_lead],
        out_specs=[pl.BlockSpec((2, step // 2, LANES), lambda b: (0, b, 0))] * 2,
        out_shape=[
            jax.ShapeDtypeStruct((2, step, LANES), F32),
            jax.ShapeDtypeStruct((2, step, LANES), F32),
        ],
        scratch_shapes=[
            pltpu.VMEM((2, slices, 4 * LANES, LANES), BF16),
            pltpu.VMEM((step, LANES), F32),
            pltpu.VMEM((step, LANES), F32),
        ],
        compiler_params=pltpu.CompilerParams(vmem_limit_bytes=40 * 2**20),
        name=f"border{chunk}",
    )(*small, density, density, density, density, right, left, *leads)


def over(a, b, a_in_front):
    color = jnp.where(a_in_front, a[0], b[0]) + (
        1.0 - jnp.where(a_in_front, a[1], b[1])
    ) * jnp.where(a_in_front, b[0], a[0])
    return color, a[1] + (1.0 - a[1]) * b[1]


def load(ref, at):
    return ref[0, at].astype(F32), ref[1, at].astype(F32)


def merge_pair_kernel(rank, mine, other, own, *sends):
    me = lax.axis_index("depth")
    z = (me // 2) % 4
    front = rank[me] < rank[jnp.bitwise_xor(me, 1)]
    for k, out in enumerate((own,) + sends):
        target = jnp.bitwise_xor(z, k)
        for y in range(mine.shape[1] // (4 * PIECE)):
            at = pl.ds(pl.multiple_of((4 * y + target) * PIECE, PIECE), PIECE)
            color, alpha = over(load(mine, at), load(other, at), front)
            out[0, y * PIECE : (y + 1) * PIECE] = color.astype(out.dtype)
            out[1, y * PIECE : (y + 1) * PIECE] = alpha.astype(out.dtype)


def four(rank, stride, parts, at):
    me = lax.axis_index("depth")
    ranks = [rank[jnp.bitwise_xor(me, stride * k)] for k in range(4)]
    values = [load(ref, at) for ref in parts]
    low = over(values[0], values[1], ranks[0] < ranks[1])
    high = over(values[2], values[3], ranks[2] < ranks[3])
    return over(low, high, ranks[0] < ranks[2])


def merge_z_kernel(rank, p0, p1, p2, p3, own, *sends):
    y = lax.axis_index("depth") // 8
    for k, out in enumerate((own,) + sends):
        target = jnp.bitwise_xor(y, k)
        at = pl.ds(pl.multiple_of(target * PIECE, PIECE), PIECE)
        color, alpha = four(rank, 2, (p0, p1, p2, p3), at)
        out[0] = color.astype(out.dtype)
        out[1] = alpha.astype(out.dtype)


def vmem_call(kernel, outs, name, rank, *arrays):
    return pl.pallas_call(
        kernel,
        in_specs=[pl.BlockSpec(memory_space=SMEM)]
        + [pl.BlockSpec(memory_space=pltpu.VMEM)] * len(arrays),
        out_specs=[pl.BlockSpec(memory_space=pltpu.VMEM)] * len(outs),
        out_shape=outs,
        name=name,
    )(rank, *arrays)


def depth_swap(value, bits):
    count = lax.axis_size("depth")
    return lax.ppermute(value, "depth", [(i, i ^ bits) for i in range(count)])


def depth_and_lat(value, bits, step):
    depth, lat = lax.axis_size("depth"), lax.axis_size("lat")
    pairs = [
        (i * lat + x, (i ^ bits) * lat + (x + step) % lat) for i in range(depth) for x in range(lat)
    ]
    return lax.ppermute(value, ("depth", "lat"), pairs)


def over_depth(keep, send, rank, name):
    width = keep.shape[2]
    other = depth_swap(send, 1)
    part = (2, keep.shape[1] // 4, width)
    outs = [jax.ShapeDtypeStruct(part, F32)] + [jax.ShapeDtypeStruct(part, WIRE)] * 3
    own, *sends = vmem_call(merge_pair_kernel, outs, f"cores_{name}", rank, keep, other)
    received = [depth_swap(v, 2 * (k + 1)) for k, v in enumerate(sends)]
    part = (2, PIECE, width)
    outs = [jax.ShapeDtypeStruct(part, F32)] + [jax.ShapeDtypeStruct(part, WIRE)] * 3
    return vmem_call(merge_z_kernel, outs, f"chips_z_{name}", rank, own, *received)


def final_kernel(rank, *refs):
    inner, near, moved = refs[:4], refs[4:8], refs[8:12]
    out_color, out_alpha = refs[12:]
    everything = slice(None)
    color, alpha = four(rank, 8, inner, everything)
    out_color[:, LANES:] = color
    out_alpha[:, LANES:] = alpha
    here = four(rank, 8, near, everything)
    there = four(rank, 8, moved, everything)
    lane = lax.broadcasted_iota(jnp.int32, here[0].shape, 1)
    out_color[:, :LANES] = jnp.where(lane < HALF, there[0], here[0])
    out_alpha[:, :LANES] = jnp.where(lane < HALF, there[1], here[1])


def shards(
    density, occupancy, shear_offsets, frac_lateral, frac_vertical, extinction, slab_gain, view_rank
):
    _, slices, rows, cols = density.shape
    slice_total = lax.axis_size("depth") * slices
    lat = lax.axis_size("lat")
    small = (occupancy, shear_offsets, frac_lateral, frac_vertical, extinction, slab_gain)
    chunks = rows // (2 * BLK)
    to_left, to_right = edge_strips(density, occupancy, chunks)
    rightwards = [(x, x + 1) for x in range(lat - 1)]
    leftwards = [(x, (x - 1) % lat) for x in range(lat)]
    halos = []
    for c in range(chunks):
        from_right = lax.ppermute(to_left[c : c + 1], "lat", leftwards)
        from_left = lax.ppermute(to_right[c : c + 1], "lat", rightwards)
        halos.append((from_right, from_left))
    keep, send = interior(density, small, slice_total)
    inner = over_depth(keep, send, view_rank, "inner")
    inner = [inner[0]] + [depth_swap(v, 8 * (k + 1)) for k, v in enumerate(inner[1:])]
    keeps, sends = [], []
    for c in range(chunks):
        k, s = border(density, small, halos[c], halos[max(c - 1, 0)], c, chunks, slice_total)
        keeps.append(k)
        sends.append(s)
    keep = jnp.concatenate(keeps, axis=1)
    send = jnp.concatenate(sends, axis=1)
    edge = over_depth(keep, send, view_rank, "edge")
    near = [edge[0]] + [depth_swap(v, 8 * (k + 1)) for k, v in enumerate(edge[1:])]
    moved = [depth_and_lat(v.astype(WIRE), 8 * k, 1) for k, v in enumerate(edge)]
    out = jax.ShapeDtypeStruct((PIECE, cols), F32)
    return tuple(
        vmem_call(final_kernel, [out, out], "chips_y", view_rank, *inner, *near, *moved)
    )


def solution(mesh):
    placed = (
        P("depth", None, None, "lat"),
        P("depth", None, "lat"),
        P("depth", None),
        P("depth", None),
        P("depth", None),
        P("depth", None),
        P("depth"),
        P(),
    )
    return jax.shard_map(
        shards,
        mesh=mesh,
        in_specs=placed,
        out_specs=(P("depth", "lat"), P("depth", "lat")),
        check_vma=False,
    )
```

```python
import functools
import math

import jax
import jax.numpy as jnp
from jax import lax
from jax.experimental import pallas as pl
from jax.experimental.pallas import tpu as pltpu
from jax.sharding import PartitionSpec as P

SHIFT = 128
BLK = 128
HALF = SHIFT // 2
LANES = 128
PIECE = 16
WIRE = jnp.float16
WIRE_SCALE = 4096.0
UNROLL = 4
LOG2E = math.log2(math.e)
SMEM = pltpu.SMEM
F32 = jnp.float32
BF16 = jnp.bfloat16


def rounded(scalar, shape):
    return jnp.full(shape, scalar, F32).astype(BF16).astype(F32)


def tap(distance, offset, fraction):
    second = jnp.where(distance == offset + 1, fraction, 0.0)
    return jnp.where(distance == offset, 1.0 - fraction, second)


def strips_kernel(chunk, occ, x_first, x_last, to_left, to_right):
    half = x_first.shape[2] // 2
    k = lax.broadcasted_iota(jnp.int32, (2 * LANES, LANES), 0)
    n = lax.broadcasted_iota(jnp.int32, (2 * LANES, LANES), 1)
    blocks = x_first.shape[2] // BLK
    first, last = 0, occ.shape[2] - 1
    for ref, out, column, source, near in (
        (x_first, to_left, first, jnp.where(n < HALF, n, n + HALF), n < HALF),
        (x_last, to_right, last, jnp.where(n < HALF, n + LANES + HALF, n), n >= HALF),
    ):
        low = occ[0, blocks * chunk, column].astype(F32)
        high = occ[0, blocks * chunk + 1, column].astype(F32)
        pick = jnp.where(k == source, jnp.where(near, low, high), 0.0).astype(BF16)
        for s in range(ref.shape[1]):
            rows = jnp.concatenate([ref[0, s, :half], ref[0, s, half:]], axis=1)
            out[s] = jnp.dot(rows, pick, preferred_element_type=F32).astype(BF16)


def edge_strips(density, occupancy, chunk):
    _, slices, _, cols = density.shape
    step = 2 * BLK
    shape = jax.ShapeDtypeStruct((slices, step // 2, LANES), BF16)
    last = cols // LANES - 1
    return pl.pallas_call(
        functools.partial(strips_kernel, chunk),
        grid=(1,),
        in_specs=[
            pl.BlockSpec(memory_space=SMEM),
            pl.BlockSpec((1, slices, step, LANES), lambda i: (0, 0, chunk, 0)),
            pl.BlockSpec((1, slices, step, LANES), lambda i: (0, 0, chunk, last)),
        ],
        out_specs=[pl.BlockSpec((slices, step // 2, LANES), lambda i: (0, 0, 0))] * 2,
        out_shape=[shape, shape],
        name=f"edge_strips{chunk}",
    )(occupancy, density, density)


def shade(s, x, base, state, refs):
    frac_vertical, extinction, slice_total = refs
    through_ref, sum_ref = state
    rows = x.shape[0] - 8
    v0 = 2.0 * rounded(1.0 - frac_vertical[0, s], (1, LANES))
    v1 = 2.0 * rounded(frac_vertical[0, s], (1, LANES))
    density = v0 * x + v1 * pltpu.roll(x, 1, 0)
    above = pltpu.roll(density, 1, 0)
    density, above = density[8:], above[8:]
    rate = extinction[0, s] * (-LOG2E / (2.0 * slice_total))
    kept = jnp.exp2(rate * density)
    slope = jnp.tanh(density - above)
    at = slice(base, base + rows)
    through = through_ref[at]
    after = through * kept
    through_ref[at] = after
    sum_ref[at] += (through - after) * slope


def finish(state, gain, swap, out_keep, out_send, tile):
    through_ref, sum_ref = state
    rows = out_keep.shape[1] * 2
    base = tile * rows
    alphas, colors = [], []
    for p in range(rows // PIECE):
        at = slice(base + p * PIECE, base + (p + 1) * PIECE)
        alpha = 1.0 - through_ref[at]
        alphas.append(alpha)
        colors.append(gain * (0.65 * alpha + 0.35 * sum_ref[at]))
    lanes = slice(tile * LANES, (tile + 1) * LANES)
    for q in range(rows // PIECE // 2):
        at = slice(q * PIECE, (q + 1) * PIECE)
        for i, values in enumerate((colors, alphas)):
            even, odd = values[2 * q], values[2 * q + 1]
            out_keep[i, at, lanes] = jnp.where(swap, odd, even)
            out_send[i, at, lanes] = jnp.where(swap, even, odd)


def splat(value):
    return jnp.full((1, LANES), value, F32).astype(BF16)


def over_slices(slices, one):
    lax.fori_loop(0, slices, one, 0, unroll=UNROLL)


def interior_kernel(
    slice_total, occ, offset, frac_lateral, frac_vertical, extinction, gain,
    x_ref, lead_ref, out_keep, out_send, weights, through_ref, sum_ref,
):
    block = pl.program_id(0)
    slices, rows = x_ref.shape[1], x_ref.shape[2]
    tiles = x_ref.shape[3] // LANES

    @pl.when(block == 0)
    def _():
        k = lax.broadcasted_iota(jnp.int32, (2 * LANES, LANES), 0)
        n = lax.broadcasted_iota(jnp.int32, (2 * LANES, LANES), 1)

        def build(s, _):
            weights[s] = tap(LANES + n - k, offset[0, s], frac_lateral[0, s]).astype(BF16)
            return 0

        lax.fori_loop(0, slices, build, 0)

    through_ref[...] = jnp.ones_like(through_ref)
    sum_ref[...] = jnp.zeros_like(sum_ref)
    inside = jnp.where(block > 0, 1, 0)
    above = jnp.maximum(block - 1, 0)
    mask = [splat(occ[0, block, t]) for t in range(tiles)]
    lead_mask = [splat(occ[0, above, t] * inside) for t in range(tiles)]
    state = (through_ref, sum_ref)
    refs = (frac_vertical, extinction, slice_total)

    def one(s, _):
        parts = []
        for t in range(tiles):
            lanes = slice(t * LANES, (t + 1) * LANES)
            lead = lead_ref[0, s, :, lanes] * lead_mask[t]
            parts.append(jnp.concatenate([lead, x_ref[0, s, :, lanes] * mask[t]], axis=0))
        for t in range(1, tiles):
            pair = jnp.concatenate([parts[t - 1], parts[t]], axis=1)
            x = jnp.dot(pair, weights[s], preferred_element_type=F32)
            shade(s, x[8:], (t - 1) * rows, state, refs)
        return 0

    over_slices(slices, one)
    swap = lax.axis_index("depth") % 2 == 1
    for t in range(tiles - 1):
        finish(state, gain[0], swap, out_keep, out_send, t)


def small_specs():
    return [pl.BlockSpec(memory_space=SMEM)] * 6


def interior(density, small, slice_total):
    _, slices, rows, cols = density.shape
    step = BLK
    width = cols - LANES
    image = jax.ShapeDtypeStruct((2, rows // 2, width), F32)
    return pl.pallas_call(
        functools.partial(interior_kernel, slice_total),
        grid=(rows // step,),
        in_specs=small_specs()
        + [
            pl.BlockSpec((1, slices, step, cols), lambda b: (0, 0, b, 0)),
            pl.BlockSpec(
                (1, slices, 16, cols), lambda b: (0, 0, jnp.maximum(b * (step // 16) - 1, 0), 0)
            ),
        ],
        out_specs=[pl.BlockSpec((2, step // 2, width), lambda b: (0, b, 0))] * 2
        + [pl.BlockSpec((slices, 2 * LANES, LANES), lambda b: (0, 0, 0))],
        out_shape=[image, image, jax.ShapeDtypeStruct((slices, 2 * LANES, LANES), BF16)],
        scratch_shapes=[pltpu.VMEM((step * (width // LANES), LANES), F32)] * 2,
        compiler_params=pltpu.CompilerParams(vmem_limit_bytes=32 * 2**20),
        name="interior",
    )(*small, density, density)


def border_kernel(
    chunk, slice_total, occ, offset, frac_lateral, frac_vertical, extinction, gain, weights,
    first_ref, last_ref, first_lead, last_lead, right_ref, left_ref, right_lead, left_lead,
    out_keep, out_send, through_ref, sum_ref,
):
    slices, rows = first_ref.shape[1], BLK
    last_tile = occ.shape[2] - 1
    follows = jnp.where(lax.axis_index("lat") < lax.axis_size("lat") - 1, 1, 0)
    own_lanes = lax.broadcasted_iota(jnp.int32, (1, LANES), 1) >= HALF
    refs = (frac_vertical, extinction, slice_total)
    state = (through_ref, sum_ref)
    through_ref[...] = jnp.ones_like(through_ref)
    sum_ref[...] = jnp.zeros_like(sum_ref)
    blocks = first_ref.shape[2] // BLK
    start = blocks * chunk
    masks = []
    for b in range(start - 1, start + blocks):
        inside = b >= 0
        masks.append(
            (
                splat(occ[0, b, 0] if inside else 0.0),
                splat(occ[0, b, last_tile] * follows if inside else 0.0),
            )
        )

    def one(s, _):
        before, own = weights[s, :LANES], weights[s, LANES:]
        turn = lambda w: jnp.concatenate([w[HALF:], w[:HALF]], axis=0)
        near = jnp.concatenate([before, own], axis=0)
        far = (
            jnp.concatenate([turn(before), own], axis=0),
            jnp.concatenate([before, turn(own)], axis=0),
        )

        def lateral(first, last, right, left, second_half):
            w_left, w_right = far if second_half else (near, near)
            here = jnp.dot(
                jnp.concatenate([left, first], axis=1), w_left, preferred_element_type=F32
            )
            there = jnp.dot(
                jnp.concatenate([last, right], axis=1), w_right, preferred_element_type=F32
            )
            return jnp.where(own_lanes, here, there)

        right, left = right_ref[s], left_ref[s]
        zero = jnp.zeros((16, LANES), BF16)
        lead = lateral(
            first_lead[0, s] * masks[0][0],
            last_lead[0, s] * masks[0][1],
            right_lead[s] if chunk else zero,
            left_lead[s] if chunk else zero,
            True,
        )[8:]
        for b in range(blocks):
            at = slice(b * rows, (b + 1) * rows)
            x = lateral(
                first_ref[0, s, at] * masks[b + 1][0],
                last_ref[0, s, at] * masks[b + 1][1],
                right,
                left,
                b == 1,
            )
            shade(s, jnp.concatenate([lead, x], axis=0), b * rows, state, refs)
            lead = x[rows - 8 :]
        return 0

    over_slices(slices, one)
    swap = lax.axis_index("depth") % 2 == 1
    finish(state, gain[0], swap, out_keep, out_send, 0)


def border(density, small, weights, halos, previous, chunk, slice_total):
    _, slices, _, cols = density.shape
    step = 2 * BLK
    last = cols // LANES - 1
    per = step // 16

    def body(column):
        return pl.BlockSpec((1, slices, step, LANES), lambda i: (0, 0, chunk, column))

    def lead(column):
        return pl.BlockSpec(
            (1, slices, 16, LANES), lambda i: (0, 0, max(chunk * per - 1, 0), column)
        )

    halo = pl.BlockSpec((slices, BLK, LANES), lambda i: (0, 0, 0))
    halo_lead = pl.BlockSpec((slices, 16, LANES), lambda i: (0, BLK // 16 - 1, 0))
    image = jax.ShapeDtypeStruct((2, step // 2, LANES), F32)
    return pl.pallas_call(
        functools.partial(border_kernel, chunk, slice_total),
        grid=(1,),
        in_specs=small_specs()
        + [pl.BlockSpec((slices, 2 * LANES, LANES), lambda i: (0, 0, 0))]
        + [body(0), body(last), lead(0), lead(last), halo, halo, halo_lead, halo_lead],
        out_specs=[pl.BlockSpec((2, step // 2, LANES), lambda i: (0, 0, 0))] * 2,
        out_shape=[image, image],
        scratch_shapes=[pltpu.VMEM((step, LANES), F32)] * 2,
        compiler_params=pltpu.CompilerParams(vmem_limit_bytes=32 * 2**20),
        name=f"border{chunk}",
    )(*small, weights, density, density, density, density, *halos, *previous)


def over(mine, other, in_front):
    color = jnp.where(in_front, mine[0], other[0]) + (
        1.0 - jnp.where(in_front, mine[1], other[1])
    ) * jnp.where(in_front, other[0], mine[0])
    return jnp.stack([color, mine[1] + (1.0 - mine[1]) * other[1]])


def depth_swap(value, bits):
    count = lax.axis_size("depth")
    return lax.ppermute(value, "depth", [(i, i ^ bits) for i in range(count)])


def wire(value):
    return (value * WIRE_SCALE).astype(WIRE)


def unwire(value):
    return value.astype(F32) * (1.0 / WIRE_SCALE)


def over_cores(keep, send, rank):
    me = lax.axis_index("depth")
    return over(keep, depth_swap(send, 1), rank[me] < rank[me ^ 1])


def over_level(image, level, axis, rank):
    me = lax.axis_index("depth")
    bit = me >> level & 1
    keep = lax.dynamic_index_in_dim(image, bit, axis, keepdims=False)
    send = lax.dynamic_index_in_dim(image, 1 - bit, axis, keepdims=False)
    other = unwire(depth_swap(wire(send), 1 << level))
    return over(keep, other, rank[me] < rank[me ^ (1 << level)])


def over_z(keep, send, rank):
    image = over_cores(keep, send, rank)
    width = image.shape[2]
    image = image.reshape(2, 4, 2, 2, PIECE, width)
    image = over_level(image, 1, 3, rank)
    return over_level(image, 2, 2, rank)


def over_y(image, rank):
    width = image.shape[3]
    image = image.reshape(2, 2, 2, PIECE, width)
    image = over_level(image, 3, 2, rank)
    return over_level(image, 4, 1, rank)


def shards(
    density, occupancy, shear_offsets, frac_lateral, frac_vertical, extinction, slab_gain, view_rank
):
    _, slices, rows, cols = density.shape
    slice_total = lax.axis_size("depth") * slices
    lat = lax.axis_size("lat")
    density = pltpu.with_memory_space_constraint(density, pltpu.HBM)
    small = (occupancy, shear_offsets, frac_lateral, frac_vertical, extinction, slab_gain)
    chunks = rows // (2 * BLK)
    rightwards = [(x, x + 1) for x in range(lat - 1)]
    leftwards = [(x, (x - 1) % lat) for x in range(lat)]
    halos = []
    for c in range(chunks):
        to_left, to_right = edge_strips(density, occupancy, c)
        from_right = lax.ppermute(to_left, "lat", leftwards)
        from_left = lax.ppermute(to_right, "lat", rightwards)
        halos.append((from_right, from_left))
    keep, send, weights = interior(density, small, slice_total)
    inner = over_z(keep, send, view_rank)
    pieces = [
        border(density, small, weights, halos[c], halos[max(c - 1, 0)], c, slice_total)
        for c in range(chunks)
    ]
    keep, send = (jnp.concatenate(p, axis=1) for p in zip(*pieces))
    edge = over_z(keep, send, view_rank)
    image = over_y(jnp.concatenate([edge, inner], axis=3), view_rank)
    moved = lax.ppermute(image[:, :, :LANES], "lat", [(x, (x + 1) % lat) for x in range(lat)])
    lane = jnp.arange(LANES, dtype=jnp.int32)
    first = jnp.where(lane < HALF, moved, image[:, :, :LANES])
    image = jnp.concatenate([first, image[:, :, LANES:]], axis=2)
    return image[0], image[1]


def solution(mesh):
    placed = (
        P("depth", None, None, "lat"),
        P("depth", None, "lat"),
        P("depth", None),
        P("depth", None),
        P("depth", None),
        P("depth", None),
        P("depth"),
        P(),
    )
    return jax.shard_map(
        shards,
        mesh=mesh,
        in_specs=placed,
        out_specs=(P("depth", "lat"), P("depth", "lat")),
        check_vma=False,
    )
```

```python
import functools
import math

import jax
import jax.numpy as jnp
from jax import lax
from jax.experimental import pallas as pl
from jax.experimental.pallas import tpu as pltpu
from jax.sharding import PartitionSpec as P

SHIFT = 128
BLK = 128
HALF = SHIFT // 2
LANES = 128
PIECE = 16
WIRE = jnp.float16
WIRE_SCALE = 4096.0
UNROLL = 16
TAIL = 1
LOG2E = math.log2(math.e)
SMEM = pltpu.SMEM
F32 = jnp.float32
BF16 = jnp.bfloat16


def rounded(scalar, shape):
    return jnp.full(shape, scalar, F32).astype(BF16).astype(F32)


def tap(distance, offset, fraction):
    second = jnp.where(distance == offset + 1, fraction, 0.0)
    return jnp.where(distance == offset, 1.0 - fraction, second)


def strips_kernel(first_block, occ, x_first, x_last, to_left, to_right):
    half = x_first.shape[2] // 2
    block = first_block + pl.program_id(0)
    k = lax.broadcasted_iota(jnp.int32, (2 * LANES, LANES), 0)
    n = lax.broadcasted_iota(jnp.int32, (2 * LANES, LANES), 1)
    for ref, out, column, source in (
        (x_first, to_left, 0, jnp.where(n < HALF, n, n + HALF)),
        (x_last, to_right, occ.shape[2] - 1, jnp.where(n < HALF, n + LANES + HALF, n)),
    ):
        occupied = occ[0, block, column].astype(F32)
        pick = jnp.where(k == source, occupied, 0.0).astype(BF16)
        for s in range(ref.shape[1]):
            rows = jnp.concatenate([ref[0, s, :half], ref[0, s, half:]], axis=1)
            out[s] = jnp.dot(rows, pick, preferred_element_type=F32).astype(BF16)


def edge_strips(density, occupancy, first, blocks):
    _, slices, _, cols = density.shape
    shape = jax.ShapeDtypeStruct((slices, blocks * BLK // 2, LANES), BF16)
    last = cols // LANES - 1
    return pl.pallas_call(
        functools.partial(strips_kernel, first),
        grid=(blocks,),
        in_specs=[
            pl.BlockSpec(memory_space=SMEM),
            pl.BlockSpec((1, slices, BLK, LANES), lambda i: (0, 0, first + i, 0)),
            pl.BlockSpec((1, slices, BLK, LANES), lambda i: (0, 0, first + i, last)),
        ],
        out_specs=[pl.BlockSpec((slices, BLK // 2, LANES), lambda i: (0, i, 0))] * 2,
        out_shape=[shape, shape],
        name=f"edge_strips{first}",
    )(occupancy, density, density)


def shade(s, x, base, state, refs):
    frac_vertical, extinction, slice_total = refs
    through_ref, sum_ref = state
    rows = x.shape[0] - 8
    v0 = 2.0 * rounded(1.0 - frac_vertical[0, s], (1, LANES))
    v1 = 2.0 * rounded(frac_vertical[0, s], (1, LANES))
    density = v0 * x + v1 * pltpu.roll(x, 1, 0)
    above = pltpu.roll(density, 1, 0)
    density, above = density[8:], above[8:]
    rate = extinction[0, s] * (-LOG2E / (2.0 * slice_total))
    kept = jnp.exp2(rate * density)
    slope = jnp.tanh(density - above)
    at = slice(base, base + rows)
    through = through_ref[at]
    after = through * kept
    through_ref[at] = after
    sum_ref[at] += (through - after) * slope


def finish(state, gain, swap, out_keep, out_send, tile):
    through_ref, sum_ref = state
    rows = out_keep.shape[1] * 2
    base = tile * rows
    alphas, colors = [], []
    for p in range(rows // PIECE):
        at = slice(base + p * PIECE, base + (p + 1) * PIECE)
        alpha = 1.0 - through_ref[at]
        alphas.append(alpha)
        colors.append(gain * (0.65 * alpha + 0.35 * sum_ref[at]))
    lanes = slice(tile * LANES, (tile + 1) * LANES)
    for q in range(rows // PIECE // 2):
        at = slice(q * PIECE, (q + 1) * PIECE)
        for i, values in enumerate((colors, alphas)):
            even, odd = values[2 * q], values[2 * q + 1]
            out_keep[i, at, lanes] = jnp.where(swap, odd, even)
            out_send[i, at, lanes] = jnp.where(swap, even, odd)


def splat(value):
    return jnp.full((1, LANES), value, F32).astype(BF16)


def over_slices(slices, one):
    lax.fori_loop(0, slices, one, 0, unroll=UNROLL)


def interior_kernel(
    slice_total, occ, offset, frac_lateral, frac_vertical, extinction, gain,
    x_ref, lead_ref, out_keep, out_send, weights, through_ref, sum_ref,
):
    block = pl.program_id(0)
    slices, rows = x_ref.shape[1], x_ref.shape[2]
    tiles = x_ref.shape[3] // LANES

    @pl.when(block == 0)
    def _():
        k = lax.broadcasted_iota(jnp.int32, (2 * LANES, LANES), 0)
        n = lax.broadcasted_iota(jnp.int32, (2 * LANES, LANES), 1)

        def build(s, _):
            weights[s] = tap(LANES + n - k, offset[0, s], frac_lateral[0, s]).astype(BF16)
            return 0

        lax.fori_loop(0, slices, build, 0)

    through_ref[...] = jnp.ones_like(through_ref)
    sum_ref[...] = jnp.zeros_like(sum_ref)
    inside = jnp.where(block > 0, 1, 0)
    above = jnp.maximum(block - 1, 0)
    mask = [splat(occ[0, block, t]) for t in range(tiles)]
    lead_mask = [splat(occ[0, above, t] * inside) for t in range(tiles)]
    state = (through_ref, sum_ref)
    refs = (frac_vertical, extinction, slice_total)

    def one(s, _):
        parts = []
        for t in range(tiles):
            lanes = slice(t * LANES, (t + 1) * LANES)
            lead = lead_ref[0, s, :, lanes] * lead_mask[t]
            parts.append(jnp.concatenate([lead, x_ref[0, s, :, lanes] * mask[t]], axis=0))
        for t in range(1, tiles):
            pair = jnp.concatenate([parts[t - 1], parts[t]], axis=1)
            x = jnp.dot(pair, weights[s], preferred_element_type=F32)
            shade(s, x[8:], (t - 1) * rows, state, refs)
        return 0

    over_slices(slices, one)
    swap = lax.axis_index("depth") % 2 == 1
    for t in range(tiles - 1):
        finish(state, gain[0], swap, out_keep, out_send, t)


def small_specs():
    return [pl.BlockSpec(memory_space=SMEM)] * 6


def interior(density, small, slice_total):
    _, slices, rows, cols = density.shape
    step = BLK
    width = cols - LANES
    image = jax.ShapeDtypeStruct((2, rows // 2, width), F32)
    return pl.pallas_call(
        functools.partial(interior_kernel, slice_total),
        grid=(rows // step,),
        in_specs=small_specs()
        + [
            pl.BlockSpec((1, slices, step, cols), lambda b: (0, 0, b, 0)),
            pl.BlockSpec(
                (1, slices, 16, cols), lambda b: (0, 0, jnp.maximum(b * (step // 16) - 1, 0), 0)
            ),
        ],
        out_specs=[pl.BlockSpec((2, step // 2, width), lambda b: (0, b, 0))] * 2
        + [pl.BlockSpec((slices, 2 * LANES, LANES), lambda b: (0, 0, 0))],
        out_shape=[image, image, jax.ShapeDtypeStruct((slices, 2 * LANES, LANES), BF16)],
        scratch_shapes=[pltpu.VMEM((step * (width // LANES), LANES), F32)] * 2,
        compiler_params=pltpu.CompilerParams(vmem_limit_bytes=32 * 2**20),
        name="interior",
    )(*small, density, density)


def border_kernel(
    start, slice_total, occ, offset, frac_lateral, frac_vertical, extinction, gain, weights,
    first_ref, last_ref, first_lead, last_lead, right_ref, left_ref, right_lead, left_lead,
    out_keep, out_send, through_ref, sum_ref,
):
    slices, half = first_ref.shape[1], BLK // 2
    last_tile = occ.shape[2] - 1
    follows = jnp.where(lax.axis_index("lat") < lax.axis_size("lat") - 1, 1, 0)
    own_lanes = lax.broadcasted_iota(jnp.int32, (1, LANES), 1) >= HALF
    refs = (frac_vertical, extinction, slice_total)
    state = (through_ref, sum_ref)
    through_ref[...] = jnp.ones_like(through_ref)
    sum_ref[...] = jnp.zeros_like(sum_ref)
    blocks = first_ref.shape[2] // BLK
    masks = []
    for b in range(start - 1, start + blocks):
        inside = b >= 0
        masks.append(
            (
                splat(occ[0, b, 0] if inside else 0.0),
                splat(occ[0, b, last_tile] * follows if inside else 0.0),
            )
        )
    zero = jnp.zeros((16, LANES), BF16)

    def one(s, _):
        before, own = weights[s, :LANES], weights[s, LANES:]
        turn = lambda w: jnp.concatenate([w[HALF:], w[:HALF]], axis=0)
        near = jnp.concatenate([before, own], axis=0)
        far_left = jnp.concatenate([turn(before), own], axis=0)
        far_right = jnp.concatenate([before, turn(own)], axis=0)

        def halves(ref, side, top, above):
            parts = [above] if above is not None else []
            for b in range(blocks):
                at = slice(b * BLK + top, b * BLK + top + half)
                parts.append(ref[0, s, at] * masks[b + 1][side])
            return jnp.concatenate(parts, axis=0) if len(parts) > 1 else parts[0]

        def lateral(first, last, right, left, w_left, w_right):
            here = jnp.dot(
                jnp.concatenate([left, first], axis=1), w_left, preferred_element_type=F32
            )
            there = jnp.dot(
                jnp.concatenate([last, right], axis=1), w_right, preferred_element_type=F32
            )
            return jnp.where(own_lanes, here, there)

        right, left = right_ref[s], left_ref[s]
        x_near = lateral(
            halves(first_ref, 0, 0, None), halves(last_ref, 1, 0, None), right, left, near, near
        )
        x_far = lateral(
            halves(first_ref, 0, half, first_lead[0, s] * masks[0][0]),
            halves(last_ref, 1, half, last_lead[0, s] * masks[0][1]),
            jnp.concatenate([right_lead[s] if start else zero, right], axis=0),
            jnp.concatenate([left_lead[s] if start else zero, left], axis=0),
            far_left,
            far_right,
        )
        for b in range(blocks):
            rows = slice(b * half, (b + 1) * half)
            far_rows = slice(b * half + 16, (b + 1) * half + 16)
            lead = x_far[b * half + 8 : b * half + 16]
            x = jnp.concatenate([lead, x_near[rows], x_far[far_rows]], axis=0)
            shade(s, x, b * BLK, state, refs)
        return 0

    over_slices(slices, one)
    swap = lax.axis_index("depth") % 2 == 1
    finish(state, gain[0], swap, out_keep, out_send, 0)


def border(density, small, weights, halos, previous, start, blocks, slice_total):
    _, slices, _, cols = density.shape
    step = blocks * BLK
    last = cols // LANES - 1
    per = BLK // 16

    def body(column):
        shape = tuple(pl.Element(n) for n in (1, slices, step, LANES))
        return pl.BlockSpec(shape, lambda i: (0, 0, start * BLK, column * LANES))

    def lead(column):
        return pl.BlockSpec(
            (1, slices, 16, LANES), lambda i: (0, 0, max(start * per - 1, 0), column)
        )

    halo = pl.BlockSpec((slices, step // 2, LANES), lambda i: (0, 0, 0))
    end = previous[0].shape[1] // 16 - 1
    halo_lead = pl.BlockSpec((slices, 16, LANES), lambda i: (0, end, 0))
    image = jax.ShapeDtypeStruct((2, step // 2, LANES), F32)
    return pl.pallas_call(
        functools.partial(border_kernel, start, slice_total),
        grid=(1,),
        in_specs=small_specs()
        + [pl.BlockSpec((slices, 2 * LANES, LANES), lambda i: (0, 0, 0))]
        + [body(0), body(last), lead(0), lead(last), halo, halo, halo_lead, halo_lead],
        out_specs=[pl.BlockSpec((2, step // 2, LANES), lambda i: (0, 0, 0))] * 2,
        out_shape=[image, image],
        scratch_shapes=[pltpu.VMEM((step, LANES), F32)] * 2,
        compiler_params=pltpu.CompilerParams(vmem_limit_bytes=32 * 2**20),
        name=f"border{start}",
    )(*small, weights, density, density, density, density, *halos, *previous)


def over(mine, other, in_front):
    color = jnp.where(in_front, mine[0], other[0]) + (
        1.0 - jnp.where(in_front, mine[1], other[1])
    ) * jnp.where(in_front, other[0], mine[0])
    return jnp.stack([color, mine[1] + (1.0 - mine[1]) * other[1]])


def depth_swap(value, bits):
    count = lax.axis_size("depth")
    return lax.ppermute(value, "depth", [(i, i ^ bits) for i in range(count)])


def wire(value):
    return (value * WIRE_SCALE).astype(WIRE)


def unwire(value):
    return value.astype(F32) * (1.0 / WIRE_SCALE)


def over_cores(keep, send, rank):
    me = lax.axis_index("depth")
    return over(keep, depth_swap(send, 1), rank[me] < rank[me ^ 1])


def over_level(image, level, axis, rank):
    me = lax.axis_index("depth")
    bit = me >> level & 1
    keep = lax.dynamic_index_in_dim(image, bit, axis, keepdims=False)
    send = lax.dynamic_index_in_dim(image, 1 - bit, axis, keepdims=False)
    other = unwire(depth_swap(wire(send), 1 << level))
    return over(keep, other, rank[me] < rank[me ^ (1 << level)])


def by_chip(image):
    return image.reshape(2, 4, 2, 2, PIECE, image.shape[2])


def over_y(image, rank):
    width = image.shape[3]
    image = image.reshape(2, 2, 2, PIECE, width)
    image = over_level(image, 3, 2, rank)
    return over_level(image, 4, 1, rank)


def shards(
    density, occupancy, shear_offsets, frac_lateral, frac_vertical, extinction, slab_gain, view_rank
):
    _, slices, rows, cols = density.shape
    slice_total = lax.axis_size("depth") * slices
    lat = lax.axis_size("lat")
    density = pltpu.with_memory_space_constraint(density, pltpu.HBM)
    small = (occupancy, shear_offsets, frac_lateral, frac_vertical, extinction, slab_gain)
    blocks = rows // BLK
    cuts = [(0, blocks - TAIL), (blocks - TAIL, TAIL)]
    rightwards = [(x, x + 1) for x in range(lat - 1)]
    leftwards = [(x, (x - 1) % lat) for x in range(lat)]

    def halo(cut):
        to_left, to_right = edge_strips(density, occupancy, *cut)
        from_right = lax.ppermute(to_left, "lat", leftwards)
        from_left = lax.ppermute(to_right, "lat", rightwards)
        return (to_left, to_right), (from_right, from_left)

    strips, most = halo(cuts[0])
    more_strips, rest = halo(cuts[1])
    after_strips, _ = lax.optimization_barrier((occupancy, (strips, more_strips)))
    small_first = (after_strips, *small[1:])
    images = interior(density, small_first, slice_total)
    (keep, send, weights), most = lax.optimization_barrier((images, most))
    inner = over_cores(keep, send, view_rank)
    pieces = [border(density, small, weights, most, most, *cuts[0], slice_total)]
    inner, weights = lax.optimization_barrier((inner, weights))
    inner = over_level(by_chip(inner), 1, 3, view_rank)
    pieces.append(border(density, small, weights, rest, most, *cuts[1], slice_total))
    keep, send = (jnp.concatenate(p, axis=1) for p in zip(*pieces))
    inner, keep, send = lax.optimization_barrier((inner, keep, send))
    inner = over_level(inner, 2, 2, view_rank)
    edge = by_chip(over_cores(keep, send, view_rank))
    edge = over_level(edge, 1, 3, view_rank)
    edge = over_level(edge, 2, 2, view_rank)
    image = over_y(jnp.concatenate([edge, inner], axis=3), view_rank)
    moved = lax.ppermute(image[:, :, :LANES], "lat", [(x, (x + 1) % lat) for x in range(lat)])
    lane = jnp.arange(LANES, dtype=jnp.int32)
    first = jnp.where(lane < HALF, moved, image[:, :, :LANES])
    image = jnp.concatenate([first, image[:, :, LANES:]], axis=2)
    return image[0], image[1]


def solution(mesh):
    placed = (
        P("depth", None, None, "lat"),
        P("depth", None, "lat"),
        P("depth", None),
        P("depth", None),
        P("depth", None),
        P("depth", None),
        P("depth"),
        P(),
    )
    return jax.shard_map(
        shards,
        mesh=mesh,
        in_specs=placed,
        out_specs=(P("depth", "lat"), P("depth", "lat")),
        check_vma=False,
    )
```

```python
import functools
import math

import jax
import jax.numpy as jnp
from jax import lax
from jax.experimental import pallas as pl
from jax.experimental.pallas import tpu as pltpu
from jax.sharding import PartitionSpec as P

SHIFT = 128
BLK = 128
HALF = SHIFT // 2
LANES = 128
PIECE = 16
PARTNERS = (1, 2, 6, 8, 24)
WIRE = jnp.float16
WIRE_SCALE = 4096.0
UNROLL = 16
LOG2E = math.log2(math.e)
SMEM = pltpu.SMEM
F32 = jnp.float32
BF16 = jnp.bfloat16


def rounded(scalar, shape):
    return jnp.full(shape, scalar, F32).astype(BF16).astype(F32)


def tap(distance, offset, fraction):
    second = jnp.where(distance == offset + 1, fraction, 0.0)
    return jnp.where(distance == offset, 1.0 - fraction, second)


def strips_kernel(first_block, occ, x_first, x_last, to_left, to_right):
    half = x_first.shape[2] // 2
    block = first_block + pl.program_id(0)
    k = lax.broadcasted_iota(jnp.int32, (2 * LANES, LANES), 0)
    n = lax.broadcasted_iota(jnp.int32, (2 * LANES, LANES), 1)
    for ref, out, column, source in (
        (x_first, to_left, 0, jnp.where(n < HALF, n, n + HALF)),
        (x_last, to_right, occ.shape[2] - 1, jnp.where(n < HALF, n + LANES + HALF, n)),
    ):
        occupied = occ[0, block, column].astype(F32)
        pick = jnp.where(k == source, occupied, 0.0).astype(BF16)
        for s in range(ref.shape[1]):
            rows = jnp.concatenate([ref[0, s, :half], ref[0, s, half:]], axis=1)
            out[s] = jnp.dot(rows, pick, preferred_element_type=F32).astype(BF16)


def edge_strips(density, occupancy, first, blocks):
    _, slices, _, cols = density.shape
    shape = jax.ShapeDtypeStruct((slices, blocks * BLK // 2, LANES), BF16)
    last = cols // LANES - 1
    return pl.pallas_call(
        functools.partial(strips_kernel, first),
        grid=(blocks,),
        in_specs=[
            pl.BlockSpec(memory_space=SMEM),
            pl.BlockSpec((1, slices, BLK, LANES), lambda i: (0, 0, first + i, 0)),
            pl.BlockSpec((1, slices, BLK, LANES), lambda i: (0, 0, first + i, last)),
        ],
        out_specs=[pl.BlockSpec((slices, BLK // 2, LANES), lambda i: (0, i, 0))] * 2,
        out_shape=[shape, shape],
        name=f"edge_strips{first}",
    )(occupancy, density, density)


def shade(s, x, base, state, refs):
    frac_vertical, extinction, slice_total = refs
    through_ref, sum_ref = state
    rows = x.shape[0] - 8
    v0 = 2.0 * rounded(1.0 - frac_vertical[0, s], (1, LANES))
    v1 = 2.0 * rounded(frac_vertical[0, s], (1, LANES))
    density = v0 * x + v1 * pltpu.roll(x, 1, 0)
    above = pltpu.roll(density, 1, 0)
    density, above = density[8:], above[8:]
    rate = extinction[0, s] * (-LOG2E / (2.0 * slice_total))
    kept = jnp.exp2(rate * density)
    slope = jnp.tanh(density - above)
    at = slice(base, base + rows)
    through = through_ref[at]
    after = through * kept
    through_ref[at] = after
    sum_ref[at] += (through - after) * slope


def gray(index):
    return index ^ (index >> 1)


def finish(state, gain, swap, out_keep, out_send, tile, first=0):
    through_ref, sum_ref = state
    rows = out_keep.shape[1] * 2
    base = tile * rows
    alphas, colors = [], []
    for p in range(rows // PIECE):
        at = slice(base + p * PIECE, base + (p + 1) * PIECE)
        alpha = 1.0 - through_ref[at]
        alphas.append(alpha)
        colors.append(gain * (0.65 * alpha + 0.35 * sum_ref[at]))
    lanes = slice(tile * LANES, (tile + 1) * LANES)
    for q in range(rows // PIECE // 2):
        place = 4 * (gray(first + q // 4) - first) + gray(q % 4)
        at = slice(place * PIECE, (place + 1) * PIECE)
        for i, values in enumerate((colors, alphas)):
            even, odd = values[2 * q], values[2 * q + 1]
            out_keep[i, at, lanes] = jnp.where(swap, odd, even)
            out_send[i, at, lanes] = jnp.where(swap, even, odd)


def splat(value):
    return jnp.full((1, LANES), value, F32).astype(BF16)


def over_slices(slices, one):
    lax.fori_loop(0, slices, one, 0, unroll=UNROLL)


def interior_kernel(
    slice_total, occ, offset, frac_lateral, frac_vertical, extinction, gain, rank,
    x_ref, lead_ref, out_keep, out_send, weights, flags, through_ref, sum_ref,
):
    block = pl.program_id(0)
    slices, rows = x_ref.shape[1], x_ref.shape[2]
    tiles = x_ref.shape[3] // LANES

    @pl.when(block == 0)
    def _():
        k = lax.broadcasted_iota(jnp.int32, (2 * LANES, LANES), 0)
        n = lax.broadcasted_iota(jnp.int32, (2 * LANES, LANES), 1)

        def build(s, _):
            weights[s] = tap(LANES + n - k, offset[0, s], frac_lateral[0, s]).astype(BF16)
            return 0

        lax.fori_loop(0, slices, build, 0)
        me = lax.axis_index("depth")
        rows_of_flags = [rank[me] < rank[jnp.bitwise_xor(me, partner)] for partner in PARTNERS]
        z, y = (me // 2) % 4, me // 8
        for place in (jnp.bitwise_xor(z, z // 2), jnp.bitwise_xor(y, y // 2)):
            rows_of_flags += [place % 2 == 1, place // 2 == 1]
        for i, flag in enumerate(rows_of_flags):
            flags[i : i + 1] = jnp.full((1, LANES), jnp.where(flag, 1.0, 0.0), F32)

    through_ref[...] = jnp.ones_like(through_ref)
    sum_ref[...] = jnp.zeros_like(sum_ref)
    inside = jnp.where(block > 0, 1, 0)
    above = jnp.maximum(block - 1, 0)
    mask = [splat(occ[0, block, t]) for t in range(tiles)]
    lead_mask = [splat(occ[0, above, t] * inside) for t in range(tiles)]
    state = (through_ref, sum_ref)
    refs = (frac_vertical, extinction, slice_total)

    def one(s, _):
        parts = []
        for t in range(tiles):
            lanes = slice(t * LANES, (t + 1) * LANES)
            lead = lead_ref[0, s, :, lanes] * lead_mask[t]
            parts.append(jnp.concatenate([lead, x_ref[0, s, :, lanes] * mask[t]], axis=0))
        for t in range(1, tiles):
            pair = jnp.concatenate([parts[t - 1], parts[t]], axis=1)
            x = jnp.dot(pair, weights[s], preferred_element_type=F32)
            shade(s, x[8:], (t - 1) * rows, state, refs)
        return 0

    over_slices(slices, one)
    swap = lax.axis_index("depth") % 2 == 1
    for t in range(tiles - 1):
        finish(state, gain[0], swap, out_keep, out_send, t)


def small_specs():
    return [pl.BlockSpec(memory_space=SMEM)] * 6


def interior(density, small, rank, slice_total):
    _, slices, rows, cols = density.shape
    step = BLK
    width = cols - LANES
    image = jax.ShapeDtypeStruct((2, rows // 2, width), F32)
    return pl.pallas_call(
        functools.partial(interior_kernel, slice_total),
        grid=(rows // step,),
        in_specs=small_specs()
        + [pl.BlockSpec(memory_space=SMEM)]
        + [
            pl.BlockSpec((1, slices, step, cols), lambda b: (0, 0, b, 0)),
            pl.BlockSpec(
                (1, slices, 16, cols), lambda b: (0, 0, jnp.maximum(b * (step // 16) - 1, 0), 0)
            ),
        ],
        out_specs=[
            pl.BlockSpec((2, step // 2, width), lambda b: (0, jnp.bitwise_xor(b, b // 2), 0))
        ]
        * 2
        + [
            pl.BlockSpec((slices, 2 * LANES, LANES), lambda b: (0, 0, 0)),
            pl.BlockSpec((16, LANES), lambda b: (0, 0)),
        ],
        out_shape=[
            image,
            image,
            jax.ShapeDtypeStruct((slices, 2 * LANES, LANES), BF16),
            jax.ShapeDtypeStruct((16, LANES), F32),
        ],
        scratch_shapes=[pltpu.VMEM((step * (width // LANES), LANES), F32)] * 2,
        compiler_params=pltpu.CompilerParams(vmem_limit_bytes=32 * 2**20),
        name="interior",
    )(*small, rank, density, density)


def border_kernel(
    start, slice_total, occ, offset, frac_lateral, frac_vertical, extinction, gain, weights,
    first_ref, last_ref, first_lead, last_lead, right_ref, left_ref, right_lead, left_lead,
    out_keep, out_send, through_ref, sum_ref,
):
    slices, half = first_ref.shape[1], BLK // 2
    last_tile = occ.shape[2] - 1
    follows = jnp.where(lax.axis_index("lat") < lax.axis_size("lat") - 1, 1, 0)
    own_lanes = lax.broadcasted_iota(jnp.int32, (1, LANES), 1) >= HALF
    refs = (frac_vertical, extinction, slice_total)
    state = (through_ref, sum_ref)
    through_ref[...] = jnp.ones_like(through_ref)
    sum_ref[...] = jnp.zeros_like(sum_ref)
    blocks = first_ref.shape[2] // BLK
    masks = []
    for b in range(start - 1, start + blocks):
        inside = b >= 0
        masks.append(
            (
                splat(occ[0, b, 0] if inside else 0.0),
                splat(occ[0, b, last_tile] * follows if inside else 0.0),
            )
        )
    zero = jnp.zeros((16, LANES), BF16)

    def one(s, _):
        before, own = weights[s, :LANES], weights[s, LANES:]
        turn = lambda w: jnp.concatenate([w[HALF:], w[:HALF]], axis=0)
        near = jnp.concatenate([before, own], axis=0)
        far_left = jnp.concatenate([turn(before), own], axis=0)
        far_right = jnp.concatenate([before, turn(own)], axis=0)

        def halves(ref, side, top, above):
            parts = [above] if above is not None else []
            for b in range(blocks):
                at = slice(b * BLK + top, b * BLK + top + half)
                parts.append(ref[0, s, at] * masks[b + 1][side])
            return jnp.concatenate(parts, axis=0) if len(parts) > 1 else parts[0]

        def lateral(first, last, right, left, w_left, w_right):
            here = jnp.dot(
                jnp.concatenate([left, first], axis=1), w_left, preferred_element_type=F32
            )
            there = jnp.dot(
                jnp.concatenate([last, right], axis=1), w_right, preferred_element_type=F32
            )
            return jnp.where(own_lanes, here, there)

        right, left = right_ref[s], left_ref[s]
        x_near = lateral(
            halves(first_ref, 0, 0, None), halves(last_ref, 1, 0, None), right, left, near, near
        )
        x_far = lateral(
            halves(first_ref, 0, half, first_lead[0, s] * masks[0][0]),
            halves(last_ref, 1, half, last_lead[0, s] * masks[0][1]),
            jnp.concatenate([right_lead[s] if start else zero, right], axis=0),
            jnp.concatenate([left_lead[s] if start else zero, left], axis=0),
            far_left,
            far_right,
        )
        for b in range(blocks):
            rows = slice(b * half, (b + 1) * half)
            far_rows = slice(b * half + 16, (b + 1) * half + 16)
            lead = x_far[b * half + 8 : b * half + 16]
            x = jnp.concatenate([lead, x_near[rows], x_far[far_rows]], axis=0)
            shade(s, x, b * BLK, state, refs)
        return 0

    over_slices(slices, one)
    swap = lax.axis_index("depth") % 2 == 1
    finish(state, gain[0], swap, out_keep, out_send, 0, start)


def border(density, small, weights, halos, start, blocks, slice_total):
    _, slices, _, cols = density.shape
    step = blocks * BLK
    last = cols // LANES - 1
    per = BLK // 16

    def body(column):
        shape = tuple(pl.Element(n) for n in (1, slices, step, LANES))
        return pl.BlockSpec(shape, lambda i: (0, 0, start * BLK, column * LANES))

    def lead(column):
        return pl.BlockSpec(
            (1, slices, 16, LANES), lambda i: (0, 0, max(start * per - 1, 0), column)
        )

    halo = pl.BlockSpec((slices, step // 2, LANES), lambda i: (0, start // blocks, 0))
    above = max(start * per // 2 - 1, 0)
    halo_lead = pl.BlockSpec((slices, 16, LANES), lambda i: (0, above, 0))
    image = jax.ShapeDtypeStruct((2, step // 2, LANES), F32)
    return pl.pallas_call(
        functools.partial(border_kernel, start, slice_total),
        grid=(1,),
        in_specs=small_specs()
        + [pl.BlockSpec((slices, 2 * LANES, LANES), lambda i: (0, 0, 0))]
        + [body(0), body(last), lead(0), lead(last), halo, halo, halo_lead, halo_lead],
        out_specs=[pl.BlockSpec((2, step // 2, LANES), lambda i: (0, 0, 0))] * 2,
        out_shape=[image, image],
        scratch_shapes=[pltpu.VMEM((step, LANES), F32)] * 2,
        compiler_params=pltpu.CompilerParams(vmem_limit_bytes=32 * 2**20),
        name=f"border{start}",
    )(*small, weights, density, density, density, density, *halos, *halos)


def over(mine, other, in_front):
    color = jnp.where(in_front, mine[0], other[0]) + (
        1.0 - jnp.where(in_front, mine[1], other[1])
    ) * jnp.where(in_front, other[0], mine[0])
    return jnp.stack([color, mine[1] + (1.0 - mine[1]) * other[1]])


def depth_swap(value, bits):
    count = lax.axis_size("depth")
    return lax.ppermute(value, "depth", [(i, i ^ bits) for i in range(count)])


def wire(value):
    return (value * WIRE_SCALE).astype(WIRE)


def unwire(value):
    return value.astype(F32) * (1.0 / WIRE_SCALE)


def over_cores(keep, send, flags):
    return over(keep, depth_swap(send, PARTNERS[0]), flags[0, 0] > 0.0)


def over_level(image, level, flags):
    axis = 5 - level
    second = flags[4 + level, 0] > 0.0
    low = lax.index_in_dim(image, 0, axis, keepdims=False)
    high = lax.index_in_dim(image, 1, axis, keepdims=False)
    send = wire(jnp.where(second, low, high))
    other = unwire(depth_swap(send, PARTNERS[level]))
    return over(jnp.where(second, high, low), other, flags[level, 0] > 0.0)


def by_chip(image):
    return image.reshape(2, 2, 2, 2, 2, PIECE, image.shape[2])


def shards(
    density, occupancy, shear_offsets, frac_lateral, frac_vertical, extinction, slab_gain, view_rank
):
    _, slices, rows, cols = density.shape
    slice_total = lax.axis_size("depth") * slices
    lat = lax.axis_size("lat")
    density = pltpu.with_memory_space_constraint(density, pltpu.HBM)
    small = (occupancy, shear_offsets, frac_lateral, frac_vertical, extinction, slab_gain)
    blocks = rows // BLK
    rightwards = [(x, x + 1) for x in range(lat - 1)]
    leftwards = [(x, (x - 1) % lat) for x in range(lat)]
    to_left, to_right = edge_strips(density, occupancy, 0, blocks)
    halos = (
        lax.ppermute(to_left, "lat", leftwards),
        lax.ppermute(to_right, "lat", rightwards),
    )
    images = interior(density, small, view_rank, slice_total)
    (keep, send, weights, flags), halos = lax.optimization_barrier((images, halos))
    inner = over_cores(keep, send, flags)
    half = blocks // 2
    top = border(density, small, weights, halos, 0, half, slice_total)
    inner, weights = lax.optimization_barrier((inner, weights))
    inner = over_level(by_chip(inner), 1, flags)
    bottom = border(density, small, weights, halos, half, blocks - half, slice_total)
    keep, send = (jnp.concatenate(p, axis=1) for p in zip(top, bottom))
    edge = by_chip(over_cores(keep, send, flags))
    edge = over_level(edge, 1, flags)
    edge = over_level(edge, 2, flags)
    inner = over_level(inner, 2, flags)
    image = jnp.concatenate([edge, inner], axis=4)
    image = over_level(image, 3, flags)
    image = over_level(image, 4, flags)
    moved = lax.ppermute(image[:, :, :LANES], "lat", [(x, (x + 1) % lat) for x in range(lat)])
    lane = jnp.arange(LANES, dtype=jnp.int32)
    first = jnp.where(lane < HALF, moved, image[:, :, :LANES])
    image = jnp.concatenate([first, image[:, :, LANES:]], axis=2)
    return image[0], image[1]


def solution(mesh):
    placed = (
        P("depth", None, None, "lat"),
        P("depth", None, "lat"),
        P("depth", None),
        P("depth", None),
        P("depth", None),
        P("depth", None),
        P("depth"),
        P(),
    )
    return jax.shard_map(
        shards,
        mesh=mesh,
        in_specs=placed,
        out_specs=(P("depth", "lat"), P("depth", "lat")),
        check_vma=False,
    )
```

```python
import functools
import math

import jax
import jax.numpy as jnp
from jax import lax
from jax.experimental import pallas as pl
from jax.experimental.pallas import tpu as pltpu
from jax.sharding import PartitionSpec as P

SHIFT = 128
BLK = 128
HALF = SHIFT // 2
LANES = 128
PIECE = 16
WIRE = jnp.float16
WIRE_SCALE = 4096.0
UNROLL = 16
LOG2E = math.log2(math.e)
SMEM = pltpu.SMEM
F32 = jnp.float32
BF16 = jnp.bfloat16


def rounded(scalar, shape):
    return jnp.full(shape, scalar, F32).astype(BF16).astype(F32)


def tap(distance, offset, fraction):
    second = jnp.where(distance == offset + 1, fraction, 0.0)
    return jnp.where(distance == offset, 1.0 - fraction, second)


def strips_kernel(first_block, occ, x_first, x_last, to_left, to_right):
    half = x_first.shape[2] // 2
    block = first_block + pl.program_id(0)
    k = lax.broadcasted_iota(jnp.int32, (2 * LANES, LANES), 0)
    n = lax.broadcasted_iota(jnp.int32, (2 * LANES, LANES), 1)
    for ref, out, column, source in (
        (x_first, to_left, 0, jnp.where(n < HALF, n, n + HALF)),
        (x_last, to_right, occ.shape[2] - 1, jnp.where(n < HALF, n + LANES + HALF, n)),
    ):
        occupied = occ[0, block, column].astype(F32)
        pick = jnp.where(k == source, occupied, 0.0).astype(BF16)
        for s in range(ref.shape[1]):
            rows = jnp.concatenate([ref[0, s, :half], ref[0, s, half:]], axis=1)
            out[s] = jnp.dot(rows, pick, preferred_element_type=F32).astype(BF16)


def edge_strips(density, occupancy, first, blocks):
    _, slices, _, cols = density.shape
    shape = jax.ShapeDtypeStruct((slices, blocks * BLK // 2, LANES), BF16)
    last = cols // LANES - 1
    return pl.pallas_call(
        functools.partial(strips_kernel, first),
        grid=(blocks,),
        in_specs=[
            pl.BlockSpec(memory_space=SMEM),
            pl.BlockSpec((1, slices, BLK, LANES), lambda i: (0, 0, first + i, 0)),
            pl.BlockSpec((1, slices, BLK, LANES), lambda i: (0, 0, first + i, last)),
        ],
        out_specs=[pl.BlockSpec((slices, BLK // 2, LANES), lambda i: (0, i, 0))] * 2,
        out_shape=[shape, shape],
        name=f"edge_strips{first}",
    )(occupancy, density, density)


def shade(s, x, base, state, refs):
    frac_vertical, extinction, slice_total = refs
    through_ref, sum_ref = state
    rows = x.shape[0] - 8
    v0 = 2.0 * rounded(1.0 - frac_vertical[0, s], (1, LANES))
    v1 = 2.0 * rounded(frac_vertical[0, s], (1, LANES))
    density = v0 * x + v1 * pltpu.roll(x, 1, 0)
    above = pltpu.roll(density, 1, 0)
    density, above = density[8:], above[8:]
    rate = extinction[0, s] * (-LOG2E / (2.0 * slice_total))
    kept = jnp.exp2(rate * density)
    slope = jnp.tanh(density - above)
    at = slice(base, base + rows)
    through = through_ref[at]
    after = through * kept
    through_ref[at] = after
    sum_ref[at] += (through - after) * slope


def finish(state, gain, swap, out_keep, out_send, tile):
    through_ref, sum_ref = state
    rows = out_keep.shape[1] * 2
    base = tile * rows
    alphas, colors = [], []
    for p in range(rows // PIECE):
        at = slice(base + p * PIECE, base + (p + 1) * PIECE)
        alpha = 1.0 - through_ref[at]
        alphas.append(alpha)
        colors.append(gain * (0.65 * alpha + 0.35 * sum_ref[at]))
    lanes = slice(tile * LANES, (tile + 1) * LANES)
    for q in range(rows // PIECE // 2):
        at = slice(q * PIECE, (q + 1) * PIECE)
        for i, values in enumerate((colors, alphas)):
            even, odd = values[2 * q], values[2 * q + 1]
            out_keep[i, at, lanes] = jnp.where(swap, odd, even)
            out_send[i, at, lanes] = jnp.where(swap, even, odd)


def splat(value):
    return jnp.full((1, LANES), value, F32).astype(BF16)


def over_slices(slices, one):
    lax.fori_loop(0, slices, one, 0, unroll=UNROLL)


def interior_kernel(
    slice_total, occ, offset, frac_lateral, frac_vertical, extinction, gain, rank,
    x_ref, lead_ref, out_keep, out_send, weights, flags, through_ref, sum_ref,
):
    block = pl.program_id(0)
    slices, rows = x_ref.shape[1], x_ref.shape[2]
    tiles = x_ref.shape[3] // LANES

    @pl.when(block == 0)
    def _():
        k = lax.broadcasted_iota(jnp.int32, (2 * LANES, LANES), 0)
        n = lax.broadcasted_iota(jnp.int32, (2 * LANES, LANES), 1)

        def build(s, _):
            weights[s] = tap(LANES + n - k, offset[0, s], frac_lateral[0, s]).astype(BF16)
            return 0

        lax.fori_loop(0, slices, build, 0)
        me = lax.axis_index("depth")
        in_front = [rank[me] < rank[jnp.bitwise_xor(me, 1)]]
        for span in (2, 4, 8, 16):
            in_front += [rank[a] < rank[a + span] for a in range(0, rank.shape[0], 2 * span)]
        for i, flag in enumerate(in_front):
            flags[i : i + 1] = jnp.full((1, flags.shape[1]), jnp.where(flag, 1.0, 0.0), F32)

    through_ref[...] = jnp.ones_like(through_ref)
    sum_ref[...] = jnp.zeros_like(sum_ref)
    inside = jnp.where(block > 0, 1, 0)
    above = jnp.maximum(block - 1, 0)
    mask = [splat(occ[0, block, t]) for t in range(tiles)]
    lead_mask = [splat(occ[0, above, t] * inside) for t in range(tiles)]
    state = (through_ref, sum_ref)
    refs = (frac_vertical, extinction, slice_total)

    def one(s, _):
        parts = []
        for t in range(tiles):
            lanes = slice(t * LANES, (t + 1) * LANES)
            lead = lead_ref[0, s, :, lanes] * lead_mask[t]
            parts.append(jnp.concatenate([lead, x_ref[0, s, :, lanes] * mask[t]], axis=0))
        for t in range(1, tiles):
            pair = jnp.concatenate([parts[t - 1], parts[t]], axis=1)
            x = jnp.dot(pair, weights[s], preferred_element_type=F32)
            shade(s, x[8:], (t - 1) * rows, state, refs)
        return 0

    over_slices(slices, one)
    swap = lax.axis_index("depth") % 2 == 1
    for t in range(tiles - 1):
        finish(state, gain[0], swap, out_keep, out_send, t)


def small_specs():
    return [pl.BlockSpec(memory_space=SMEM)] * 6


def interior(density, small, rank, slice_total):
    _, slices, rows, cols = density.shape
    step = BLK
    width = cols - LANES
    image = jax.ShapeDtypeStruct((2, rows // 2, width), F32)
    return pl.pallas_call(
        functools.partial(interior_kernel, slice_total),
        grid=(rows // step,),
        in_specs=small_specs()
        + [pl.BlockSpec(memory_space=SMEM)]
        + [
            pl.BlockSpec((1, slices, step, cols), lambda b: (0, 0, b, 0)),
            pl.BlockSpec(
                (1, slices, 16, cols), lambda b: (0, 0, jnp.maximum(b * (step // 16) - 1, 0), 0)
            ),
        ],
        out_specs=[
            pl.BlockSpec((2, step // 2, width), lambda b: (0, b, 0))
        ]
        * 2
        + [
            pl.BlockSpec((slices, 2 * LANES, LANES), lambda b: (0, 0, 0)),
            pl.BlockSpec((16, cols), lambda b: (0, 0)),
        ],
        out_shape=[
            image,
            image,
            jax.ShapeDtypeStruct((slices, 2 * LANES, LANES), BF16),
            jax.ShapeDtypeStruct((16, cols), F32),
        ],
        scratch_shapes=[pltpu.VMEM((step * (width // LANES), LANES), F32)] * 2,
        compiler_params=pltpu.CompilerParams(vmem_limit_bytes=32 * 2**20),
        name="interior",
    )(*small, rank, density, density)


def border_kernel(
    start, slice_total, occ, offset, frac_lateral, frac_vertical, extinction, gain, weights,
    first_ref, last_ref, first_lead, last_lead, right_ref, left_ref, right_lead, left_lead,
    out_keep, out_send, through_ref, sum_ref,
):
    slices, half = first_ref.shape[1], BLK // 2
    last_tile = occ.shape[2] - 1
    follows = jnp.where(lax.axis_index("lat") < lax.axis_size("lat") - 1, 1, 0)
    own_lanes = lax.broadcasted_iota(jnp.int32, (1, LANES), 1) >= HALF
    refs = (frac_vertical, extinction, slice_total)
    state = (through_ref, sum_ref)
    through_ref[...] = jnp.ones_like(through_ref)
    sum_ref[...] = jnp.zeros_like(sum_ref)
    blocks = first_ref.shape[2] // BLK
    masks = []
    for b in range(start - 1, start + blocks):
        inside = b >= 0
        masks.append(
            (
                splat(occ[0, b, 0] if inside else 0.0),
                splat(occ[0, b, last_tile] * follows if inside else 0.0),
            )
        )
    zero = jnp.zeros((16, LANES), BF16)

    def one(s, _):
        before, own = weights[s, :LANES], weights[s, LANES:]
        turn = lambda w: jnp.concatenate([w[HALF:], w[:HALF]], axis=0)
        near = jnp.concatenate([before, own], axis=0)
        far_left = jnp.concatenate([turn(before), own], axis=0)
        far_right = jnp.concatenate([before, turn(own)], axis=0)

        def halves(ref, side, top, above):
            parts = [above] if above is not None else []
            for b in range(blocks):
                at = slice(b * BLK + top, b * BLK + top + half)
                parts.append(ref[0, s, at] * masks[b + 1][side])
            return jnp.concatenate(parts, axis=0) if len(parts) > 1 else parts[0]

        def lateral(first, last, right, left, w_left, w_right):
            here = jnp.dot(
                jnp.concatenate([left, first], axis=1), w_left, preferred_element_type=F32
            )
            there = jnp.dot(
                jnp.concatenate([last, right], axis=1), w_right, preferred_element_type=F32
            )
            return jnp.where(own_lanes, here, there)

        right, left = right_ref[s], left_ref[s]
        x_near = lateral(
            halves(first_ref, 0, 0, None), halves(last_ref, 1, 0, None), right, left, near, near
        )
        x_far = lateral(
            halves(first_ref, 0, half, first_lead[0, s] * masks[0][0]),
            halves(last_ref, 1, half, last_lead[0, s] * masks[0][1]),
            jnp.concatenate([right_lead[s] if start else zero, right], axis=0),
            jnp.concatenate([left_lead[s] if start else zero, left], axis=0),
            far_left,
            far_right,
        )
        for b in range(blocks):
            rows = slice(b * half, (b + 1) * half)
            far_rows = slice(b * half + 16, (b + 1) * half + 16)
            lead = x_far[b * half + 8 : b * half + 16]
            x = jnp.concatenate([lead, x_near[rows], x_far[far_rows]], axis=0)
            shade(s, x, b * BLK, state, refs)
        return 0

    over_slices(slices, one)
    swap = lax.axis_index("depth") % 2 == 1
    finish(state, gain[0], swap, out_keep, out_send, 0)


def border(density, small, weights, halos, above, start, blocks, slice_total):
    _, slices, _, cols = density.shape
    step = blocks * BLK
    last = cols // LANES - 1
    per = BLK // 16

    def body(column):
        shape = tuple(pl.Element(n) for n in (1, slices, step, LANES))
        return pl.BlockSpec(shape, lambda i: (0, 0, start * BLK, column * LANES))

    def lead(column):
        return pl.BlockSpec(
            (1, slices, 16, LANES), lambda i: (0, 0, max(start * per - 1, 0), column)
        )

    halo = pl.BlockSpec((slices, step // 2, LANES), lambda i: (0, 0, 0))
    last_rows = above[0].shape[1] // 16 - 1
    halo_lead = pl.BlockSpec((slices, 16, LANES), lambda i: (0, last_rows, 0))
    image = jax.ShapeDtypeStruct((2, step // 2, LANES), F32)
    return pl.pallas_call(
        functools.partial(border_kernel, start, slice_total),
        grid=(1,),
        in_specs=small_specs()
        + [pl.BlockSpec((slices, 2 * LANES, LANES), lambda i: (0, 0, 0))]
        + [body(0), body(last), lead(0), lead(last), halo, halo, halo_lead, halo_lead],
        out_specs=[pl.BlockSpec((2, step // 2, LANES), lambda i: (0, 0, 0))] * 2,
        out_shape=[image, image],
        scratch_shapes=[pltpu.VMEM((step, LANES), F32)] * 2,
        compiler_params=pltpu.CompilerParams(vmem_limit_bytes=32 * 2**20),
        name=f"border{start}",
    )(*small, weights, density, density, density, density, *halos, *above)


def over(mine, other, in_front):
    color = mine[0] * (1.0 - (1.0 - in_front) * other[1]) + other[0] * (1.0 - in_front * mine[1])
    return color, mine[1] + (1.0 - mine[1]) * other[1]


def over_cores(keep, send, flags):
    count = lax.axis_size("depth")
    other = lax.ppermute(send, "depth", [(i, i ^ 1) for i in range(count)])
    return jnp.stack(over(keep, other, flags[0, : keep.shape[2]]))


def over_chips(image, flags):
    count = lax.axis_size("depth")
    chips = count // 2
    width = image.shape[2]
    pieces = image.reshape(2, chips, PIECE, width).transpose(1, 0, 2, 3)
    pieces = (pieces * WIRE_SCALE).astype(WIRE)
    groups = [[2 * i + core for i in range(chips)] for core in range(2)]
    pieces = lax.all_to_all(
        pieces, "depth", 0, 0, axis_index_groups=groups, tiled=True
    )
    pieces = pieces.astype(F32) * (1.0 / WIRE_SCALE)
    level = [(pieces[i, 0], pieces[i, 1]) for i in range(chips)]
    row = 1
    while len(level) > 1:
        half = len(level) // 2
        level = [over(level[2 * i], level[2 * i + 1], flags[row + i]) for i in range(half)]
        row += half
    return level[0]


def shards(
    density, occupancy, shear_offsets, frac_lateral, frac_vertical, extinction, slab_gain, view_rank
):
    _, slices, rows, cols = density.shape
    slice_total = lax.axis_size("depth") * slices
    lat = lax.axis_size("lat")
    density = pltpu.with_memory_space_constraint(density, pltpu.HBM)
    small = (occupancy, shear_offsets, frac_lateral, frac_vertical, extinction, slab_gain)
    blocks = rows // BLK
    half = blocks // 2
    rightwards = [(x, x + 1) for x in range(lat - 1)]
    leftwards = [(x, (x - 1) % lat) for x in range(lat)]
    halos = []
    for first, count in ((0, half), (half, blocks - half)):
        to_left, to_right = edge_strips(density, occupancy, first, count)
        halos.append(
            (lax.ppermute(to_left, "lat", leftwards), lax.ppermute(to_right, "lat", rightwards))
        )
    keep, send, weights, flags = interior(density, small, view_rank, slice_total)
    top = border(density, small, weights, halos[0], halos[0], 0, half, slice_total)
    send, top = lax.optimization_barrier((send, top))
    inner = over_cores(keep, send, flags)
    bottom = border(density, small, weights, halos[1], halos[0], half, blocks - half, slice_total)
    keep, send = (jnp.concatenate(p, axis=1) for p in zip(top, bottom))
    edge = over_cores(keep, send, flags)
    color, alpha = over_chips(jnp.concatenate([edge, inner], axis=2), flags)
    image = jnp.stack([color, alpha])
    moved = lax.ppermute(image[:, :, :LANES], "lat", [(x, (x + 1) % lat) for x in range(lat)])
    lane = jnp.arange(LANES, dtype=jnp.int32)
    first = jnp.where(lane < HALF, moved, image[:, :, :LANES])
    return tuple(jnp.concatenate([first[i], image[i, :, LANES:]], axis=1) for i in range(2))


def solution(mesh):
    placed = (
        P("depth", None, None, "lat"),
        P("depth", None, "lat"),
        P("depth", None),
        P("depth", None),
        P("depth", None),
        P("depth", None),
        P("depth"),
        P(),
    )
    return jax.shard_map(
        shards,
        mesh=mesh,
        in_specs=placed,
        out_specs=(P("depth", "lat"), P("depth", "lat")),
        check_vma=False,
    )
```

```python
import functools
import math

import jax
import jax.numpy as jnp
from jax import lax
from jax.experimental import pallas as pl
from jax.experimental.pallas import tpu as pltpu
from jax.sharding import PartitionSpec as P

SHIFT = 128
BLK = 128
HALF = SHIFT // 2
LANES = 128
PIECE = 16
WIRE = jnp.float16
WIRE_SCALE = 4096.0
STEPS = 4
TAIL = 1
LOG2E = math.log2(math.e)
SMEM = pltpu.SMEM
F32 = jnp.float32
BF16 = jnp.bfloat16


def rounded(scalar, shape):
    return jnp.full(shape, scalar, F32).astype(BF16).astype(F32)


def tap(distance, offset, fraction):
    second = jnp.where(distance == offset + 1, fraction, 0.0)
    return jnp.where(distance == offset, 1.0 - fraction, second)


def strips_kernel(first_block, occ, x_first, x_last, to_left, to_right):
    half = BLK // 2
    count = x_first.shape[1]
    k = lax.broadcasted_iota(jnp.int32, (2 * LANES, LANES), 0)
    n = lax.broadcasted_iota(jnp.int32, (2 * LANES, LANES), 1)
    for ref, out, column, source in (
        (x_first, to_left, 0, jnp.where(n < HALF, n, n + HALF)),
        (x_last, to_right, occ.shape[2] - 1, jnp.where(n < HALF, n + LANES + HALF, n)),
    ):
        for b in range(x_first.shape[2] // BLK):
            occupied = occ[0, first_block + b, column].astype(F32)
            pick = jnp.where(k == source, occupied, 0.0).astype(BF16)
            top, bottom = slice(b * BLK, b * BLK + half), slice(b * BLK + half, (b + 1) * BLK)
            for u in range(count):
                rows = jnp.concatenate([ref[0, u, top], ref[0, u, bottom]], axis=1)
                moved = jnp.dot(rows, pick, preferred_element_type=F32)
                out[u, b * half : (b + 1) * half] = moved.astype(BF16)


def column_tile(slices, first, blocks, column):
    shape = tuple(pl.Element(n) for n in (1, slices // STEPS, blocks * BLK, LANES))
    return pl.BlockSpec(
        shape, lambda i: (0, i * (slices // STEPS), first * BLK, column * LANES)
    )


def whole():
    return pl.BlockSpec(memory_space=pltpu.VMEM)


def edge_strips(density, occupancy, first, blocks):
    _, slices, _, cols = density.shape
    shape = jax.ShapeDtypeStruct((slices, blocks * BLK // 2, LANES), BF16)
    last = cols // LANES - 1
    return pl.pallas_call(
        functools.partial(strips_kernel, first),
        grid=(STEPS,),
        in_specs=[
            pl.BlockSpec(memory_space=SMEM),
            column_tile(slices, first, blocks, 0),
            column_tile(slices, first, blocks, last),
        ],
        out_specs=[
            pl.BlockSpec((slices // STEPS, blocks * BLK // 2, LANES), lambda i: (i, 0, 0))
        ]
        * 2,
        out_shape=[shape, shape],
        name=f"edge_strips{first}",
    )(occupancy, density, density)


def shade(s, x, base, state, refs):
    frac_vertical, extinction, slice_total = refs
    through_ref, sum_ref = state
    rows = x.shape[0] - 8
    v0 = 2.0 * rounded(1.0 - frac_vertical[0, s], (1, LANES))
    v1 = 2.0 * rounded(frac_vertical[0, s], (1, LANES))
    density = v0 * x + v1 * pltpu.roll(x, 1, 0)
    above = pltpu.roll(density, 1, 0)
    density, above = density[8:], above[8:]
    rate = extinction[0, s] * (-LOG2E / (2.0 * slice_total))
    kept = jnp.exp2(rate * density)
    slope = jnp.tanh(density - above)
    at = slice(base, base + rows)
    through = through_ref[at]
    after = through * kept
    through_ref[at] = after
    sum_ref[at] += (through - after) * slope


def finish(state, gain, swap, out_keep, out_send, tile):
    through_ref, sum_ref = state
    rows = out_keep.shape[0] * 2 * PIECE
    base = tile * rows
    alphas, colors = [], []
    for p in range(rows // PIECE):
        at = slice(base + p * PIECE, base + (p + 1) * PIECE)
        alpha = 1.0 - through_ref[at]
        alphas.append(alpha)
        colors.append(gain * (0.65 * alpha + 0.35 * sum_ref[at]))
    lanes = slice(tile * LANES, (tile + 1) * LANES)
    for q in range(rows // PIECE // 2):
        for i, values in enumerate((colors, alphas)):
            even, odd = values[2 * q], values[2 * q + 1]
            out_keep[q, i, :, lanes] = jnp.where(swap, odd, even)
            out_send[q, i, :, lanes] = jnp.where(swap, even, odd)


def splat(value):
    return jnp.full((1, LANES), value, F32).astype(BF16)


def over_slices(slices, one):
    for s in range(slices):
        one(s, 0)


def interior_kernel(
    slice_total, occ, offset, frac_lateral, frac_vertical, extinction, gain, rank,
    x_ref, lead_ref, out_keep, out_send, weights, flags, through_ref, sum_ref,
):
    block = pl.program_id(0)
    slices, rows = x_ref.shape[1], x_ref.shape[2]
    tiles = x_ref.shape[3] // LANES

    @pl.when(block == 0)
    def _():
        k = lax.broadcasted_iota(jnp.int32, (2 * LANES, LANES), 0)
        n = lax.broadcasted_iota(jnp.int32, (2 * LANES, LANES), 1)

        def build(s, _):
            weights[s] = tap(LANES + n - k, offset[0, s], frac_lateral[0, s]).astype(BF16)
            return 0

        lax.fori_loop(0, slices, build, 0)
        me = lax.axis_index("depth")
        in_front = [rank[me] < rank[jnp.bitwise_xor(me, 1)]]
        for span in (2, 4, 8, 16):
            in_front += [rank[a] < rank[a + span] for a in range(0, rank.shape[0], 2 * span)]
        for i, flag in enumerate(in_front):
            flags[i : i + 1] = jnp.full((1, flags.shape[1]), jnp.where(flag, 1.0, 0.0), F32)

    through_ref[...] = jnp.ones_like(through_ref)
    sum_ref[...] = jnp.zeros_like(sum_ref)
    inside = jnp.where(block > 0, 1, 0)
    above = jnp.maximum(block - 1, 0)
    mask = [splat(occ[0, block, t]) for t in range(tiles)]
    lead_mask = [splat(occ[0, above, t] * inside) for t in range(tiles)]
    state = (through_ref, sum_ref)
    refs = (frac_vertical, extinction, slice_total)

    def one(s, _):
        parts = []
        for t in range(tiles):
            lanes = slice(t * LANES, (t + 1) * LANES)
            lead = lead_ref[0, s, :, lanes] * lead_mask[t]
            parts.append(jnp.concatenate([lead, x_ref[0, s, :, lanes] * mask[t]], axis=0))
        for t in range(1, tiles):
            pair = jnp.concatenate([parts[t - 1], parts[t]], axis=1)
            x = jnp.dot(pair, weights[s], preferred_element_type=F32)
            shade(s, x[8:], (t - 1) * rows, state, refs)
        return 0

    over_slices(slices, one)
    swap = lax.axis_index("depth") % 2 == 1
    for t in range(tiles - 1):
        finish(state, gain[0], swap, out_keep, out_send, t)


def small_specs():
    return [pl.BlockSpec(memory_space=SMEM)] * 6


def interior(density, small, rank, slice_total):
    _, slices, rows, cols = density.shape
    step = BLK
    width = cols - LANES
    pieces = step // (2 * PIECE)
    image = jax.ShapeDtypeStruct((rows // (2 * PIECE), 2, PIECE, width), F32)
    return pl.pallas_call(
        functools.partial(interior_kernel, slice_total),
        grid=(rows // step,),
        in_specs=small_specs()
        + [pl.BlockSpec(memory_space=SMEM)]
        + [
            pl.BlockSpec((1, slices, step, cols), lambda b: (0, 0, b, 0)),
            pl.BlockSpec(
                (1, slices, 16, cols), lambda b: (0, 0, jnp.maximum(b * (step // 16) - 1, 0), 0)
            ),
        ],
        out_specs=[
            pl.BlockSpec((pieces, 2, PIECE, width), lambda b: (b, 0, 0, 0))
        ]
        * 2
        + [
            pl.BlockSpec((slices, 2 * LANES, LANES), lambda b: (0, 0, 0)),
            pl.BlockSpec((16, cols), lambda b: (0, 0)),
        ],
        out_shape=[
            image,
            image,
            jax.ShapeDtypeStruct((slices, 2 * LANES, LANES), BF16),
            jax.ShapeDtypeStruct((16, cols), F32),
        ],
        scratch_shapes=[pltpu.VMEM((step * (width // LANES), LANES), F32)] * 2,
        compiler_params=pltpu.CompilerParams(vmem_limit_bytes=32 * 2**20),
        name="interior",
    )(*small, rank, density, density)


def border_kernel(
    start, slice_total, occ, offset, frac_lateral, frac_vertical, extinction, gain, weights,
    first_ref, last_ref, first_lead, last_lead, right_ref, left_ref, right_lead, left_lead,
    out_keep, out_send, through_ref, sum_ref,
):
    count, half = first_ref.shape[1], BLK // 2
    step = pl.program_id(0)
    last_tile = occ.shape[2] - 1
    follows = jnp.where(lax.axis_index("lat") < lax.axis_size("lat") - 1, 1, 0)
    own_lanes = lax.broadcasted_iota(jnp.int32, (1, LANES), 1) >= HALF
    refs = (frac_vertical, extinction, slice_total)
    state = (through_ref, sum_ref)

    @pl.when(step == 0)
    def _():
        through_ref[...] = jnp.ones_like(through_ref)
        sum_ref[...] = jnp.zeros_like(sum_ref)

    blocks = first_ref.shape[2] // BLK
    masks = []
    for b in range(start - 1, start + blocks):
        inside = b >= 0
        masks.append(
            (
                splat(occ[0, b, 0] if inside else 0.0),
                splat(occ[0, b, last_tile] * follows if inside else 0.0),
            )
        )
    zero = jnp.zeros((16, LANES), BF16)

    def one(u, _):
        s = step * count + u
        before, own = weights[s, :LANES], weights[s, LANES:]
        turn = lambda w: jnp.concatenate([w[HALF:], w[:HALF]], axis=0)
        near = jnp.concatenate([before, own], axis=0)
        far_left = jnp.concatenate([turn(before), own], axis=0)
        far_right = jnp.concatenate([before, turn(own)], axis=0)

        def halves(ref, side, top, above):
            parts = [above] if above is not None else []
            for b in range(blocks):
                at = slice(b * BLK + top, b * BLK + top + half)
                parts.append(ref[0, u, at] * masks[b + 1][side])
            return jnp.concatenate(parts, axis=0) if len(parts) > 1 else parts[0]

        def lateral(first, last, right, left, w_left, w_right):
            here = jnp.dot(
                jnp.concatenate([left, first], axis=1), w_left, preferred_element_type=F32
            )
            there = jnp.dot(
                jnp.concatenate([last, right], axis=1), w_right, preferred_element_type=F32
            )
            return jnp.where(own_lanes, here, there)

        right, left = right_ref[s], left_ref[s]
        x_near = lateral(
            halves(first_ref, 0, 0, None), halves(last_ref, 1, 0, None), right, left, near, near
        )
        x_far = lateral(
            halves(first_ref, 0, half, first_lead[0, u] * masks[0][0]),
            halves(last_ref, 1, half, last_lead[0, u] * masks[0][1]),
            jnp.concatenate([right_lead[s, -16:] if start else zero, right], axis=0),
            jnp.concatenate([left_lead[s, -16:] if start else zero, left], axis=0),
            far_left,
            far_right,
        )
        for b in range(blocks):
            rows = slice(b * half, (b + 1) * half)
            far_rows = slice(b * half + 16, (b + 1) * half + 16)
            lead = x_far[b * half + 8 : b * half + 16]
            x = jnp.concatenate([lead, x_near[rows], x_far[far_rows]], axis=0)
            shade(s, x, b * BLK, state, refs)
        return 0

    over_slices(count, one)

    @pl.when(step == pl.num_programs(0) - 1)
    def _():
        swap = lax.axis_index("depth") % 2 == 1
        finish(state, gain[0], swap, out_keep, out_send, 0)


def border(density, small, weights, halos, above, start, blocks, slice_total):
    _, slices, _, cols = density.shape
    step = blocks * BLK
    last = cols // LANES - 1
    lead_rows = max(start * BLK // 16 - 1, 0)

    def lead(column):
        return pl.BlockSpec((1, slices // STEPS, 16, LANES), lambda i: (0, i, lead_rows, column))

    image = jax.ShapeDtypeStruct((step // (2 * PIECE), 2, PIECE, LANES), F32)
    return pl.pallas_call(
        functools.partial(border_kernel, start, slice_total),
        grid=(STEPS,),
        in_specs=small_specs()
        + [whole()]
        + [column_tile(slices, start, blocks, column) for column in (0, last)]
        + [lead(0), lead(last)]
        + [whole()] * 4,
        out_specs=[whole()] * 2,
        out_shape=[image, image],
        scratch_shapes=[pltpu.VMEM((step, LANES), F32)] * 2,
        compiler_params=pltpu.CompilerParams(vmem_limit_bytes=32 * 2**20),
        name=f"border{start}",
    )(*small, weights, density, density, density, density, *halos, *above)


def over(mine, other, in_front):
    color = mine[0] * (1.0 - (1.0 - in_front) * other[1]) + other[0] * (1.0 - in_front * mine[1])
    return color, mine[1] + (1.0 - mine[1]) * other[1]


def over_cores(keep, send, flags):
    count = lax.axis_size("depth")
    other = lax.ppermute(send, "depth", [(i, i ^ 1) for i in range(count)])
    front = flags[0, : keep.shape[3]]
    return jnp.stack(over((keep[:, 0], keep[:, 1]), (other[:, 0], other[:, 1]), front), axis=1)


def over_chips(pieces, flags):
    count = lax.axis_size("depth")
    chips = count // 2
    pieces = (pieces * WIRE_SCALE).astype(WIRE)
    groups = [[2 * i + core for i in range(chips)] for core in range(2)]
    pieces = lax.all_to_all(
        pieces, "depth", 0, 0, axis_index_groups=groups, tiled=True
    )
    pieces = pieces.astype(F32) * (1.0 / WIRE_SCALE)
    level = [(pieces[i, 0], pieces[i, 1]) for i in range(chips)]
    row = 1
    while len(level) > 1:
        half = len(level) // 2
        level = [over(level[2 * i], level[2 * i + 1], flags[row + i]) for i in range(half)]
        row += half
    return level[0]


def shards(
    density, occupancy, shear_offsets, frac_lateral, frac_vertical, extinction, slab_gain, view_rank
):
    _, slices, rows, cols = density.shape
    slice_total = lax.axis_size("depth") * slices
    lat = lax.axis_size("lat")
    density = pltpu.with_memory_space_constraint(density, pltpu.HBM)
    small = (occupancy, shear_offsets, frac_lateral, frac_vertical, extinction, slab_gain)
    blocks = rows // BLK
    half = blocks - TAIL
    rightwards = [(x, x + 1) for x in range(lat - 1)]
    leftwards = [(x, (x - 1) % lat) for x in range(lat)]
    halos = []
    for first, count in ((0, half), (half, blocks - half)):
        to_left, to_right = edge_strips(density, occupancy, first, count)
        halos.append(
            (lax.ppermute(to_left, "lat", leftwards), lax.ppermute(to_right, "lat", rightwards))
        )
    keep, send, weights, flags = interior(density, small, view_rank, slice_total)
    top = border(density, small, weights, halos[0], halos[0], 0, half, slice_total)
    send, top = lax.optimization_barrier((send, top))
    inner = over_cores(keep, send, flags)
    bottom = border(density, small, weights, halos[1], halos[0], half, blocks - half, slice_total)
    keep, send = (jnp.concatenate(p, axis=0) for p in zip(top, bottom))
    edge = over_cores(keep, send, flags)
    color, alpha = over_chips(jnp.concatenate([edge, inner], axis=3), flags)
    image = jnp.stack([color, alpha])
    moved = lax.ppermute(image[:, :, :LANES], "lat", [(x, (x + 1) % lat) for x in range(lat)])
    lane = jnp.arange(LANES, dtype=jnp.int32)
    first = jnp.where(lane < HALF, moved, image[:, :, :LANES])
    return tuple(jnp.concatenate([first[i], image[i, :, LANES:]], axis=1) for i in range(2))


def solution(mesh):
    placed = (
        P("depth", None, None, "lat"),
        P("depth", None, "lat"),
        P("depth", None),
        P("depth", None),
        P("depth", None),
        P("depth", None),
        P("depth"),
        P(),
    )
    return jax.shard_map(
        shards,
        mesh=mesh,
        in_specs=placed,
        out_specs=(P("depth", "lat"), P("depth", "lat")),
        check_vma=False,
    )
```

```python
import functools
import math

import jax
import jax.numpy as jnp
from jax import lax
from jax.experimental import pallas as pl
from jax.experimental.pallas import tpu as pltpu
from jax.sharding import PartitionSpec as P

SHIFT = 128
BLK = 128
LANES = 128
PIECE = 16
WIRE = jnp.float16
WIRE_SCALE = 4096.0
PACKED = 4 * LANES
LOG2E = math.log2(math.e)
SMEM = pltpu.SMEM
F32 = jnp.float32
BF16 = jnp.bfloat16


def rounded(scalar, shape):
    return jnp.full(shape, scalar, F32).astype(BF16).astype(F32)


def tap(distance, offset, fraction):
    second = jnp.where(distance == offset + 1, fraction, 0.0)
    return jnp.where(distance == offset, 1.0 - fraction, second)


class Packing:
    def __init__(self, offset):
        slices = offset.shape[1]
        lane = lax.broadcasted_iota(jnp.int32, (8, LANES), 1)
        right, left = jnp.zeros_like(lane), jnp.zeros_like(lane)
        for s in range(slices):
            right = right + jnp.maximum(lane - offset[0, s], 0)
            left = left + jnp.maximum(offset[0, s] + 1 - lane, 0)
        fits = (right <= PACKED) & (left <= PACKED)
        self.border = jnp.min(jnp.where(fits, lane.astype(F32), 127.0)).astype(jnp.int32)
        self.from_left, self.count, self.tile, self.first = [], [], [], []
        used = [0, 0]
        for s in range(slices):
            o = offset[0, s]
            from_left = o >= self.border
            count = jnp.where(from_left, o + 1 - self.border, self.border - o)
            first = jnp.where(from_left, used[1], used[0])
            used[1] = used[1] + jnp.where(from_left, count, 0)
            used[0] = used[0] + jnp.where(from_left, 0, count)
            tile = jnp.minimum(jnp.right_shift(first, 7), PACKED // LANES - 2)
            self.from_left.append(from_left)
            self.count.append(count)
            self.tile.append(tile)
            self.first.append(first - LANES * tile)


def pack_kernel(occ, offset, x_first, x_last, to_left, to_right, picks, packed):
    block = pl.program_id(0)
    slices, cols = x_first.shape[1], LANES
    packing = Packing(offset)

    @pl.when(block == 0)
    def _():
        k = lax.broadcasted_iota(jnp.int32, (LANES, 2 * LANES), 0)
        p = lax.broadcasted_iota(jnp.int32, (LANES, 2 * LANES), 1)
        for s in range(slices):
            skip = jnp.where(packing.from_left[s], cols - packing.count[s], 0)
            inside = (k >= skip) & (k < skip + packing.count[s])
            same = k - skip == p - packing.first[s]
            picks[s] = jnp.where(inside & same, 1.0, 0.0).astype(BF16)

    packed[...] = jnp.zeros_like(packed)
    first_occ = occ[0, block, 0].astype(F32)
    last_occ = occ[0, block, occ.shape[2] - 1].astype(F32)
    for s in range(slices):
        from_left = packing.from_left[s]
        columns = x_first[0, s] * splat(jnp.where(from_left, 0.0, first_occ)) + x_last[
            0, s
        ] * splat(jnp.where(from_left, last_occ, 0.0))
        moved = jnp.dot(columns, picks[s], preferred_element_type=F32).astype(BF16)
        way = jnp.where(from_left, 1, 0)
        tile = packing.tile[s]
        packed[way, tile] += moved[:, :LANES]
        packed[way, tile + 1] += moved[:, LANES:]
    to_left[...] = packed[0]
    to_right[...] = packed[1]


def pack_halo(density, occupancy, offsets):
    _, slices, rows, cols = density.shape
    tiles = PACKED // LANES
    shape = jax.ShapeDtypeStruct((tiles, rows, LANES), BF16)
    last = cols // LANES - 1
    return pl.pallas_call(
        pack_kernel,
        grid=(rows // BLK,),
        in_specs=[
            pl.BlockSpec(memory_space=SMEM),
            pl.BlockSpec(memory_space=SMEM),
            pl.BlockSpec((1, slices, BLK, LANES), lambda b: (0, 0, b, 0)),
            pl.BlockSpec((1, slices, BLK, LANES), lambda b: (0, 0, b, last)),
        ],
        out_specs=[pl.BlockSpec((tiles, BLK, LANES), lambda b: (0, b, 0))] * 2,
        out_shape=[shape, shape],
        scratch_shapes=[
            pltpu.VMEM((slices, LANES, 2 * LANES), BF16),
            pltpu.VMEM((2, tiles, BLK, LANES), BF16),
        ],
        name="pack_halo",
    )(occupancy, offsets, density, density)


def whole():
    return pl.BlockSpec(memory_space=pltpu.VMEM)


def border_weights(s, offset, frac_lateral, packing, weights, out):
    n = lax.broadcasted_iota(jnp.int32, (2 * LANES, LANES), 1)
    p = lax.broadcasted_iota(jnp.int32, (2 * LANES, LANES), 0)
    own = jnp.where(n[:1] >= packing.border, 1.0, 0.0)
    out[s, :LANES] = weights[s, LANES:] * own.astype(BF16)
    out[s, LANES : 2 * LANES] = weights[s, :LANES] * (1.0 - own).astype(BF16)
    from_left, count = packing.from_left[s], packing.count[s]
    index = p - packing.first[s]
    reach = n + jnp.where(from_left, count, 0) - index
    weight = tap(reach, offset[0, s], frac_lateral[0, s])
    weight = jnp.where((index >= 0) & (index < count), weight, 0.0)
    mine = jnp.where(from_left, own, 1.0 - own)
    out[s, 2 * LANES :] = (weight * mine).astype(BF16)


def shade(s, x, base, state, refs):
    frac_vertical, extinction, slice_total = refs
    through_ref, sum_ref = state
    rows = x.shape[0] - 8
    v0 = 2.0 * rounded(1.0 - frac_vertical[0, s], (1, LANES))
    v1 = 2.0 * rounded(frac_vertical[0, s], (1, LANES))
    density = v0 * x + v1 * pltpu.roll(x, 1, 0)
    above = pltpu.roll(density, 1, 0)
    density, above = density[8:], above[8:]
    rate = extinction[0, s] * (-LOG2E / (2.0 * slice_total))
    kept = jnp.exp2(rate * density)
    slope = jnp.tanh(density - above)
    at = slice(base, base + rows)
    through = through_ref[at]
    after = through * kept
    through_ref[at] = after
    sum_ref[at] += (through - after) * slope


def finish(state, gain, swap, out_keep, out_send, tile):
    through_ref, sum_ref = state
    rows = out_keep.shape[0] * 2 * PIECE
    base = tile * rows
    alphas, colors = [], []
    for p in range(rows // PIECE):
        at = slice(base + p * PIECE, base + (p + 1) * PIECE)
        alpha = 1.0 - through_ref[at]
        alphas.append(alpha)
        colors.append(gain * (0.65 * alpha + 0.35 * sum_ref[at]))
    lanes = slice(tile * LANES, (tile + 1) * LANES)
    for q in range(rows // PIECE // 2):
        for i, values in enumerate((colors, alphas)):
            even, odd = values[2 * q], values[2 * q + 1]
            out_keep[q, i, :, lanes] = jnp.where(swap, odd, even)
            out_send[q, i, :, lanes] = jnp.where(swap, even, odd)


def splat(value):
    return jnp.full((1, LANES), value, F32).astype(BF16)


def over_slices(slices, one):
    for s in range(slices):
        one(s, 0)


def interior_kernel(
    slice_total, occ, offset, frac_lateral, frac_vertical, extinction, gain, rank,
    x_ref, lead_ref, out_keep, out_send, out_weights, flags, weights, through_ref, sum_ref,
):
    block = pl.program_id(0)
    slices, rows = x_ref.shape[1], x_ref.shape[2]
    tiles = x_ref.shape[3] // LANES

    @pl.when(block == 0)
    def _():
        k = lax.broadcasted_iota(jnp.int32, (2 * LANES, LANES), 0)
        n = lax.broadcasted_iota(jnp.int32, (2 * LANES, LANES), 1)

        def build(s, _):
            weights[s] = tap(LANES + n - k, offset[0, s], frac_lateral[0, s]).astype(BF16)
            return 0

        lax.fori_loop(0, slices, build, 0)
        packing = Packing(offset)
        for s in range(slices):
            border_weights(s, offset, frac_lateral, packing, weights, out_weights)
        lane = lax.broadcasted_iota(jnp.int32, (1, flags.shape[1]), 1)
        flags[16:17] = jnp.where(lane < packing.border, 1.0, 0.0)
        me = lax.axis_index("depth")
        in_front = [rank[me] < rank[jnp.bitwise_xor(me, 1)]]
        for span in (2, 4, 8, 16):
            in_front += [rank[a] < rank[a + span] for a in range(0, rank.shape[0], 2 * span)]
        for i, flag in enumerate(in_front):
            flags[i : i + 1] = jnp.full((1, flags.shape[1]), jnp.where(flag, 1.0, 0.0), F32)

    through_ref[...] = jnp.ones_like(through_ref)
    sum_ref[...] = jnp.zeros_like(sum_ref)
    inside = jnp.where(block > 0, 1, 0)
    above = jnp.maximum(block - 1, 0)
    mask = [splat(occ[0, block, t]) for t in range(tiles)]
    lead_mask = [splat(occ[0, above, t] * inside) for t in range(tiles)]
    state = (through_ref, sum_ref)
    refs = (frac_vertical, extinction, slice_total)

    def one(s, _):
        parts = []
        for t in range(tiles):
            lanes = slice(t * LANES, (t + 1) * LANES)
            lead = lead_ref[0, s, :, lanes] * lead_mask[t]
            parts.append(jnp.concatenate([lead, x_ref[0, s, :, lanes] * mask[t]], axis=0))
        for t in range(1, tiles):
            pair = jnp.concatenate([parts[t - 1], parts[t]], axis=1)
            x = jnp.dot(pair, weights[s], preferred_element_type=F32)
            shade(s, x[8:], (t - 1) * rows, state, refs)
        return 0

    over_slices(slices, one)
    swap = lax.axis_index("depth") % 2 == 1
    for t in range(tiles - 1):
        finish(state, gain[0], swap, out_keep, out_send, t)


def small_specs():
    return [pl.BlockSpec(memory_space=SMEM)] * 6


def interior(density, small, rank, slice_total):
    _, slices, rows, cols = density.shape
    step = BLK
    width = cols - LANES
    pieces = step // (2 * PIECE)
    image = jax.ShapeDtypeStruct((rows // (2 * PIECE), 2, PIECE, width), F32)
    return pl.pallas_call(
        functools.partial(interior_kernel, slice_total),
        grid=(rows // step,),
        in_specs=small_specs()
        + [pl.BlockSpec(memory_space=SMEM)]
        + [
            pl.BlockSpec((1, slices, step, cols), lambda b: (0, 0, b, 0)),
            pl.BlockSpec(
                (1, slices, 16, cols), lambda b: (0, 0, jnp.maximum(b * (step // 16) - 1, 0), 0)
            ),
        ],
        out_specs=[
            pl.BlockSpec((pieces, 2, PIECE, width), lambda b: (b, 0, 0, 0))
        ]
        * 2
        + [
            pl.BlockSpec((slices, 4 * LANES, LANES), lambda b: (0, 0, 0)),
            pl.BlockSpec((24, cols), lambda b: (0, 0)),
        ],
        out_shape=[
            image,
            image,
            jax.ShapeDtypeStruct((slices, 4 * LANES, LANES), BF16),
            jax.ShapeDtypeStruct((24, cols), F32),
        ],
        scratch_shapes=[pltpu.VMEM((slices, 2 * LANES, LANES), BF16)]
        + [pltpu.VMEM((step * (width // LANES), LANES), F32)] * 2,
        compiler_params=pltpu.CompilerParams(vmem_limit_bytes=32 * 2**20),
        name="interior",
    )(*small, rank, density, density)


def border_kernel(
    start, slice_total, occ, offset, frac_lateral, frac_vertical, extinction, gain, weights,
    first_ref, last_ref, first_lead, last_lead, right_ref, left_ref,
    out_keep, out_send, through_ref, sum_ref,
):
    slices = first_ref.shape[1]
    blocks = first_ref.shape[2] // BLK
    last_tile = occ.shape[2] - 1
    follows = jnp.where(lax.axis_index("lat") < lax.axis_size("lat") - 1, 1, 0)
    refs = (frac_vertical, extinction, slice_total)
    state = (through_ref, sum_ref)
    through_ref[...] = jnp.ones_like(through_ref)
    sum_ref[...] = jnp.zeros_like(sum_ref)
    packing = Packing(offset)
    masks = []
    for b in range(start - 1, start + blocks):
        inside = b >= 0
        masks.append(
            (
                splat(occ[0, b, 0] if inside else 0.0),
                splat(occ[0, b, last_tile] * follows if inside else 0.0),
            )
        )
    top = start * BLK

    def tiles(ref, lead, s, side):
        parts = [lead[0, s] * masks[0][side]]
        for b in range(blocks):
            parts.append(ref[0, s, b * BLK : (b + 1) * BLK] * masks[b + 1][side])
        return jnp.concatenate(parts, axis=0)

    def one(s, _):
        is_left = splat(jnp.where(packing.from_left[s], 1.0, 0.0))
        is_right = splat(jnp.where(packing.from_left[s], 0.0, 1.0))

        def halo(tile):
            rows = slice(top - 16 if start else top, top + blocks * BLK)
            columns = left_ref[tile, rows] * is_left + right_ref[tile, rows] * is_right
            if start == 0:
                columns = jnp.concatenate([jnp.zeros((16, LANES), BF16), columns], axis=0)
            return columns

        tile = packing.tile[s]
        operand = jnp.concatenate(
            [
                tiles(first_ref, first_lead, s, 0),
                tiles(last_ref, last_lead, s, 1),
                halo(tile),
                halo(tile + 1),
            ],
            axis=1,
        )
        x = jnp.dot(operand, weights[s], preferred_element_type=F32)
        for b in range(blocks):
            shade(s, x[b * BLK + 8 : (b + 1) * BLK + 16], b * BLK, state, refs)
        return 0

    over_slices(slices, one)
    swap = lax.axis_index("depth") % 2 == 1
    finish(state, gain[0], swap, out_keep, out_send, 0)


def border(density, small, weights, halos, start, blocks, slice_total):
    _, slices, _, cols = density.shape
    step = blocks * BLK
    last = cols // LANES - 1
    lead_rows = max(start * BLK // 16 - 1, 0)

    def tile(column):
        shape = tuple(pl.Element(n) for n in (1, slices, step, LANES))
        return pl.BlockSpec(shape, lambda i: (0, 0, start * BLK, column * LANES))

    def lead(column):
        return pl.BlockSpec((1, slices, 16, LANES), lambda i: (0, 0, lead_rows, column))

    image = jax.ShapeDtypeStruct((step // (2 * PIECE), 2, PIECE, LANES), F32)
    return pl.pallas_call(
        functools.partial(border_kernel, start, slice_total),
        grid=(1,),
        in_specs=small_specs()
        + [whole(), tile(0), tile(last), lead(0), lead(last), whole(), whole()],
        out_specs=[whole()] * 2,
        out_shape=[image, image],
        scratch_shapes=[pltpu.VMEM((step, LANES), F32)] * 2,
        compiler_params=pltpu.CompilerParams(vmem_limit_bytes=32 * 2**20),
        name=f"border{start}",
    )(*small, weights, density, density, density, density, *halos)


def over(mine, other, in_front):
    color = mine[0] * (1.0 - (1.0 - in_front) * other[1]) + other[0] * (1.0 - in_front * mine[1])
    return color, mine[1] + (1.0 - mine[1]) * other[1]


def over_cores(keep, send, flags):
    count = lax.axis_size("depth")
    other = lax.ppermute(send, "depth", [(i, i ^ 1) for i in range(count)])
    front = flags[0, : keep.shape[3]]
    return jnp.stack(over((keep[:, 0], keep[:, 1]), (other[:, 0], other[:, 1]), front), axis=1)


def over_chips(pieces, flags):
    count = lax.axis_size("depth")
    chips = count // 2
    pieces = (pieces * WIRE_SCALE).astype(WIRE)
    groups = [[2 * i + core for i in range(chips)] for core in range(2)]
    pieces = lax.all_to_all(
        pieces, "depth", 0, 0, axis_index_groups=groups, tiled=True
    )
    pieces = pieces.astype(F32) * (1.0 / WIRE_SCALE)
    level = [(pieces[i, 0], pieces[i, 1]) for i in range(chips)]
    row = 1
    while len(level) > 1:
        half = len(level) // 2
        level = [over(level[2 * i], level[2 * i + 1], flags[row + i]) for i in range(half)]
        row += half
    return level[0]


def shards(
    density, occupancy, shear_offsets, frac_lateral, frac_vertical, extinction, slab_gain, view_rank
):
    _, slices, rows, cols = density.shape
    slice_total = lax.axis_size("depth") * slices
    lat = lax.axis_size("lat")
    density = pltpu.with_memory_space_constraint(density, pltpu.HBM)
    small = (occupancy, shear_offsets, frac_lateral, frac_vertical, extinction, slab_gain)
    blocks = rows // BLK
    rightwards = [(x, x + 1) for x in range(lat - 1)]
    leftwards = [(x, (x - 1) % lat) for x in range(lat)]
    around = [(x, (x + 1) % lat) for x in range(lat)]
    to_left, to_right = pack_halo(density, occupancy, shear_offsets)
    halos = (
        lax.ppermute(to_left, "lat", leftwards),
        lax.ppermute(to_right, "lat", rightwards),
    )
    images = interior(density, small, view_rank, slice_total)
    (keep, send, weights, flags), halos = lax.optimization_barrier((images, halos))
    inner = over_cores(keep, send, flags)

    def edge_rows(first, count, weights):
        image = jnp.stack(border(density, small, weights, halos, first, count, slice_total))
        moved = lax.ppermute((image * WIRE_SCALE).astype(WIRE), "lat", around)
        below = flags[16, :LANES]
        return image, image * (1.0 - below) + moved.astype(F32) * (below / WIRE_SCALE)

    half = blocks // 2
    top, moved_top = edge_rows(0, half, weights)
    weights, _ = lax.optimization_barrier((weights, top))
    _, moved_bottom = edge_rows(half, blocks - half, weights)
    keep, send = jnp.concatenate([moved_top, moved_bottom], axis=1)
    edge = over_cores(keep, send, flags)
    return tuple(over_chips(jnp.concatenate([edge, inner], axis=3), flags))


def solution(mesh):
    placed = (
        P("depth", None, None, "lat"),
        P("depth", None, "lat"),
        P("depth", None),
        P("depth", None),
        P("depth", None),
        P("depth", None),
        P("depth"),
        P(),
    )
    return jax.shard_map(
        shards,
        mesh=mesh,
        in_specs=placed,
        out_specs=(P("depth", "lat"), P("depth", "lat")),
        check_vma=False,
    )
```

```python
import functools
import math

import jax
import jax.numpy as jnp
from jax import lax
from jax.experimental import pallas as pl
from jax.experimental.pallas import tpu as pltpu
from jax.sharding import PartitionSpec as P

SHIFT = 128
BLK = 128
LANES = 128
PIECE = 16
WIRE = jnp.float16
WIRE_SCALE = 4096.0
PACKED = 4 * LANES
LOG2E = math.log2(math.e)
SMEM = pltpu.SMEM
F32 = jnp.float32
BF16 = jnp.bfloat16


def rounded(scalar, shape):
    return jnp.full(shape, scalar, F32).astype(BF16).astype(F32)


def tap(distance, offset, fraction):
    second = jnp.where(distance == offset + 1, fraction, 0.0)
    return jnp.where(distance == offset, 1.0 - fraction, second)


class Packing:
    def __init__(self, offset):
        slices = offset.shape[1]
        lane = lax.broadcasted_iota(jnp.int32, (8, LANES), 1)
        right, left = jnp.zeros_like(lane), jnp.zeros_like(lane)
        for s in range(slices):
            right = right + jnp.maximum(lane - offset[0, s], 0)
            left = left + jnp.maximum(offset[0, s] + 1 - lane, 0)
        fits = (right <= PACKED) & (left <= PACKED)
        self.border = jnp.min(jnp.where(fits, lane.astype(F32), 127.0)).astype(jnp.int32)
        self.from_left, self.count, self.tile, self.first = [], [], [], []
        used = [0, 0]
        for s in range(slices):
            o = offset[0, s]
            from_left = o >= self.border
            count = jnp.where(from_left, o + 1 - self.border, self.border - o)
            first = jnp.where(from_left, used[1], used[0])
            used[1] = used[1] + jnp.where(from_left, count, 0)
            used[0] = used[0] + jnp.where(from_left, 0, count)
            tile = jnp.minimum(jnp.right_shift(first, 7), PACKED // LANES - 2)
            self.from_left.append(from_left)
            self.count.append(count)
            self.tile.append(tile)
            self.first.append(first - LANES * tile)


def pack_kernel(occ, offset, density, to_left, to_right, columns, picks, packed, arrived):
    slices, rows, cols = density.shape[1:]
    packing = Packing(offset)
    copies = []
    for s in range(slices):
        column = pl.multiple_of(jnp.where(packing.from_left[s], cols - LANES, 0), LANES)
        copy = pltpu.make_async_copy(
            density.at[0, s, :, pl.ds(column, LANES)], columns.at[s], arrived.at[s]
        )
        copy.start()
        copies.append(copy)
    k = lax.broadcasted_iota(jnp.int32, (LANES, 2 * LANES), 0)
    p = lax.broadcasted_iota(jnp.int32, (LANES, 2 * LANES), 1)
    for s in range(slices):
        skip = jnp.where(packing.from_left[s], LANES - packing.count[s], 0)
        inside = (k >= skip) & (k < skip + packing.count[s])
        same = k - skip == p - packing.first[s]
        picks[s] = jnp.where(inside & same, 1.0, 0.0).astype(BF16)
    packed[...] = jnp.zeros_like(packed)
    last = occ.shape[2] - 1
    for s in range(slices):
        copies[s].wait()
        from_left = packing.from_left[s]
        way = jnp.where(from_left, 1, 0)
        tile = packing.tile[s]
        for b in range(rows // BLK):
            at = slice(b * BLK, (b + 1) * BLK)
            occupied = jnp.where(from_left, occ[0, b, last], occ[0, b, 0])
            moved = jnp.dot(
                columns[s, at] * splat(occupied), picks[s], preferred_element_type=F32
            ).astype(BF16)
            packed[way, tile, at] += moved[:, :LANES]
            packed[way, tile + 1, at] += moved[:, LANES:]
    to_left[...] = packed[0]
    to_right[...] = packed[1]


def pack_halo(density, occupancy, offsets):
    _, slices, rows, _ = density.shape
    tiles = PACKED // LANES
    shape = jax.ShapeDtypeStruct((tiles, rows, LANES), BF16)
    return pl.pallas_call(
        pack_kernel,
        in_specs=[
            pl.BlockSpec(memory_space=SMEM),
            pl.BlockSpec(memory_space=SMEM),
            pl.BlockSpec(memory_space=pl.ANY),
        ],
        out_specs=[whole()] * 2,
        out_shape=[shape, shape],
        scratch_shapes=[
            pltpu.VMEM((slices, rows, LANES), BF16),
            pltpu.VMEM((slices, LANES, 2 * LANES), BF16),
            pltpu.VMEM((2, tiles, rows, LANES), BF16),
            pltpu.SemaphoreType.DMA((slices,)),
        ],
        compiler_params=pltpu.CompilerParams(vmem_limit_bytes=32 * 2**20),
        name="pack_halo",
    )(occupancy, offsets, density)


def whole():
    return pl.BlockSpec(memory_space=pltpu.VMEM)


def border_weights(s, offset, frac_lateral, packing, weights, out):
    n = lax.broadcasted_iota(jnp.int32, (2 * LANES, LANES), 1)
    p = lax.broadcasted_iota(jnp.int32, (2 * LANES, LANES), 0)
    own = jnp.where(n[:1] >= packing.border, 1.0, 0.0)
    out[s, :LANES] = weights[s, LANES:] * own.astype(BF16)
    out[s, LANES : 2 * LANES] = weights[s, :LANES] * (1.0 - own).astype(BF16)
    from_left, count = packing.from_left[s], packing.count[s]
    index = p - packing.first[s]
    reach = n + jnp.where(from_left, count, 0) - index
    weight = tap(reach, offset[0, s], frac_lateral[0, s])
    weight = jnp.where((index >= 0) & (index < count), weight, 0.0)
    mine = jnp.where(from_left, own, 1.0 - own)
    out[s, 2 * LANES :] = (weight * mine).astype(BF16)


def shade(s, x, base, state, refs):
    frac_vertical, extinction, slice_total = refs
    through_ref, sum_ref = state
    rows = x.shape[0] - 8
    v0 = 2.0 * rounded(1.0 - frac_vertical[0, s], (1, LANES))
    v1 = 2.0 * rounded(frac_vertical[0, s], (1, LANES))
    density = v0 * x + v1 * pltpu.roll(x, 1, 0)
    above = pltpu.roll(density, 1, 0)
    density, above = density[8:], above[8:]
    rate = extinction[0, s] * (-LOG2E / (2.0 * slice_total))
    kept = jnp.exp2(rate * density)
    slope = jnp.tanh(density - above)
    at = slice(base, base + rows)
    through = through_ref[at]
    after = through * kept
    through_ref[at] = after
    sum_ref[at] += (through - after) * slope


def finish(state, gain, swap, out_keep, out_send, tile):
    through_ref, sum_ref = state
    rows = out_keep.shape[0] * 2 * PIECE
    base = tile * rows
    alphas, colors = [], []
    for p in range(rows // PIECE):
        at = slice(base + p * PIECE, base + (p + 1) * PIECE)
        alpha = 1.0 - through_ref[at]
        alphas.append(alpha)
        colors.append(gain * (0.65 * alpha + 0.35 * sum_ref[at]))
    lanes = slice(tile * LANES, (tile + 1) * LANES)
    for q in range(rows // PIECE // 2):
        for i, values in enumerate((colors, alphas)):
            even, odd = values[2 * q], values[2 * q + 1]
            out_keep[q, i, :, lanes] = jnp.where(swap, odd, even)
            out_send[q, i, :, lanes] = jnp.where(swap, even, odd)


def splat(value):
    return jnp.full((1, LANES), value, F32).astype(BF16)


def over_slices(slices, one):
    for s in range(slices):
        one(s, 0)


def interior_kernel(
    slice_total, occ, offset, frac_lateral, frac_vertical, extinction, gain, rank,
    x_ref, lead_ref, out_keep, out_send, out_weights, flags, weights, through_ref, sum_ref,
):
    block = pl.program_id(0)
    slices, rows = x_ref.shape[1], x_ref.shape[2]
    tiles = x_ref.shape[3] // LANES

    @pl.when(block == 0)
    def _():
        k = lax.broadcasted_iota(jnp.int32, (2 * LANES, LANES), 0)
        n = lax.broadcasted_iota(jnp.int32, (2 * LANES, LANES), 1)

        def build(s, _):
            weights[s] = tap(LANES + n - k, offset[0, s], frac_lateral[0, s]).astype(BF16)
            return 0

        lax.fori_loop(0, slices, build, 0)
        packing = Packing(offset)
        for s in range(slices):
            border_weights(s, offset, frac_lateral, packing, weights, out_weights)
        lane = lax.broadcasted_iota(jnp.int32, (1, flags.shape[1]), 1)
        flags[16:17] = jnp.where(lane < packing.border, 1.0, 0.0)
        me = lax.axis_index("depth")
        in_front = [rank[me] < rank[jnp.bitwise_xor(me, 1)]]
        for span in (2, 4, 8, 16):
            in_front += [rank[a] < rank[a + span] for a in range(0, rank.shape[0], 2 * span)]
        for i, flag in enumerate(in_front):
            flags[i : i + 1] = jnp.full((1, flags.shape[1]), jnp.where(flag, 1.0, 0.0), F32)

    through_ref[...] = jnp.ones_like(through_ref)
    sum_ref[...] = jnp.zeros_like(sum_ref)
    inside = jnp.where(block > 0, 1, 0)
    above = jnp.maximum(block - 1, 0)
    mask = [splat(occ[0, block, t]) for t in range(tiles)]
    lead_mask = [splat(occ[0, above, t] * inside) for t in range(tiles)]
    state = (through_ref, sum_ref)
    refs = (frac_vertical, extinction, slice_total)

    def one(s, _):
        parts = []
        for t in range(tiles):
            lanes = slice(t * LANES, (t + 1) * LANES)
            lead = lead_ref[0, s, :, lanes] * lead_mask[t]
            parts.append(jnp.concatenate([lead, x_ref[0, s, :, lanes] * mask[t]], axis=0))
        for t in range(1, tiles):
            pair = jnp.concatenate([parts[t - 1], parts[t]], axis=1)
            x = jnp.dot(pair, weights[s], preferred_element_type=F32)
            shade(s, x[8:], (t - 1) * rows, state, refs)
        return 0

    over_slices(slices, one)
    swap = lax.axis_index("depth") % 2 == 1
    for t in range(tiles - 1):
        finish(state, gain[0], swap, out_keep, out_send, t)


def small_specs():
    return [pl.BlockSpec(memory_space=SMEM)] * 6


def interior(density, small, rank, slice_total):
    _, slices, rows, cols = density.shape
    step = BLK
    width = cols - LANES
    pieces = step // (2 * PIECE)
    image = jax.ShapeDtypeStruct((rows // (2 * PIECE), 2, PIECE, width), F32)
    return pl.pallas_call(
        functools.partial(interior_kernel, slice_total),
        grid=(rows // step,),
        in_specs=small_specs()
        + [pl.BlockSpec(memory_space=SMEM)]
        + [
            pl.BlockSpec((1, slices, step, cols), lambda b: (0, 0, b, 0)),
            pl.BlockSpec(
                (1, slices, 16, cols), lambda b: (0, 0, jnp.maximum(b * (step // 16) - 1, 0), 0)
            ),
        ],
        out_specs=[
            pl.BlockSpec((pieces, 2, PIECE, width), lambda b: (b, 0, 0, 0))
        ]
        * 2
        + [
            pl.BlockSpec((slices, 4 * LANES, LANES), lambda b: (0, 0, 0)),
            pl.BlockSpec((24, cols), lambda b: (0, 0)),
        ],
        out_shape=[
            image,
            image,
            jax.ShapeDtypeStruct((slices, 4 * LANES, LANES), BF16),
            jax.ShapeDtypeStruct((24, cols), F32),
        ],
        scratch_shapes=[pltpu.VMEM((slices, 2 * LANES, LANES), BF16)]
        + [pltpu.VMEM((step * (width // LANES), LANES), F32)] * 2,
        compiler_params=pltpu.CompilerParams(vmem_limit_bytes=32 * 2**20),
        name="interior",
    )(*small, rank, density, density)


def border_kernel(
    start, slice_total, occ, offset, frac_lateral, frac_vertical, extinction, gain, weights,
    first_ref, last_ref, first_lead, last_lead, right_ref, left_ref,
    out_keep, out_send, through_ref, sum_ref,
):
    slices = first_ref.shape[1]
    blocks = first_ref.shape[2] // BLK
    last_tile = occ.shape[2] - 1
    follows = jnp.where(lax.axis_index("lat") < lax.axis_size("lat") - 1, 1, 0)
    refs = (frac_vertical, extinction, slice_total)
    state = (through_ref, sum_ref)
    through_ref[...] = jnp.ones_like(through_ref)
    sum_ref[...] = jnp.zeros_like(sum_ref)
    packing = Packing(offset)
    masks = []
    for b in range(start - 1, start + blocks):
        inside = b >= 0
        masks.append(
            (
                splat(occ[0, b, 0] if inside else 0.0),
                splat(occ[0, b, last_tile] * follows if inside else 0.0),
            )
        )
    top = start * BLK

    def tiles(ref, lead, s, side):
        parts = [lead[0, s] * masks[0][side]]
        for b in range(blocks):
            parts.append(ref[0, s, b * BLK : (b + 1) * BLK] * masks[b + 1][side])
        return jnp.concatenate(parts, axis=0)

    def one(s, _):
        is_left = splat(jnp.where(packing.from_left[s], 1.0, 0.0))
        is_right = splat(jnp.where(packing.from_left[s], 0.0, 1.0))

        def halo(tile):
            rows = slice(top - 16 if start else top, top + blocks * BLK)
            columns = left_ref[tile, rows] * is_left + right_ref[tile, rows] * is_right
            if start == 0:
                columns = jnp.concatenate([jnp.zeros((16, LANES), BF16), columns], axis=0)
            return columns

        tile = packing.tile[s]
        operand = jnp.concatenate(
            [
                tiles(first_ref, first_lead, s, 0),
                tiles(last_ref, last_lead, s, 1),
                halo(tile),
                halo(tile + 1),
            ],
            axis=1,
        )
        x = jnp.dot(operand, weights[s], preferred_element_type=F32)
        for b in range(blocks):
            shade(s, x[b * BLK + 8 : (b + 1) * BLK + 16], b * BLK, state, refs)
        return 0

    over_slices(slices, one)
    swap = lax.axis_index("depth") % 2 == 1
    finish(state, gain[0], swap, out_keep, out_send, 0)


def border(density, small, weights, halos, start, blocks, slice_total):
    _, slices, _, cols = density.shape
    step = blocks * BLK
    last = cols // LANES - 1
    lead_rows = max(start * BLK // 16 - 1, 0)

    def tile(column):
        shape = tuple(pl.Element(n) for n in (1, slices, step, LANES))
        return pl.BlockSpec(shape, lambda i: (0, 0, start * BLK, column * LANES))

    def lead(column):
        return pl.BlockSpec((1, slices, 16, LANES), lambda i: (0, 0, lead_rows, column))

    image = jax.ShapeDtypeStruct((step // (2 * PIECE), 2, PIECE, LANES), F32)
    return pl.pallas_call(
        functools.partial(border_kernel, start, slice_total),
        grid=(1,),
        in_specs=small_specs()
        + [whole(), tile(0), tile(last), lead(0), lead(last), whole(), whole()],
        out_specs=[whole()] * 2,
        out_shape=[image, image],
        scratch_shapes=[pltpu.VMEM((step, LANES), F32)] * 2,
        compiler_params=pltpu.CompilerParams(vmem_limit_bytes=32 * 2**20),
        name=f"border{start}",
    )(*small, weights, density, density, density, density, *halos)


def over(mine, other, in_front):
    color = mine[0] * (1.0 - (1.0 - in_front) * other[1]) + other[0] * (1.0 - in_front * mine[1])
    return color, mine[1] + (1.0 - mine[1]) * other[1]


def over_cores(keep, send, flags):
    count = lax.axis_size("depth")
    other = lax.ppermute(send, "depth", [(i, i ^ 1) for i in range(count)])
    front = flags[0, : keep.shape[3]]
    return jnp.stack(over((keep[:, 0], keep[:, 1]), (other[:, 0], other[:, 1]), front), axis=1)


def wire(image):
    return (image * WIRE_SCALE).astype(WIRE)


def over_chips(pieces, flags):
    count = lax.axis_size("depth")
    chips = count // 2
    pieces = wire(pieces)
    groups = [[2 * i + core for i in range(chips)] for core in range(2)]
    pieces = lax.all_to_all(
        pieces, "depth", 0, 0, axis_index_groups=groups, tiled=True
    )
    pieces = pieces.astype(F32) * (1.0 / WIRE_SCALE)
    level = [(pieces[i, 0], pieces[i, 1]) for i in range(chips)]
    row = 1
    while len(level) > 1:
        half = len(level) // 2
        level = [over(level[2 * i], level[2 * i + 1], flags[row + i]) for i in range(half)]
        row += half
    return level[0]


def shards(
    density, occupancy, shear_offsets, frac_lateral, frac_vertical, extinction, slab_gain, view_rank
):
    _, slices, rows, cols = density.shape
    slice_total = lax.axis_size("depth") * slices
    lat = lax.axis_size("lat")
    density = pltpu.with_memory_space_constraint(density, pltpu.HBM)
    small = (occupancy, shear_offsets, frac_lateral, frac_vertical, extinction, slab_gain)
    blocks = rows // BLK
    rightwards = [(x, x + 1) for x in range(lat - 1)]
    leftwards = [(x, (x - 1) % lat) for x in range(lat)]
    around = [(x, (x + 1) % lat) for x in range(lat)]
    to_left, to_right = pack_halo(density, occupancy, shear_offsets)
    halos = (
        lax.ppermute(to_left, "lat", leftwards),
        lax.ppermute(to_right, "lat", rightwards),
    )
    images = interior(density, small, view_rank, slice_total)
    (keep, send, weights, flags), halos = lax.optimization_barrier((images, halos))
    inner = over_cores(keep, send, flags)

    half = blocks // 2
    tops = jnp.stack(border(density, small, weights, halos, 0, half, slice_total))
    moved_tops = lax.ppermute(wire(tops), "lat", around)
    weights, tops = lax.optimization_barrier((weights, tops))
    ends = jnp.stack(border(density, small, weights, halos, half, blocks - half, slice_total))
    ends, moved_tops = lax.optimization_barrier((ends, moved_tops))
    moved_ends = lax.ppermute(wire(ends), "lat", around)
    images = jnp.concatenate([tops, ends], axis=1)
    moved = jnp.concatenate([moved_tops, moved_ends], axis=1)
    below = flags[16, :LANES]
    keep, send = images * (1.0 - below) + moved.astype(F32) * (below / WIRE_SCALE)
    edge = over_cores(keep, send, flags)
    return tuple(over_chips(jnp.concatenate([edge, inner], axis=3), flags))


def solution(mesh):
    placed = (
        P("depth", None, None, "lat"),
        P("depth", None, "lat"),
        P("depth", None),
        P("depth", None),
        P("depth", None),
        P("depth", None),
        P("depth"),
        P(),
    )
    return jax.shard_map(
        shards,
        mesh=mesh,
        in_specs=placed,
        out_specs=(P("depth", "lat"), P("depth", "lat")),
        check_vma=False,
    )
```

```python
import functools
import math

import jax
import jax.numpy as jnp
from jax import lax
from jax.experimental import pallas as pl
from jax.experimental.pallas import tpu as pltpu
from jax.sharding import PartitionSpec as P

SHIFT = 128
BLK = 128
LANES = 128
PIECE = 16
WIRE = jnp.float16
WIRE_SCALE = 4096.0
PACKED = 5 * LANES
HALF = SHIFT // 2
LOG2E = math.log2(math.e)
SMEM = pltpu.SMEM
F32 = jnp.float32
BF16 = jnp.bfloat16


def rounded(scalar, shape):
    return jnp.full(shape, scalar, F32).astype(BF16).astype(F32)


def tap(distance, offset, fraction):
    second = jnp.where(distance == offset + 1, fraction, 0.0)
    return jnp.where(distance == offset, 1.0 - fraction, second)


class Packing:
    def __init__(self, offset):
        slices = offset.shape[1]
        self.border = HALF
        self.from_left, self.count, self.tile, self.first = [], [], [], []
        used = [0, 0]
        for s in range(slices):
            o = offset[0, s]
            from_left = o >= self.border
            count = jnp.where(from_left, o + 1 - self.border, self.border - o)
            first = jnp.where(from_left, used[1], used[0])
            used[1] = used[1] + jnp.where(from_left, count, 0)
            used[0] = used[0] + jnp.where(from_left, 0, count)
            tile = jnp.minimum(jnp.right_shift(first, 7), PACKED // LANES - 2)
            self.from_left.append(from_left)
            self.count.append(count)
            self.tile.append(tile)
            self.first.append(first - LANES * tile)
        self.overflow = jnp.maximum(used[0], used[1]) > PACKED


def pack_kernel(occ, offset, x_first, x_last, to_left, to_right, picks, packed):
    block = pl.program_id(0)
    slices, cols = x_first.shape[1], LANES
    packing = Packing(offset)

    @pl.when(block == 0)
    def _():
        k = lax.broadcasted_iota(jnp.int32, (LANES, 2 * LANES), 0)
        p = lax.broadcasted_iota(jnp.int32, (LANES, 2 * LANES), 1)
        for s in range(slices):
            skip = jnp.where(packing.from_left[s], cols - packing.count[s], 0)
            inside = (k >= skip) & (k < skip + packing.count[s])
            same = k - skip == p - packing.first[s]
            picks[s] = jnp.where(inside & same, 1.0, 0.0).astype(BF16)

    packed[...] = jnp.zeros_like(packed)
    first_occ = occ[0, block, 0].astype(F32)
    last_occ = occ[0, block, occ.shape[2] - 1].astype(F32)
    for s in range(slices):
        from_left = packing.from_left[s]
        columns = x_first[0, s] * splat(jnp.where(from_left, 0.0, first_occ)) + x_last[
            0, s
        ] * splat(jnp.where(from_left, last_occ, 0.0))
        moved = jnp.dot(columns, picks[s], preferred_element_type=F32).astype(BF16)
        way = jnp.where(from_left, 1, 0)
        tile = packing.tile[s]
        packed[way, tile] += moved[:, :LANES]
        packed[way, tile + 1] += moved[:, LANES:]
    to_left[...] = packed[0]
    to_right[...] = packed[1]


def pack_halo(density, occupancy, offsets):
    _, slices, rows, cols = density.shape
    tiles = PACKED // LANES
    shape = jax.ShapeDtypeStruct((tiles, rows, LANES), BF16)
    last = cols // LANES - 1
    return pl.pallas_call(
        pack_kernel,
        grid=(rows // BLK,),
        in_specs=[
            pl.BlockSpec(memory_space=SMEM),
            pl.BlockSpec(memory_space=SMEM),
            pl.BlockSpec((1, slices, BLK, LANES), lambda b: (0, 0, b, 0)),
            pl.BlockSpec((1, slices, BLK, LANES), lambda b: (0, 0, b, last)),
        ],
        out_specs=[pl.BlockSpec((tiles, BLK, LANES), lambda b: (0, b, 0))] * 2,
        out_shape=[shape, shape],
        scratch_shapes=[
            pltpu.VMEM((slices, LANES, 2 * LANES), BF16),
            pltpu.VMEM((2, tiles, BLK, LANES), BF16),
        ],
        name="pack_halo",
    )(occupancy, offsets, density, density)


def whole():
    return pl.BlockSpec(memory_space=pltpu.VMEM)


def border_weights(s, offset, frac_lateral, packing, weights, out):
    n = lax.broadcasted_iota(jnp.int32, (2 * LANES, LANES), 1)
    p = lax.broadcasted_iota(jnp.int32, (2 * LANES, LANES), 0)
    own = jnp.where(n[:1] >= packing.border, 1.0, 0.0)
    out[s, :LANES] = weights[s, LANES:] * own.astype(BF16)
    out[s, LANES : 2 * LANES] = weights[s, :LANES] * (1.0 - own).astype(BF16)
    from_left, count = packing.from_left[s], packing.count[s]
    index = p - packing.first[s]
    reach = n + jnp.where(from_left, count, 0) - index
    weight = tap(reach, offset[0, s], frac_lateral[0, s])
    weight = jnp.where((index >= 0) & (index < count), weight, 0.0)
    mine = jnp.where(from_left, own, 1.0 - own)
    out[s, 2 * LANES :] = (weight * mine).astype(BF16)


def shade(s, x, base, state, refs):
    frac_vertical, extinction, slice_total = refs
    through_ref, sum_ref = state
    rows = x.shape[0] - 8
    v0 = 2.0 * rounded(1.0 - frac_vertical[0, s], (1, LANES))
    v1 = 2.0 * rounded(frac_vertical[0, s], (1, LANES))
    density = v0 * x + v1 * pltpu.roll(x, 1, 0)
    above = pltpu.roll(density, 1, 0)
    density, above = density[8:], above[8:]
    rate = extinction[0, s] * (-LOG2E / (2.0 * slice_total))
    kept = jnp.exp2(rate * density)
    slope = jnp.tanh(density - above)
    at = slice(base, base + rows)
    through = through_ref[at]
    after = through * kept
    through_ref[at] = after
    sum_ref[at] += (through - after) * slope


def finish(state, gain, swap, out_keep, out_send, tile):
    through_ref, sum_ref = state
    rows = out_keep.shape[0] * 2 * PIECE
    base = tile * rows
    alphas, colors = [], []
    for p in range(rows // PIECE):
        at = slice(base + p * PIECE, base + (p + 1) * PIECE)
        alpha = 1.0 - through_ref[at]
        alphas.append(alpha)
        colors.append(gain * (0.65 * alpha + 0.35 * sum_ref[at]))
    lanes = slice(tile * LANES, (tile + 1) * LANES)
    for q in range(rows // PIECE // 2):
        for i, values in enumerate((colors, alphas)):
            even, odd = values[2 * q], values[2 * q + 1]
            out_keep[q, i, :, lanes] = jnp.where(swap, odd, even)
            out_send[q, i, :, lanes] = jnp.where(swap, even, odd)


def splat(value):
    return jnp.full((1, LANES), value, F32).astype(BF16)


def over_slices(slices, one):
    for s in range(slices):
        one(s, 0)


def interior_kernel(
    slice_total, occ, offset, frac_lateral, frac_vertical, extinction, gain, rank,
    x_ref, lead_ref, out_keep, out_send, out_weights, weights, flags, overflow, through_ref, sum_ref,
):
    block = pl.program_id(0)
    slices, rows = x_ref.shape[1], x_ref.shape[2]
    tiles = x_ref.shape[3] // LANES

    @pl.when(block == 0)
    def _():
        k = lax.broadcasted_iota(jnp.int32, (2 * LANES, LANES), 0)
        n = lax.broadcasted_iota(jnp.int32, (2 * LANES, LANES), 1)

        def build(s, _):
            weights[s] = tap(LANES + n - k, offset[0, s], frac_lateral[0, s]).astype(BF16)
            return 0

        lax.fori_loop(0, slices, build, 0)
        packing = Packing(offset)
        for s in range(slices):
            border_weights(s, offset, frac_lateral, packing, weights, out_weights)
        overflow[0] = jnp.where(packing.overflow, 1, 0)
        me = lax.axis_index("depth")
        in_front = [rank[me] < rank[jnp.bitwise_xor(me, 1)]]
        for span in (2, 4, 8, 16):
            in_front += [rank[a] < rank[a + span] for a in range(0, rank.shape[0], 2 * span)]
        for i, flag in enumerate(in_front):
            flags[i : i + 1] = jnp.full((1, flags.shape[1]), jnp.where(flag, 1.0, 0.0), F32)

    through_ref[...] = jnp.ones_like(through_ref)
    sum_ref[...] = jnp.zeros_like(sum_ref)
    inside = jnp.where(block > 0, 1, 0)
    above = jnp.maximum(block - 1, 0)
    mask = [splat(occ[0, block, t]) for t in range(tiles)]
    lead_mask = [splat(occ[0, above, t] * inside) for t in range(tiles)]
    state = (through_ref, sum_ref)
    refs = (frac_vertical, extinction, slice_total)

    def one(s, _):
        parts = []
        for t in range(tiles):
            lanes = slice(t * LANES, (t + 1) * LANES)
            lead = lead_ref[0, s, :, lanes] * lead_mask[t]
            parts.append(jnp.concatenate([lead, x_ref[0, s, :, lanes] * mask[t]], axis=0))
        for t in range(1, tiles):
            pair = jnp.concatenate([parts[t - 1], parts[t]], axis=1)
            x = jnp.dot(pair, weights[s], preferred_element_type=F32)
            shade(s, x[8:], (t - 1) * rows, state, refs)
        return 0

    over_slices(slices, one)
    swap = lax.axis_index("depth") % 2 == 1
    for t in range(tiles - 1):
        finish(state, gain[0], swap, out_keep, out_send, t)


def small_specs():
    return [pl.BlockSpec(memory_space=SMEM)] * 6


def interior(density, small, rank, slice_total):
    _, slices, rows, cols = density.shape
    step = BLK
    width = cols - LANES
    pieces = step // (2 * PIECE)
    image = jax.ShapeDtypeStruct((rows // (2 * PIECE), 2, PIECE, width), F32)
    return pl.pallas_call(
        functools.partial(interior_kernel, slice_total),
        grid=(rows // step,),
        in_specs=small_specs()
        + [pl.BlockSpec(memory_space=SMEM)]
        + [
            pl.BlockSpec((1, slices, step, cols), lambda b: (0, 0, b, 0)),
            pl.BlockSpec(
                (1, slices, 16, cols), lambda b: (0, 0, jnp.maximum(b * (step // 16) - 1, 0), 0)
            ),
        ],
        out_specs=[
            pl.BlockSpec((pieces, 2, PIECE, width), lambda b: (b, 0, 0, 0))
        ]
        * 2
        + [
            pl.BlockSpec((slices, 4 * LANES, LANES), lambda b: (0, 0, 0)),
            pl.BlockSpec((slices, 2 * LANES, LANES), lambda b: (0, 0, 0)),
            pl.BlockSpec((16, cols), lambda b: (0, 0)),
            pl.BlockSpec(memory_space=SMEM),
        ],
        out_shape=[
            image,
            image,
            jax.ShapeDtypeStruct((slices, 4 * LANES, LANES), BF16),
            jax.ShapeDtypeStruct((slices, 2 * LANES, LANES), BF16),
            jax.ShapeDtypeStruct((16, cols), F32),
            jax.ShapeDtypeStruct((1,), jnp.int32),
        ],
        scratch_shapes=[pltpu.VMEM((step * (width // LANES), LANES), F32)] * 2,
        compiler_params=pltpu.CompilerParams(vmem_limit_bytes=32 * 2**20),
        name="interior",
    )(*small, rank, density, density)


def border_kernel(
    start, slice_total, occ, offset, frac_lateral, frac_vertical, extinction, gain, weights,
    first_ref, last_ref, first_lead, last_lead, right_ref, left_ref,
    out_keep, out_send, through_ref, sum_ref,
):
    slices = first_ref.shape[1]
    blocks = first_ref.shape[2] // BLK
    last_tile = occ.shape[2] - 1
    follows = jnp.where(lax.axis_index("lat") < lax.axis_size("lat") - 1, 1, 0)
    refs = (frac_vertical, extinction, slice_total)
    state = (through_ref, sum_ref)
    through_ref[...] = jnp.ones_like(through_ref)
    sum_ref[...] = jnp.zeros_like(sum_ref)
    packing = Packing(offset)
    masks = []
    for b in range(start - 1, start + blocks):
        inside = b >= 0
        masks.append(
            (
                splat(occ[0, b, 0] if inside else 0.0),
                splat(occ[0, b, last_tile] * follows if inside else 0.0),
            )
        )
    top = start * BLK

    def tiles(ref, lead, s, side):
        parts = [lead[0, s] * masks[0][side]]
        for b in range(blocks):
            parts.append(ref[0, s, b * BLK : (b + 1) * BLK] * masks[b + 1][side])
        return jnp.concatenate(parts, axis=0)

    def one(s, _):
        is_left = splat(jnp.where(packing.from_left[s], 1.0, 0.0))
        is_right = splat(jnp.where(packing.from_left[s], 0.0, 1.0))

        def halo(tile):
            rows = slice(top - 16 if start else top, top + blocks * BLK)
            columns = left_ref[tile, rows] * is_left + right_ref[tile, rows] * is_right
            if start == 0:
                columns = jnp.concatenate([jnp.zeros((16, LANES), BF16), columns], axis=0)
            return columns

        tile = packing.tile[s]
        operand = jnp.concatenate(
            [
                tiles(first_ref, first_lead, s, 0),
                tiles(last_ref, last_lead, s, 1),
                halo(tile),
                halo(tile + 1),
            ],
            axis=1,
        )
        x = jnp.dot(operand, weights[s], preferred_element_type=F32)
        for b in range(blocks):
            shade(s, x[b * BLK + 8 : (b + 1) * BLK + 16], b * BLK, state, refs)
        return 0

    over_slices(slices, one)
    swap = lax.axis_index("depth") % 2 == 1
    finish(state, gain[0], swap, out_keep, out_send, 0)


def border(density, small, weights, halos, start, blocks, slice_total):
    _, slices, _, cols = density.shape
    step = blocks * BLK
    last = cols // LANES - 1
    lead_rows = max(start * BLK // 16 - 1, 0)

    def tile(column):
        shape = tuple(pl.Element(n) for n in (1, slices, step, LANES))
        return pl.BlockSpec(shape, lambda i: (0, 0, start * BLK, column * LANES))

    def lead(column):
        return pl.BlockSpec((1, slices, 16, LANES), lambda i: (0, 0, lead_rows, column))

    image = jax.ShapeDtypeStruct((step // (2 * PIECE), 2, PIECE, LANES), F32)
    return pl.pallas_call(
        functools.partial(border_kernel, start, slice_total),
        grid=(1,),
        in_specs=small_specs()
        + [whole(), tile(0), tile(last), lead(0), lead(last), whole(), whole()],
        out_specs=[whole()] * 2,
        out_shape=[image, image],
        scratch_shapes=[pltpu.VMEM((step, LANES), F32)] * 2,
        compiler_params=pltpu.CompilerParams(vmem_limit_bytes=32 * 2**20),
        name=f"border{start}",
    )(*small, weights, density, density, density, density, *halos)


def column_tile(slices, first, blocks, column):
    shape = tuple(pl.Element(n) for n in (1, slices, blocks * BLK, LANES))
    return pl.BlockSpec(
        shape, lambda i: (0, i * (slices), first * BLK, column * LANES)
    )


def strips_kernel(first_block, occ, x_first, x_last, to_left, to_right):
    half = x_first.shape[2] // 2
    block = first_block + pl.program_id(0)
    k = lax.broadcasted_iota(jnp.int32, (2 * LANES, LANES), 0)
    n = lax.broadcasted_iota(jnp.int32, (2 * LANES, LANES), 1)
    for ref, out, column, source in (
        (x_first, to_left, 0, jnp.where(n < HALF, n, n + HALF)),
        (x_last, to_right, occ.shape[2] - 1, jnp.where(n < HALF, n + LANES + HALF, n)),
    ):
        occupied = occ[0, block, column].astype(F32)
        pick = jnp.where(k == source, occupied, 0.0).astype(BF16)
        for s in range(ref.shape[1]):
            rows = jnp.concatenate([ref[0, s, :half], ref[0, s, half:]], axis=1)
            out[s] = jnp.dot(rows, pick, preferred_element_type=F32).astype(BF16)


def edge_strips(density, occupancy, first, blocks):
    _, slices, _, cols = density.shape
    shape = jax.ShapeDtypeStruct((slices, blocks * BLK // 2, LANES), BF16)
    last = cols // LANES - 1
    return pl.pallas_call(
        functools.partial(strips_kernel, first),
        grid=(blocks,),
        in_specs=[
            pl.BlockSpec(memory_space=SMEM),
            pl.BlockSpec((1, slices, BLK, LANES), lambda i: (0, 0, first + i, 0)),
            pl.BlockSpec((1, slices, BLK, LANES), lambda i: (0, 0, first + i, last)),
        ],
        out_specs=[pl.BlockSpec((slices, BLK // 2, LANES), lambda i: (0, i, 0))] * 2,
        out_shape=[shape, shape],
        name=f"edge_strips{first}",
    )(occupancy, density, density)


def full_border_kernel(
    start, slice_total, occ, offset, frac_lateral, frac_vertical, extinction, gain, weights,
    first_ref, last_ref, first_lead, last_lead, right_ref, left_ref, right_lead, left_lead,
    out_keep, out_send, through_ref, sum_ref,
):
    count, half = first_ref.shape[1], BLK // 2
    step = pl.program_id(0)
    last_tile = occ.shape[2] - 1
    follows = jnp.where(lax.axis_index("lat") < lax.axis_size("lat") - 1, 1, 0)
    own_lanes = lax.broadcasted_iota(jnp.int32, (1, LANES), 1) >= HALF
    refs = (frac_vertical, extinction, slice_total)
    state = (through_ref, sum_ref)

    @pl.when(step == 0)
    def _():
        through_ref[...] = jnp.ones_like(through_ref)
        sum_ref[...] = jnp.zeros_like(sum_ref)

    blocks = first_ref.shape[2] // BLK
    masks = []
    for b in range(start - 1, start + blocks):
        inside = b >= 0
        masks.append(
            (
                splat(occ[0, b, 0] if inside else 0.0),
                splat(occ[0, b, last_tile] * follows if inside else 0.0),
            )
        )
    zero = jnp.zeros((16, LANES), BF16)

    def one(u, _):
        s = step * count + u
        before, own = weights[s, :LANES], weights[s, LANES:]
        turn = lambda w: jnp.concatenate([w[HALF:], w[:HALF]], axis=0)
        near = jnp.concatenate([before, own], axis=0)
        far_left = jnp.concatenate([turn(before), own], axis=0)
        far_right = jnp.concatenate([before, turn(own)], axis=0)

        def halves(ref, side, top, above):
            parts = [above] if above is not None else []
            for b in range(blocks):
                at = slice(b * BLK + top, b * BLK + top + half)
                parts.append(ref[0, u, at] * masks[b + 1][side])
            return jnp.concatenate(parts, axis=0) if len(parts) > 1 else parts[0]

        def lateral(first, last, right, left, w_left, w_right):
            here = jnp.dot(
                jnp.concatenate([left, first], axis=1), w_left, preferred_element_type=F32
            )
            there = jnp.dot(
                jnp.concatenate([last, right], axis=1), w_right, preferred_element_type=F32
            )
            return jnp.where(own_lanes, here, there)

        right, left = right_ref[s], left_ref[s]
        x_near = lateral(
            halves(first_ref, 0, 0, None), halves(last_ref, 1, 0, None), right, left, near, near
        )
        x_far = lateral(
            halves(first_ref, 0, half, first_lead[0, u] * masks[0][0]),
            halves(last_ref, 1, half, last_lead[0, u] * masks[0][1]),
            jnp.concatenate([right_lead[s, -16:] if start else zero, right], axis=0),
            jnp.concatenate([left_lead[s, -16:] if start else zero, left], axis=0),
            far_left,
            far_right,
        )
        for b in range(blocks):
            rows = slice(b * half, (b + 1) * half)
            far_rows = slice(b * half + 16, (b + 1) * half + 16)
            lead = x_far[b * half + 8 : b * half + 16]
            x = jnp.concatenate([lead, x_near[rows], x_far[far_rows]], axis=0)
            shade(s, x, b * BLK, state, refs)
        return 0

    over_slices(count, one)

    @pl.when(step == pl.num_programs(0) - 1)
    def _():
        swap = lax.axis_index("depth") % 2 == 1
        finish(state, gain[0], swap, out_keep, out_send, 0)


def full_border(density, small, weights, halos, above, start, blocks, slice_total):
    _, slices, _, cols = density.shape
    step = blocks * BLK
    last = cols // LANES - 1
    lead_rows = max(start * BLK // 16 - 1, 0)

    def lead(column):
        return pl.BlockSpec((1, slices, 16, LANES), lambda i: (0, i, lead_rows, column))

    image = jax.ShapeDtypeStruct((step // (2 * PIECE), 2, PIECE, LANES), F32)
    return pl.pallas_call(
        functools.partial(full_border_kernel, start, slice_total),
        grid=(1,),
        in_specs=small_specs()
        + [whole()]
        + [column_tile(slices, start, blocks, column) for column in (0, last)]
        + [lead(0), lead(last)]
        + [whole()] * 4,
        out_specs=[whole()] * 2,
        out_shape=[image, image],
        scratch_shapes=[pltpu.VMEM((step, LANES), F32)] * 2,
        compiler_params=pltpu.CompilerParams(vmem_limit_bytes=32 * 2**20),
        name=f"full_border{start}",
    )(*small, weights, density, density, density, density, *halos, *above)


def over(mine, other, in_front):
    color = mine[0] * (1.0 - (1.0 - in_front) * other[1]) + other[0] * (1.0 - in_front * mine[1])
    return color, mine[1] + (1.0 - mine[1]) * other[1]


def over_cores(keep, send, flags):
    count = lax.axis_size("depth")
    other = lax.ppermute(send, "depth", [(i, i ^ 1) for i in range(count)])
    front = flags[0, : keep.shape[3]]
    return jnp.stack(over((keep[:, 0], keep[:, 1]), (other[:, 0], other[:, 1]), front), axis=1)


def over_chips(pieces, flags):
    count = lax.axis_size("depth")
    chips = count // 2
    pieces = (pieces * WIRE_SCALE).astype(WIRE)
    groups = [[2 * i + core for i in range(chips)] for core in range(2)]
    pieces = lax.all_to_all(
        pieces, "depth", 0, 0, axis_index_groups=groups, tiled=True
    )
    pieces = pieces.astype(F32) * (1.0 / WIRE_SCALE)
    level = [(pieces[i, 0], pieces[i, 1]) for i in range(chips)]
    row = 1
    while len(level) > 1:
        half = len(level) // 2
        level = [over(level[2 * i], level[2 * i + 1], flags[row + i]) for i in range(half)]
        row += half
    return level[0]


def shards(
    density, occupancy, shear_offsets, frac_lateral, frac_vertical, extinction, slab_gain, view_rank
):
    _, slices, rows, cols = density.shape
    slice_total = lax.axis_size("depth") * slices
    lat = lax.axis_size("lat")
    density = pltpu.with_memory_space_constraint(density, pltpu.HBM)
    small = (occupancy, shear_offsets, frac_lateral, frac_vertical, extinction, slab_gain)
    blocks = rows // BLK
    rightwards = [(x, x + 1) for x in range(lat - 1)]
    leftwards = [(x, (x - 1) % lat) for x in range(lat)]

    def travel(to_left, to_right):
        return lax.ppermute(to_left, "lat", leftwards), lax.ppermute(to_right, "lat", rightwards)

    halos = travel(*pack_halo(density, occupancy, shear_offsets))
    images = interior(density, small, view_rank, slice_total)
    images, halos = lax.optimization_barrier((images, halos))
    keep, send, packed_weights, weights, flags, overflow = images
    half = blocks // 2
    cuts = ((0, half), (half, blocks - half))

    def packed_border():
        parts = [
            border(density, small, packed_weights, halos, *cut, slice_total) for cut in cuts
        ]
        return tuple(jnp.concatenate(p, axis=0) for p in zip(*parts))

    def full_exchange():
        parts, above = [], None
        for cut in cuts:
            strips = travel(*edge_strips(density, occupancy, *cut))
            above = strips if above is None else above
            parts.append(
                full_border(density, small, weights, strips, above, *cut, slice_total)
            )
        return tuple(jnp.concatenate(p, axis=0) for p in zip(*parts))

    inner = over_cores(keep, send, flags)
    keep, send = lax.cond(overflow[0] > 0, full_exchange, packed_border)
    edge = over_cores(keep, send, flags)
    color, alpha = over_chips(jnp.concatenate([edge, inner], axis=3), flags)
    image = jnp.stack([color, alpha])
    moved = lax.ppermute(image[:, :, :LANES], "lat", [(x, (x + 1) % lat) for x in range(lat)])
    lane = jnp.arange(LANES, dtype=jnp.int32)
    first = jnp.where(lane < HALF, moved, image[:, :, :LANES])
    return tuple(jnp.concatenate([first[i], image[i, :, LANES:]], axis=1) for i in range(2))


def solution(mesh):
    placed = (
        P("depth", None, None, "lat"),
        P("depth", None, "lat"),
        P("depth", None),
        P("depth", None),
        P("depth", None),
        P("depth", None),
        P("depth"),
        P(),
    )
    return jax.shard_map(
        shards,
        mesh=mesh,
        in_specs=placed,
        out_specs=(P("depth", "lat"), P("depth", "lat")),
        check_vma=False,
    )
```

```python
import functools
import math

import jax
import jax.numpy as jnp
from jax import lax
from jax.experimental import pallas as pl
from jax.experimental.pallas import tpu as pltpu
from jax.sharding import PartitionSpec as P

SHIFT = 128
BLK = 128
HALF = SHIFT // 2
LANES = 128
PIECE = 16
WIRE = jnp.float16
WIRE_SCALE = 4096.0
TAIL = 2
LOG2E = math.log2(math.e)
SMEM = pltpu.SMEM
F32 = jnp.float32
BF16 = jnp.bfloat16


def rounded(scalar, shape):
    return jnp.full(shape, scalar, F32).astype(BF16).astype(F32)


def tap(distance, offset, fraction):
    second = jnp.where(distance == offset + 1, fraction, 0.0)
    return jnp.where(distance == offset, 1.0 - fraction, second)


def whole():
    return pl.BlockSpec(memory_space=pltpu.VMEM)


def strips_kernel(
    first_block, occ, density, to_left, to_right, first_tile, last_tile, first_here, last_here
):
    slices, cols = density.shape[1], density.shape[3]
    rows, half = first_tile.shape[1], BLK // 2
    copies = []
    for s in range(slices):
        pair = []
        for buffer, arrived, column in (
            (first_tile, first_here, 0),
            (last_tile, last_here, cols - LANES),
        ):
            copy = pltpu.make_async_copy(
                density.at[0, s, pl.ds(first_block * BLK, rows), pl.ds(column, LANES)],
                buffer.at[s],
                arrived.at[s],
            )
            copy.start()
            pair.append(copy)
        copies.append(pair)
    k = lax.broadcasted_iota(jnp.int32, (2 * LANES, LANES), 0)
    n = lax.broadcasted_iota(jnp.int32, (2 * LANES, LANES), 1)
    left = jnp.where(k == jnp.where(n < HALF, n, n + HALF), 1.0, 0.0).astype(BF16)
    right = jnp.where(k == jnp.where(n < HALF, n + LANES + HALF, n), 1.0, 0.0).astype(BF16)
    for s in range(slices):
        for copy in copies[s]:
            copy.wait()
        for buffer, out, pick, column in (
            (first_tile, to_left, left, 0),
            (last_tile, to_right, right, occ.shape[2] - 1),
        ):
            parts = []
            for b in range(rows // BLK):
                top, middle, end = b * BLK, b * BLK + half, (b + 1) * BLK
                pair = jnp.concatenate([buffer[s, top:middle], buffer[s, middle:end]], axis=1)
                parts.append(pair * jnp.full((1, 2 * LANES), occ[0, first_block + b, column], F32).astype(BF16))
            moved = jnp.dot(jnp.concatenate(parts, axis=0), pick, preferred_element_type=F32)
            out[s] = moved.astype(BF16)


def edge_strips(density, occupancy, first, blocks):
    slices = density.shape[1]
    rows = blocks * BLK
    shape = jax.ShapeDtypeStruct((slices, rows // 2, LANES), BF16)
    return pl.pallas_call(
        functools.partial(strips_kernel, first),
        in_specs=[pl.BlockSpec(memory_space=SMEM), pl.BlockSpec(memory_space=pl.ANY)],
        out_specs=[whole()] * 2,
        out_shape=[shape, shape],
        scratch_shapes=[pltpu.VMEM((slices, rows, LANES), BF16)] * 2
        + [pltpu.SemaphoreType.DMA((slices,))] * 2,
        compiler_params=pltpu.CompilerParams(vmem_limit_bytes=32 * 2**20),
        name=f"edge_strips{first}",
    )(occupancy, density)


def shade(s, x, base, state, refs):
    frac_vertical, extinction, slice_total = refs
    through_ref, sum_ref = state
    rows = x.shape[0] - 8
    v0 = 2.0 * rounded(1.0 - frac_vertical[0, s], (1, LANES))
    v1 = 2.0 * rounded(frac_vertical[0, s], (1, LANES))
    density = v0 * x + v1 * pltpu.roll(x, 1, 0)
    above = pltpu.roll(density, 1, 0)
    density, above = density[8:], above[8:]
    rate = extinction[0, s] * (-LOG2E / (2.0 * slice_total))
    kept = jnp.exp2(rate * density)
    slope = jnp.tanh(density - above)
    at = slice(base, base + rows)
    through = through_ref[at]
    after = through * kept
    through_ref[at] = after
    sum_ref[at] += (through - after) * slope


def finish(state, gain, swap, out_keep, out_send, tile):
    through_ref, sum_ref = state
    rows = out_keep.shape[0] * 2 * PIECE
    base = tile * rows
    alphas, colors = [], []
    for p in range(rows // PIECE):
        at = slice(base + p * PIECE, base + (p + 1) * PIECE)
        alpha = 1.0 - through_ref[at]
        alphas.append(alpha)
        colors.append(gain * (0.65 * alpha + 0.35 * sum_ref[at]))
    lanes = slice(tile * LANES, (tile + 1) * LANES)
    for q in range(rows // PIECE // 2):
        for i, values in enumerate((colors, alphas)):
            even, odd = values[2 * q], values[2 * q + 1]
            out_keep[q, i, :, lanes] = jnp.where(swap, odd, even)
            out_send[q, i, :, lanes] = jnp.where(swap, even, odd)


def splat(value):
    return jnp.full((1, LANES), value, F32).astype(BF16)


def over_slices(slices, one):
    for s in range(slices):
        one(s, 0)


def interior_kernel(
    slice_total, occ, offset, frac_lateral, frac_vertical, extinction, gain, rank,
    x_ref, lead_ref, out_keep, out_send, weights, flags, through_ref, sum_ref,
):
    block = pl.program_id(0)
    slices, rows = x_ref.shape[1], x_ref.shape[2]
    tiles = x_ref.shape[3] // LANES

    @pl.when(block == 0)
    def _():
        k = lax.broadcasted_iota(jnp.int32, (2 * LANES, LANES), 0)
        n = lax.broadcasted_iota(jnp.int32, (2 * LANES, LANES), 1)

        def build(s, _):
            weights[s] = tap(LANES + n - k, offset[0, s], frac_lateral[0, s]).astype(BF16)
            return 0

        lax.fori_loop(0, slices, build, 0)
        me = lax.axis_index("depth")
        in_front = [rank[me] < rank[jnp.bitwise_xor(me, 1)]]
        for span in (2, 4, 8, 16):
            in_front += [rank[a] < rank[a + span] for a in range(0, rank.shape[0], 2 * span)]
        for i, flag in enumerate(in_front):
            flags[i : i + 1] = jnp.full((1, flags.shape[1]), jnp.where(flag, 1.0, 0.0), F32)

    through_ref[...] = jnp.ones_like(through_ref)
    sum_ref[...] = jnp.zeros_like(sum_ref)
    inside = jnp.where(block > 0, 1, 0)
    above = jnp.maximum(block - 1, 0)
    mask = [splat(occ[0, block, t]) for t in range(tiles)]
    lead_mask = [splat(occ[0, above, t] * inside) for t in range(tiles)]
    state = (through_ref, sum_ref)
    refs = (frac_vertical, extinction, slice_total)

    def one(s, _):
        parts = []
        for t in range(tiles):
            lanes = slice(t * LANES, (t + 1) * LANES)
            lead = lead_ref[0, s, :, lanes] * lead_mask[t]
            parts.append(jnp.concatenate([lead, x_ref[0, s, :, lanes] * mask[t]], axis=0))
        for t in range(1, tiles):
            pair = jnp.concatenate([parts[t - 1], parts[t]], axis=1)
            x = jnp.dot(pair, weights[s], preferred_element_type=F32)
            shade(s, x[8:], (t - 1) * rows, state, refs)
        return 0

    over_slices(slices, one)
    swap = lax.axis_index("depth") % 2 == 1
    for t in range(tiles - 1):
        finish(state, gain[0, 0], swap, out_keep, out_send, t)


def small_specs():
    return [pl.BlockSpec(memory_space=SMEM)] * 6


def interior(density, small, rank, slice_total):
    _, slices, rows, cols = density.shape
    step = BLK
    width = cols - LANES
    pieces = step // (2 * PIECE)
    image = jax.ShapeDtypeStruct((rows // (2 * PIECE), 2, PIECE, width), F32)
    return pl.pallas_call(
        functools.partial(interior_kernel, slice_total),
        grid=(rows // step,),
        in_specs=small_specs()
        + [pl.BlockSpec(memory_space=SMEM)]
        + [
            pl.BlockSpec((1, slices, step, cols), lambda b: (0, 0, b, 0)),
            pl.BlockSpec(
                (1, slices, 16, cols), lambda b: (0, 0, jnp.maximum(b * (step // 16) - 1, 0), 0)
            ),
        ],
        out_specs=[
            pl.BlockSpec((pieces, 2, PIECE, width), lambda b: (b, 0, 0, 0))
        ]
        * 2
        + [
            pl.BlockSpec((slices, 2 * LANES, LANES), lambda b: (0, 0, 0)),
            pl.BlockSpec((16, cols), lambda b: (0, 0)),
        ],
        out_shape=[
            image,
            image,
            jax.ShapeDtypeStruct((slices, 2 * LANES, LANES), BF16),
            jax.ShapeDtypeStruct((16, cols), F32),
        ],
        scratch_shapes=[pltpu.VMEM((step * (width // LANES), LANES), F32)] * 2,
        compiler_params=pltpu.CompilerParams(vmem_limit_bytes=32 * 2**20),
        name="interior",
    )(*small, rank, density, density)


def border_kernel(
    start, slice_total, occ, offset, frac_lateral, frac_vertical, extinction, gain, weights,
    first_ref, last_ref, first_lead, last_lead, right_ref, left_ref, right_lead, left_lead,
    out_keep, out_send, through_ref, sum_ref,
):
    slices, half = first_ref.shape[1], BLK // 2
    last_tile = occ.shape[2] - 1
    follows = jnp.where(lax.axis_index("lat") < lax.axis_size("lat") - 1, 1, 0)
    own_lanes = lax.broadcasted_iota(jnp.int32, (1, LANES), 1) >= HALF
    refs = (frac_vertical, extinction, slice_total)
    state = (through_ref, sum_ref)
    through_ref[...] = jnp.ones_like(through_ref)
    sum_ref[...] = jnp.zeros_like(sum_ref)
    blocks = first_ref.shape[2] // BLK
    masks = []
    for b in range(start - 1, start + blocks):
        inside = b >= 0
        masks.append(
            (
                splat(occ[0, b, 0] if inside else 0.0),
                splat(occ[0, b, last_tile] * follows if inside else 0.0),
            )
        )
    zero = jnp.zeros((16, LANES), BF16)

    def one(s, _):
        before, own = weights[s, :LANES], weights[s, LANES:]
        turn = lambda w: jnp.concatenate([w[HALF:], w[:HALF]], axis=0)
        near = jnp.concatenate([before, own], axis=0)
        far_left = jnp.concatenate([turn(before), own], axis=0)
        far_right = jnp.concatenate([before, turn(own)], axis=0)

        def halves(ref, side, top, above):
            parts = [above] if above is not None else []
            for b in range(blocks):
                at = slice(b * BLK + top, b * BLK + top + half)
                parts.append(ref[0, s, at] * masks[b + 1][side])
            return jnp.concatenate(parts, axis=0) if len(parts) > 1 else parts[0]

        def lateral(first, last, right, left, w_left, w_right):
            here = jnp.dot(
                jnp.concatenate([left, first], axis=1), w_left, preferred_element_type=F32
            )
            there = jnp.dot(
                jnp.concatenate([last, right], axis=1), w_right, preferred_element_type=F32
            )
            return jnp.where(own_lanes, here, there)

        right, left = right_ref[s], left_ref[s]
        x_near = lateral(
            halves(first_ref, 0, 0, None), halves(last_ref, 1, 0, None), right, left, near, near
        )
        x_far = lateral(
            halves(first_ref, 0, half, first_lead[0, s] * masks[0][0]),
            halves(last_ref, 1, half, last_lead[0, s] * masks[0][1]),
            jnp.concatenate([right_lead[s] if start else zero, right], axis=0),
            jnp.concatenate([left_lead[s] if start else zero, left], axis=0),
            far_left,
            far_right,
        )
        for b in range(blocks):
            rows = slice(b * half, (b + 1) * half)
            far_rows = slice(b * half + 16, (b + 1) * half + 16)
            lead = x_far[b * half + 8 : b * half + 16]
            x = jnp.concatenate([lead, x_near[rows], x_far[far_rows]], axis=0)
            shade(s, x, b * BLK, state, refs)
        return 0

    over_slices(slices, one)
    swap = lax.axis_index("depth") % 2 == 1
    finish(state, gain[0, 0], swap, out_keep, out_send, 0)


def border(density, small, weights, halos, above, start, blocks, slice_total):
    _, slices, _, cols = density.shape
    step = blocks * BLK
    last = cols // LANES - 1
    per = BLK // 16

    def body(column):
        shape = tuple(pl.Element(n) for n in (1, slices, step, LANES))
        return pl.BlockSpec(shape, lambda i: (0, 0, start * BLK, column * LANES))

    def lead(column):
        return pl.BlockSpec(
            (1, slices, 16, LANES), lambda i: (0, 0, max(start * per - 1, 0), column)
        )

    halo = pl.BlockSpec((slices, step // 2, LANES), lambda i: (0, 0, 0))
    last_rows = above[0].shape[1] // 16 - 1
    halo_lead = pl.BlockSpec((slices, 16, LANES), lambda i: (0, last_rows, 0))
    shape = (step // (2 * PIECE), 2, PIECE, LANES)
    image = jax.ShapeDtypeStruct(shape, F32)
    return pl.pallas_call(
        functools.partial(border_kernel, start, slice_total),
        grid=(1,),
        in_specs=small_specs()
        + [pl.BlockSpec((slices, 2 * LANES, LANES), lambda i: (0, 0, 0))]
        + [body(0), body(last), lead(0), lead(last), halo, halo, halo_lead, halo_lead],
        out_specs=[pl.BlockSpec(shape, lambda i: (0, 0, 0, 0))] * 2,
        out_shape=[image, image],
        scratch_shapes=[pltpu.VMEM((step, LANES), F32)] * 2,
        compiler_params=pltpu.CompilerParams(vmem_limit_bytes=32 * 2**20),
        name=f"border{start}",
    )(*small, weights, density, density, density, density, *halos, *above)


def over(mine, other, in_front):
    color = mine[0] * (1.0 - (1.0 - in_front) * other[1]) + other[0] * (1.0 - in_front * mine[1])
    return color, mine[1] + (1.0 - mine[1]) * other[1]


def over_cores(keep, send, flags):
    count = lax.axis_size("depth")
    other = lax.ppermute(send, "depth", [(i, i ^ 1) for i in range(count)])
    front = flags[0, : keep.shape[3]]
    return jnp.stack(over((keep[:, 0], keep[:, 1]), (other[:, 0], other[:, 1]), front), axis=1)


def over_chips(pieces, flags):
    count = lax.axis_size("depth")
    chips = count // 2
    pieces = (pieces * WIRE_SCALE).astype(WIRE)
    groups = [[2 * i + core for i in range(chips)] for core in range(2)]
    pieces = lax.all_to_all(
        pieces, "depth", 0, 0, axis_index_groups=groups, tiled=True
    )
    pieces = pieces.astype(F32) * (1.0 / WIRE_SCALE)
    level = [(pieces[i, 0], pieces[i, 1]) for i in range(chips)]
    row = 1
    while len(level) > 1:
        half = len(level) // 2
        level = [over(level[2 * i], level[2 * i + 1], flags[row + i]) for i in range(half)]
        row += half
    return level[0]


def shards(
    density, occupancy, shear_offsets, frac_lateral, frac_vertical, extinction, slab_gain, view_rank
):
    _, slices, rows, cols = density.shape
    slice_total = lax.axis_size("depth") * slices
    lat = lax.axis_size("lat")
    density = pltpu.with_memory_space_constraint(density, pltpu.HBM)
    small = (occupancy, shear_offsets, frac_lateral, frac_vertical, extinction, slab_gain[None])
    blocks = rows // BLK
    half = blocks - TAIL
    rightwards = [(x, x + 1) for x in range(lat - 1)]
    leftwards = [(x, (x - 1) % lat) for x in range(lat)]
    halos = []
    for first, count in ((0, half), (half, blocks - half)):
        to_left, to_right = edge_strips(density, occupancy, first, count)
        halos.append(
            (lax.ppermute(to_left, "lat", leftwards), lax.ppermute(to_right, "lat", rightwards))
        )
    keep, send, weights, flags = interior(density, small, view_rank, slice_total)
    top = border(density, small, weights, halos[0], halos[0], 0, half, slice_total)
    send, top = lax.optimization_barrier((send, top))
    inner = over_cores(keep, send, flags)
    bottom = border(density, small, weights, halos[1], halos[0], half, blocks - half, slice_total)
    keep, send = (jnp.concatenate(p, axis=0) for p in zip(top, bottom))
    edge = over_cores(keep, send, flags)
    color, alpha = over_chips(jnp.concatenate([edge, inner], axis=3), flags)
    image = jnp.stack([color, alpha])
    moved = lax.ppermute(image[:, :, :LANES], "lat", [(x, (x + 1) % lat) for x in range(lat)])
    lane = jnp.arange(LANES, dtype=jnp.int32)
    first = jnp.where(lane < HALF, moved, image[:, :, :LANES])
    return tuple(jnp.concatenate([first[i], image[i, :, LANES:]], axis=1) for i in range(2))


def solution(mesh):
    placed = (
        P("depth", None, None, "lat"),
        P("depth", None, "lat"),
        P("depth", None),
        P("depth", None),
        P("depth", None),
        P("depth", None),
        P("depth"),
        P(),
    )
    return jax.shard_map(
        shards,
        mesh=mesh,
        in_specs=placed,
        out_specs=(P("depth", "lat"), P("depth", "lat")),
        check_vma=False,
    )
```

```python
import functools
import math

import jax
import jax.numpy as jnp
from jax import lax
from jax.experimental import pallas as pl
from jax.experimental.pallas import tpu as pltpu
from jax.sharding import PartitionSpec as P

SHIFT = 128
BLK = 128
HALF = SHIFT // 2
LANES = 128
PIECE = 16
WIRE = jnp.float16
WIRE_SCALE = 4096.0
TAIL = 2
LOG2E = math.log2(math.e)
SMEM = pltpu.SMEM
F32 = jnp.float32
BF16 = jnp.bfloat16


def rounded(scalar, shape):
    return jnp.full(shape, scalar, F32).astype(BF16).astype(F32)


def tap(distance, offset, fraction):
    second = jnp.where(distance == offset + 1, fraction, 0.0)
    return jnp.where(distance == offset, 1.0 - fraction, second)


def whole():
    return pl.BlockSpec(memory_space=pltpu.VMEM)


def strips_kernel(first_block, occ, x_first, x_last, to_left, to_right):
    half = x_first.shape[2] // 2
    block = first_block + pl.program_id(0)
    k = lax.broadcasted_iota(jnp.int32, (2 * LANES, LANES), 0)
    n = lax.broadcasted_iota(jnp.int32, (2 * LANES, LANES), 1)
    for ref, out, column, source in (
        (x_first, to_left, 0, jnp.where(n < HALF, n, n + HALF)),
        (x_last, to_right, occ.shape[2] - 1, jnp.where(n < HALF, n + LANES + HALF, n)),
    ):
        occupied = occ[0, block, column].astype(F32)
        pick = jnp.where(k == source, occupied, 0.0).astype(BF16)
        for s in range(ref.shape[1]):
            rows = jnp.concatenate([ref[0, s, :half], ref[0, s, half:]], axis=1)
            out[s] = jnp.dot(rows, pick, preferred_element_type=F32).astype(BF16)


def edge_strips(density, occupancy, first, blocks):
    _, slices, _, cols = density.shape
    shape = jax.ShapeDtypeStruct((slices, blocks * BLK // 2, LANES), BF16)
    last = cols // LANES - 1
    return pl.pallas_call(
        functools.partial(strips_kernel, first),
        grid=(blocks,),
        in_specs=[
            pl.BlockSpec(memory_space=SMEM),
            pl.BlockSpec((1, slices, BLK, LANES), lambda i: (0, 0, first + i, 0)),
            pl.BlockSpec((1, slices, BLK, LANES), lambda i: (0, 0, first + i, last)),
        ],
        out_specs=[pl.BlockSpec((slices, BLK // 2, LANES), lambda i: (0, i, 0))] * 2,
        out_shape=[shape, shape],
        name=f"edge_strips{first}",
    )(occupancy, density, density)


def shade(s, x, base, state, refs):
    frac_vertical, extinction, slice_total = refs
    through_ref, sum_ref = state
    rows = x.shape[0] - 8
    v0 = 2.0 * rounded(1.0 - frac_vertical[0, s], (1, LANES))
    v1 = 2.0 * rounded(frac_vertical[0, s], (1, LANES))
    density = v0 * x + v1 * pltpu.roll(x, 1, 0)
    above = pltpu.roll(density, 1, 0)
    density, above = density[8:], above[8:]
    rate = extinction[0, s] * (-LOG2E / (2.0 * slice_total))
    kept = jnp.exp2(rate * density)
    slope = jnp.tanh(density - above)
    at = slice(base, base + rows)
    through = through_ref[at]
    after = through * kept
    through_ref[at] = after
    sum_ref[at] += (through - after) * slope


def finish(state, gain, swap, out_keep, out_send, tile):
    through_ref, sum_ref = state
    rows = out_keep.shape[0] * 2 * PIECE
    base = tile * rows
    alphas, colors = [], []
    for p in range(rows // PIECE):
        at = slice(base + p * PIECE, base + (p + 1) * PIECE)
        alpha = 1.0 - through_ref[at]
        alphas.append(alpha)
        colors.append(gain * (0.65 * alpha + 0.35 * sum_ref[at]))
    lanes = slice(tile * LANES, (tile + 1) * LANES)
    for q in range(rows // PIECE // 2):
        for i, values in enumerate((colors, alphas)):
            even, odd = values[2 * q], values[2 * q + 1]
            out_keep[q, i, :, lanes] = jnp.where(swap, odd, even)
            out_send[q, i, :, lanes] = jnp.where(swap, even, odd)


def splat(value):
    return jnp.full((1, LANES), value, F32).astype(BF16)


def over_slices(slices, one):
    for s in range(slices):
        one(s, 0)


def interior_kernel(
    slice_total, occ, offset, frac_lateral, frac_vertical, extinction, gain, rank,
    x_ref, lead_ref, out_keep, out_send, weights, flags, through_ref, sum_ref,
):
    block = pl.program_id(0)
    slices, rows = x_ref.shape[1], x_ref.shape[2]
    tiles = x_ref.shape[3] // LANES

    @pl.when(block == 0)
    def _():
        k = lax.broadcasted_iota(jnp.int32, (2 * LANES, LANES), 0)
        n = lax.broadcasted_iota(jnp.int32, (2 * LANES, LANES), 1)

        def build(s, _):
            weights[s] = tap(LANES + n - k, offset[0, s], frac_lateral[0, s]).astype(BF16)
            return 0

        lax.fori_loop(0, slices, build, 0)
        me = lax.axis_index("depth")
        in_front = [rank[me] < rank[jnp.bitwise_xor(me, 1)]]
        for span in (2, 4, 8, 16):
            in_front += [rank[a] < rank[a + span] for a in range(0, rank.shape[0], 2 * span)]
        for i, flag in enumerate(in_front):
            flags[i : i + 1] = jnp.full((1, flags.shape[1]), jnp.where(flag, 1.0, 0.0), F32)

    through_ref[...] = jnp.ones_like(through_ref)
    sum_ref[...] = jnp.zeros_like(sum_ref)
    inside = jnp.where(block > 0, 1, 0)
    per = rows // BLK
    above = jnp.maximum(per * block - 1, 0)

    def mask_of(t):
        parts = [
            jnp.broadcast_to(splat(occ[0, per * block + b, t]), (BLK, LANES)) for b in range(per)
        ]
        return jnp.concatenate(parts, axis=0)

    mask = [mask_of(t) for t in range(tiles)]
    lead_mask = [splat(occ[0, above, t] * inside) for t in range(tiles)]
    state = (through_ref, sum_ref)
    refs = (frac_vertical, extinction, slice_total)

    def one(s, _):
        parts = []
        for t in range(tiles):
            lanes = slice(t * LANES, (t + 1) * LANES)
            lead = lead_ref[0, s, :, lanes] * lead_mask[t]
            parts.append(jnp.concatenate([lead, x_ref[0, s, :, lanes] * mask[t]], axis=0))
        for t in range(1, tiles):
            pair = jnp.concatenate([parts[t - 1], parts[t]], axis=1)
            x = jnp.dot(pair, weights[s], preferred_element_type=F32)
            shade(s, x[8:], (t - 1) * rows, state, refs)
        return 0

    over_slices(slices, one)
    swap = lax.axis_index("depth") % 2 == 1
    for t in range(tiles - 1):
        finish(state, gain[...], swap, out_keep, out_send, t)


def small_specs():
    return [pl.BlockSpec(memory_space=SMEM)] * 5 + [whole()]


def interior(density, small, rank, slice_total):
    _, slices, rows, cols = density.shape
    step = 2 * BLK
    width = cols - LANES
    pieces = step // (2 * PIECE)
    image = jax.ShapeDtypeStruct((rows // (2 * PIECE), 2, PIECE, width), F32)
    return pl.pallas_call(
        functools.partial(interior_kernel, slice_total),
        grid=(rows // step,),
        in_specs=small_specs()
        + [pl.BlockSpec(memory_space=SMEM)]
        + [
            pl.BlockSpec((1, slices, step, cols), lambda b: (0, 0, b, 0)),
            pl.BlockSpec(
                (1, slices, 16, cols), lambda b: (0, 0, jnp.maximum(b * (step // 16) - 1, 0), 0)
            ),
        ],
        out_specs=[
            pl.BlockSpec((pieces, 2, PIECE, width), lambda b: (b, 0, 0, 0))
        ]
        * 2
        + [
            pl.BlockSpec((slices, 2 * LANES, LANES), lambda b: (0, 0, 0)),
            pl.BlockSpec((16, cols), lambda b: (0, 0)),
        ],
        out_shape=[
            image,
            image,
            jax.ShapeDtypeStruct((slices, 2 * LANES, LANES), BF16),
            jax.ShapeDtypeStruct((16, cols), F32),
        ],
        scratch_shapes=[pltpu.VMEM((step * (width // LANES), LANES), F32)] * 2,
        compiler_params=pltpu.CompilerParams(vmem_limit_bytes=32 * 2**20),
        name="interior",
    )(*small, rank, density, density)


def border_kernel(
    start, slice_total, occ, offset, frac_lateral, frac_vertical, extinction, gain, weights,
    first_ref, last_ref, first_lead, last_lead, right_ref, left_ref, right_lead, left_lead,
    out_keep, out_send, through_ref, sum_ref,
):
    slices, half = first_ref.shape[1], BLK // 2
    last_tile = occ.shape[2] - 1
    follows = jnp.where(lax.axis_index("lat") < lax.axis_size("lat") - 1, 1, 0)
    own_lanes = lax.broadcasted_iota(jnp.int32, (1, LANES), 1) >= HALF
    refs = (frac_vertical, extinction, slice_total)
    state = (through_ref, sum_ref)
    through_ref[...] = jnp.ones_like(through_ref)
    sum_ref[...] = jnp.zeros_like(sum_ref)
    blocks = first_ref.shape[2] // BLK
    masks = []
    for b in range(start - 1, start + blocks):
        inside = b >= 0
        masks.append(
            (
                splat(occ[0, b, 0] if inside else 0.0),
                splat(occ[0, b, last_tile] * follows if inside else 0.0),
            )
        )
    zero = jnp.zeros((16, LANES), BF16)

    def one(s, _):
        before, own = weights[s, :LANES], weights[s, LANES:]
        turn = lambda w: jnp.concatenate([w[HALF:], w[:HALF]], axis=0)
        near = jnp.concatenate([before, own], axis=0)
        far_left = jnp.concatenate([turn(before), own], axis=0)
        far_right = jnp.concatenate([before, turn(own)], axis=0)

        def halves(ref, side, top, above):
            parts = [above] if above is not None else []
            for b in range(blocks):
                at = slice(b * BLK + top, b * BLK + top + half)
                parts.append(ref[0, s, at] * masks[b + 1][side])
            return jnp.concatenate(parts, axis=0) if len(parts) > 1 else parts[0]

        def lateral(first, last, right, left, w_left, w_right):
            here = jnp.dot(
                jnp.concatenate([left, first], axis=1), w_left, preferred_element_type=F32
            )
            there = jnp.dot(
                jnp.concatenate([last, right], axis=1), w_right, preferred_element_type=F32
            )
            return jnp.where(own_lanes, here, there)

        right, left = right_ref[s], left_ref[s]
        x_near = lateral(
            halves(first_ref, 0, 0, None), halves(last_ref, 1, 0, None), right, left, near, near
        )
        x_far = lateral(
            halves(first_ref, 0, half, first_lead[0, s] * masks[0][0]),
            halves(last_ref, 1, half, last_lead[0, s] * masks[0][1]),
            jnp.concatenate([right_lead[s] if start else zero, right], axis=0),
            jnp.concatenate([left_lead[s] if start else zero, left], axis=0),
            far_left,
            far_right,
        )
        for b in range(blocks):
            rows = slice(b * half, (b + 1) * half)
            far_rows = slice(b * half + 16, (b + 1) * half + 16)
            lead = x_far[b * half + 8 : b * half + 16]
            x = jnp.concatenate([lead, x_near[rows], x_far[far_rows]], axis=0)
            shade(s, x, b * BLK, state, refs)
        return 0

    over_slices(slices, one)
    swap = lax.axis_index("depth") % 2 == 1
    finish(state, gain[...], swap, out_keep, out_send, 0)


def border(density, small, weights, halos, above, start, blocks, slice_total):
    _, slices, _, cols = density.shape
    step = blocks * BLK
    last = cols // LANES - 1
    per = BLK // 16

    def body(column):
        shape = tuple(pl.Element(n) for n in (1, slices, step, LANES))
        return pl.BlockSpec(shape, lambda i: (0, 0, start * BLK, column * LANES))

    def lead(column):
        return pl.BlockSpec(
            (1, slices, 16, LANES), lambda i: (0, 0, max(start * per - 1, 0), column)
        )

    halo = pl.BlockSpec((slices, step // 2, LANES), lambda i: (0, 0, 0))
    last_rows = above[0].shape[1] // 16 - 1
    halo_lead = pl.BlockSpec((slices, 16, LANES), lambda i: (0, last_rows, 0))
    shape = (step // (2 * PIECE), 2, PIECE, LANES)
    image = jax.ShapeDtypeStruct(shape, F32)
    return pl.pallas_call(
        functools.partial(border_kernel, start, slice_total),
        grid=(1,),
        in_specs=small_specs()
        + [pl.BlockSpec((slices, 2 * LANES, LANES), lambda i: (0, 0, 0))]
        + [body(0), body(last), lead(0), lead(last), halo, halo, halo_lead, halo_lead],
        out_specs=[pl.BlockSpec(shape, lambda i: (0, 0, 0, 0))] * 2,
        out_shape=[image, image],
        scratch_shapes=[pltpu.VMEM((step, LANES), F32)] * 2,
        compiler_params=pltpu.CompilerParams(vmem_limit_bytes=32 * 2**20),
        name=f"border{start}",
    )(*small, weights, density, density, density, density, *halos, *above)


def over(mine, other, in_front):
    color = mine[0] * (1.0 - (1.0 - in_front) * other[1]) + other[0] * (1.0 - in_front * mine[1])
    return color, mine[1] + (1.0 - mine[1]) * other[1]


def over_cores(keep, send, flags):
    count = lax.axis_size("depth")
    other = lax.ppermute(send, "depth", [(i, i ^ 1) for i in range(count)])
    front = flags[0, : keep.shape[3]]
    return jnp.stack(over((keep[:, 0], keep[:, 1]), (other[:, 0], other[:, 1]), front), axis=1)


def over_chips(pieces, flags):
    count = lax.axis_size("depth")
    chips = count // 2
    pieces = (pieces * WIRE_SCALE).astype(WIRE)
    groups = [[2 * i + core for i in range(chips)] for core in range(2)]
    pieces = lax.all_to_all(
        pieces, "depth", 0, 0, axis_index_groups=groups, tiled=True
    )
    pieces = pieces.astype(F32) * (1.0 / WIRE_SCALE)
    level = [(pieces[i, 0], pieces[i, 1]) for i in range(chips)]
    row = 1
    while len(level) > 1:
        half = len(level) // 2
        level = [over(level[2 * i], level[2 * i + 1], flags[row + i]) for i in range(half)]
        row += half
    return level[0]


def shards(
    density, occupancy, shear_offsets, frac_lateral, frac_vertical, extinction, slab_gain, view_rank
):
    _, slices, rows, cols = density.shape
    slice_total = lax.axis_size("depth") * slices
    lat = lax.axis_size("lat")
    density = pltpu.with_memory_space_constraint(density, pltpu.HBM)
    small = (occupancy, shear_offsets, frac_lateral, frac_vertical, extinction, slab_gain[None])
    blocks = rows // BLK
    half = blocks - TAIL
    rightwards = [(x, x + 1) for x in range(lat - 1)]
    leftwards = [(x, (x - 1) % lat) for x in range(lat)]
    halos = []
    for first, count in ((0, half), (half, blocks - half)):
        to_left, to_right = edge_strips(density, occupancy, first, count)
        halos.append(
            (lax.ppermute(to_left, "lat", leftwards), lax.ppermute(to_right, "lat", rightwards))
        )
    keep, send, weights, flags = interior(density, small, view_rank, slice_total)
    top = border(density, small, weights, halos[0], halos[0], 0, half, slice_total)
    send, top = lax.optimization_barrier((send, top))
    inner = over_cores(keep, send, flags)
    bottom = border(density, small, weights, halos[1], halos[0], half, blocks - half, slice_total)
    keep, send = (jnp.concatenate(p, axis=0) for p in zip(top, bottom))
    edge = over_cores(keep, send, flags)
    color, alpha = over_chips(jnp.concatenate([edge, inner], axis=3), flags)
    image = jnp.stack([color, alpha])
    moved = lax.ppermute(image[:, :, :LANES], "lat", [(x, (x + 1) % lat) for x in range(lat)])
    lane = jnp.arange(LANES, dtype=jnp.int32)
    first = jnp.where(lane < HALF, moved, image[:, :, :LANES])
    return tuple(jnp.concatenate([first[i], image[i, :, LANES:]], axis=1) for i in range(2))


def solution(mesh):
    placed = (
        P("depth", None, None, "lat"),
        P("depth", None, "lat"),
        P("depth", None),
        P("depth", None),
        P("depth", None),
        P("depth", None),
        P("depth"),
        P(),
    )
    return jax.shard_map(
        shards,
        mesh=mesh,
        in_specs=placed,
        out_specs=(P("depth", "lat"), P("depth", "lat")),
        check_vma=False,
    )
```

```python
import functools
import math

import jax
import jax.numpy as jnp
from jax import lax
from jax.experimental import pallas as pl
from jax.experimental.pallas import tpu as pltpu
from jax.sharding import PartitionSpec as P

SHIFT = 128
BLK = 128
HALF = SHIFT // 2
LANES = 128
PIECE = 16
WIRE = jnp.float16
WIRE_SCALE = 4096.0
TAIL = 2
PARTS = 2
LOG2E = math.log2(math.e)
SMEM = pltpu.SMEM
F32 = jnp.float32
BF16 = jnp.bfloat16


def rounded(scalar, shape):
    return jnp.full(shape, scalar, F32).astype(BF16).astype(F32)


def tap(distance, offset, fraction):
    second = jnp.where(distance == offset + 1, fraction, 0.0)
    return jnp.where(distance == offset, 1.0 - fraction, second)


def whole():
    return pl.BlockSpec(memory_space=pltpu.VMEM)


def strips_kernel(first_block, occ, x_first, x_last, to_left, to_right):
    half = x_first.shape[2] // 2
    block = first_block + pl.program_id(0)
    k = lax.broadcasted_iota(jnp.int32, (2 * LANES, LANES), 0)
    n = lax.broadcasted_iota(jnp.int32, (2 * LANES, LANES), 1)
    for ref, out, column, source in (
        (x_first, to_left, 0, jnp.where(n < HALF, n, n + HALF)),
        (x_last, to_right, occ.shape[2] - 1, jnp.where(n < HALF, n + LANES + HALF, n)),
    ):
        occupied = occ[0, block, column].astype(F32)
        pick = jnp.where(k == source, occupied, 0.0).astype(BF16)
        for s in range(ref.shape[1]):
            rows = jnp.concatenate([ref[0, s, :half], ref[0, s, half:]], axis=1)
            out[s] = jnp.dot(rows, pick, preferred_element_type=F32).astype(BF16)


def edge_strips(density, occupancy, first, blocks):
    _, slices, _, cols = density.shape
    shape = jax.ShapeDtypeStruct((slices, blocks * BLK // 2, LANES), BF16)
    last = cols // LANES - 1
    return pl.pallas_call(
        functools.partial(strips_kernel, first),
        grid=(blocks,),
        in_specs=[
            pl.BlockSpec(memory_space=SMEM),
            pl.BlockSpec((1, slices, BLK, LANES), lambda i: (0, 0, first + i, 0)),
            pl.BlockSpec((1, slices, BLK, LANES), lambda i: (0, 0, first + i, last)),
        ],
        out_specs=[pl.BlockSpec((slices, BLK // 2, LANES), lambda i: (0, i, 0))] * 2,
        out_shape=[shape, shape],
        name=f"edge_strips{first}",
    )(occupancy, density, density)


def shade(s, x, base, state, refs):
    frac_vertical, extinction, slice_total = refs
    through_ref, sum_ref = state
    rows = x.shape[0] - 8
    v0 = 2.0 * rounded(1.0 - frac_vertical[0, s], (1, LANES))
    v1 = 2.0 * rounded(frac_vertical[0, s], (1, LANES))
    density = v0 * x + v1 * pltpu.roll(x, 1, 0)
    above = pltpu.roll(density, 1, 0)
    density, above = density[8:], above[8:]
    rate = extinction[0, s] * (-LOG2E / (2.0 * slice_total))
    kept = jnp.exp2(rate * density)
    slope = jnp.tanh(density - above)
    at = slice(base, base + rows)
    through = through_ref[at]
    after = through * kept
    through_ref[at] = after
    sum_ref[at] += (through - after) * slope


def finish(state, gain, swap, out_keep, out_send, tile):
    through_ref, sum_ref = state
    rows = out_keep.shape[0] * 2 * PIECE
    base = tile * rows
    alphas, colors = [], []
    for p in range(rows // PIECE):
        at = slice(base + p * PIECE, base + (p + 1) * PIECE)
        alpha = 1.0 - through_ref[at]
        alphas.append(alpha)
        colors.append(gain * (0.65 * alpha + 0.35 * sum_ref[at]))
    lanes = slice(tile * LANES, (tile + 1) * LANES)
    for q in range(rows // PIECE // 2):
        for i, values in enumerate((colors, alphas)):
            even, odd = values[2 * q], values[2 * q + 1]
            out_keep[q, i, :, lanes] = jnp.where(swap, odd, even)
            out_send[q, i, :, lanes] = jnp.where(swap, even, odd)


def splat(value):
    return jnp.full((1, LANES), value, F32).astype(BF16)


def over_slices(slices, one):
    for s in range(slices):
        one(s, 0)


def interior_kernel(
    slice_total, occ, offset, frac_lateral, frac_vertical, extinction, gain, rank,
    x_ref, lead_ref, out_keep, out_send, weights, flags, through_ref, sum_ref,
):
    block, part = pl.program_id(0), pl.program_id(1)
    slices, rows = weights.shape[0], x_ref.shape[2]
    count = x_ref.shape[1]
    tiles = x_ref.shape[3] // LANES

    @pl.when((block == 0) & (part == 0))
    def _():
        k = lax.broadcasted_iota(jnp.int32, (2 * LANES, LANES), 0)
        n = lax.broadcasted_iota(jnp.int32, (2 * LANES, LANES), 1)

        def build(s, _):
            weights[s] = tap(LANES + n - k, offset[0, s], frac_lateral[0, s]).astype(BF16)
            return 0

        lax.fori_loop(0, slices, build, 0)
        me = lax.axis_index("depth")
        in_front = [rank[me] < rank[jnp.bitwise_xor(me, 1)]]
        for span in (2, 4, 8, 16):
            in_front += [rank[a] < rank[a + span] for a in range(0, rank.shape[0], 2 * span)]
        for i, flag in enumerate(in_front):
            flags[i : i + 1] = jnp.full((1, flags.shape[1]), jnp.where(flag, 1.0, 0.0), F32)

    @pl.when(part == 0)
    def _():
        through_ref[...] = jnp.ones_like(through_ref)
        sum_ref[...] = jnp.zeros_like(sum_ref)

    inside = jnp.where(block > 0, 1, 0)
    per = rows // BLK
    above = jnp.maximum(per * block - 1, 0)

    def mask_of(t):
        parts = [
            jnp.broadcast_to(splat(occ[0, per * block + b, t]), (BLK, LANES)) for b in range(per)
        ]
        return jnp.concatenate(parts, axis=0)

    mask = [mask_of(t) for t in range(tiles)]
    lead_mask = [splat(occ[0, above, t] * inside) for t in range(tiles)]
    state = (through_ref, sum_ref)
    refs = (frac_vertical, extinction, slice_total)

    def one(u, _):
        s = part * count + u
        parts = []
        for t in range(tiles):
            lanes = slice(t * LANES, (t + 1) * LANES)
            lead = lead_ref[0, u, :, lanes] * lead_mask[t]
            parts.append(jnp.concatenate([lead, x_ref[0, u, :, lanes] * mask[t]], axis=0))
        for t in range(1, tiles):
            pair = jnp.concatenate([parts[t - 1], parts[t]], axis=1)
            x = jnp.dot(pair, weights[s], preferred_element_type=F32)
            shade(s, x[8:], (t - 1) * rows, state, refs)
        return 0

    over_slices(count, one)

    @pl.when(part == pl.num_programs(1) - 1)
    def _():
        swap = lax.axis_index("depth") % 2 == 1
        for t in range(tiles - 1):
            finish(state, gain[...], swap, out_keep, out_send, t)


def small_specs():
    return [pl.BlockSpec(memory_space=SMEM)] * 5 + [whole()]


def interior(density, small, rank, slice_total):
    _, slices, rows, cols = density.shape
    step = 2 * BLK
    width = cols - LANES
    pieces = step // (2 * PIECE)
    image = jax.ShapeDtypeStruct((rows // (2 * PIECE), 2, PIECE, width), F32)
    return pl.pallas_call(
        functools.partial(interior_kernel, slice_total),
        grid=(rows // step, PARTS),
        in_specs=small_specs()
        + [pl.BlockSpec(memory_space=SMEM)]
        + [
            pl.BlockSpec((1, slices // PARTS, step, cols), lambda b, g: (0, g, b, 0)),
            pl.BlockSpec(
                (1, slices // PARTS, 16, cols),
                lambda b, g: (0, g, jnp.maximum(b * (step // 16) - 1, 0), 0),
            ),
        ],
        out_specs=[
            pl.BlockSpec((pieces, 2, PIECE, width), lambda b, g: (b, 0, 0, 0))
        ]
        * 2
        + [
            pl.BlockSpec((slices, 2 * LANES, LANES), lambda b, g: (0, 0, 0)),
            pl.BlockSpec((16, cols), lambda b, g: (0, 0)),
        ],
        out_shape=[
            image,
            image,
            jax.ShapeDtypeStruct((slices, 2 * LANES, LANES), BF16),
            jax.ShapeDtypeStruct((16, cols), F32),
        ],
        scratch_shapes=[pltpu.VMEM((step * (width // LANES), LANES), F32)] * 2,
        compiler_params=pltpu.CompilerParams(vmem_limit_bytes=32 * 2**20),
        name="interior",
    )(*small, rank, density, density)


def border_kernel(
    start, slice_total, occ, offset, frac_lateral, frac_vertical, extinction, gain, weights,
    first_ref, last_ref, first_lead, last_lead, right_ref, left_ref, right_lead, left_lead,
    out_keep, out_send, through_ref, sum_ref,
):
    slices, half = first_ref.shape[1], BLK // 2
    last_tile = occ.shape[2] - 1
    follows = jnp.where(lax.axis_index("lat") < lax.axis_size("lat") - 1, 1, 0)
    own_lanes = lax.broadcasted_iota(jnp.int32, (1, LANES), 1) >= HALF
    refs = (frac_vertical, extinction, slice_total)
    state = (through_ref, sum_ref)
    through_ref[...] = jnp.ones_like(through_ref)
    sum_ref[...] = jnp.zeros_like(sum_ref)
    blocks = first_ref.shape[2] // BLK
    masks = []
    for b in range(start - 1, start + blocks):
        inside = b >= 0
        masks.append(
            (
                splat(occ[0, b, 0] if inside else 0.0),
                splat(occ[0, b, last_tile] * follows if inside else 0.0),
            )
        )
    zero = jnp.zeros((16, LANES), BF16)

    def one(s, _):
        before, own = weights[s, :LANES], weights[s, LANES:]
        turn = lambda w: jnp.concatenate([w[HALF:], w[:HALF]], axis=0)
        near = jnp.concatenate([before, own], axis=0)
        far_left = jnp.concatenate([turn(before), own], axis=0)
        far_right = jnp.concatenate([before, turn(own)], axis=0)

        def halves(ref, side, top, above):
            parts = [above] if above is not None else []
            for b in range(blocks):
                at = slice(b * BLK + top, b * BLK + top + half)
                parts.append(ref[0, s, at] * masks[b + 1][side])
            return jnp.concatenate(parts, axis=0) if len(parts) > 1 else parts[0]

        def lateral(first, last, right, left, w_left, w_right):
            here = jnp.dot(
                jnp.concatenate([left, first], axis=1), w_left, preferred_element_type=F32
            )
            there = jnp.dot(
                jnp.concatenate([last, right], axis=1), w_right, preferred_element_type=F32
            )
            return jnp.where(own_lanes, here, there)

        right, left = right_ref[s], left_ref[s]
        x_near = lateral(
            halves(first_ref, 0, 0, None), halves(last_ref, 1, 0, None), right, left, near, near
        )
        x_far = lateral(
            halves(first_ref, 0, half, first_lead[0, s] * masks[0][0]),
            halves(last_ref, 1, half, last_lead[0, s] * masks[0][1]),
            jnp.concatenate([right_lead[s] if start else zero, right], axis=0),
            jnp.concatenate([left_lead[s] if start else zero, left], axis=0),
            far_left,
            far_right,
        )
        for b in range(blocks):
            rows = slice(b * half, (b + 1) * half)
            far_rows = slice(b * half + 16, (b + 1) * half + 16)
            lead = x_far[b * half + 8 : b * half + 16]
            x = jnp.concatenate([lead, x_near[rows], x_far[far_rows]], axis=0)
            shade(s, x, b * BLK, state, refs)
        return 0

    over_slices(slices, one)
    swap = lax.axis_index("depth") % 2 == 1
    finish(state, gain[...], swap, out_keep, out_send, 0)


def border(density, small, weights, halos, above, start, blocks, slice_total):
    _, slices, _, cols = density.shape
    step = blocks * BLK
    last = cols // LANES - 1
    per = BLK // 16

    def body(column):
        shape = tuple(pl.Element(n) for n in (1, slices, step, LANES))
        return pl.BlockSpec(shape, lambda i: (0, 0, start * BLK, column * LANES))

    def lead(column):
        return pl.BlockSpec(
            (1, slices, 16, LANES), lambda i: (0, 0, max(start * per - 1, 0), column)
        )

    halo = pl.BlockSpec((slices, step // 2, LANES), lambda i: (0, 0, 0))
    last_rows = above[0].shape[1] // 16 - 1
    halo_lead = pl.BlockSpec((slices, 16, LANES), lambda i: (0, last_rows, 0))
    shape = (step // (2 * PIECE), 2, PIECE, LANES)
    image = jax.ShapeDtypeStruct(shape, F32)
    return pl.pallas_call(
        functools.partial(border_kernel, start, slice_total),
        grid=(1,),
        in_specs=small_specs()
        + [pl.BlockSpec((slices, 2 * LANES, LANES), lambda i: (0, 0, 0))]
        + [body(0), body(last), lead(0), lead(last), halo, halo, halo_lead, halo_lead],
        out_specs=[pl.BlockSpec(shape, lambda i: (0, 0, 0, 0))] * 2,
        out_shape=[image, image],
        scratch_shapes=[pltpu.VMEM((step, LANES), F32)] * 2,
        compiler_params=pltpu.CompilerParams(vmem_limit_bytes=32 * 2**20),
        name=f"border{start}",
    )(*small, weights, density, density, density, density, *halos, *above)


def over(mine, other, in_front):
    color = mine[0] * (1.0 - (1.0 - in_front) * other[1]) + other[0] * (1.0 - in_front * mine[1])
    return color, mine[1] + (1.0 - mine[1]) * other[1]


def over_cores(keep, send, flags):
    count = lax.axis_size("depth")
    other = lax.ppermute(send, "depth", [(i, i ^ 1) for i in range(count)])
    front = flags[0, : keep.shape[3]]
    return jnp.stack(over((keep[:, 0], keep[:, 1]), (other[:, 0], other[:, 1]), front), axis=1)


def over_chips(pieces, flags):
    count = lax.axis_size("depth")
    chips = count // 2
    pieces = (pieces * WIRE_SCALE).astype(WIRE)
    groups = [[2 * i + core for i in range(chips)] for core in range(2)]
    pieces = lax.all_to_all(
        pieces, "depth", 0, 0, axis_index_groups=groups, tiled=True
    )
    pieces = pieces.astype(F32) * (1.0 / WIRE_SCALE)
    level = [(pieces[i, 0], pieces[i, 1]) for i in range(chips)]
    row = 1
    while len(level) > 1:
        half = len(level) // 2
        level = [over(level[2 * i], level[2 * i + 1], flags[row + i]) for i in range(half)]
        row += half
    return level[0]


def shards(
    density, occupancy, shear_offsets, frac_lateral, frac_vertical, extinction, slab_gain, view_rank
):
    _, slices, rows, cols = density.shape
    slice_total = lax.axis_size("depth") * slices
    lat = lax.axis_size("lat")
    density = pltpu.with_memory_space_constraint(density, pltpu.HBM)
    small = (occupancy, shear_offsets, frac_lateral, frac_vertical, extinction, slab_gain[None])
    blocks = rows // BLK
    half = blocks - TAIL
    rightwards = [(x, x + 1) for x in range(lat - 1)]
    leftwards = [(x, (x - 1) % lat) for x in range(lat)]
    halos = []
    for first, count in ((0, half), (half, blocks - half)):
        to_left, to_right = edge_strips(density, occupancy, first, count)
        halos.append(
            (lax.ppermute(to_left, "lat", leftwards), lax.ppermute(to_right, "lat", rightwards))
        )
    keep, send, weights, flags = interior(density, small, view_rank, slice_total)
    top = border(density, small, weights, halos[0], halos[0], 0, half, slice_total)
    send, top = lax.optimization_barrier((send, top))
    inner = over_cores(keep, send, flags)
    bottom = border(density, small, weights, halos[1], halos[0], half, blocks - half, slice_total)
    keep, send = (jnp.concatenate(p, axis=0) for p in zip(top, bottom))
    edge = over_cores(keep, send, flags)
    color, alpha = over_chips(jnp.concatenate([edge, inner], axis=3), flags)
    image = jnp.stack([color, alpha])
    moved = lax.ppermute(image[:, :, :LANES], "lat", [(x, (x + 1) % lat) for x in range(lat)])
    lane = jnp.arange(LANES, dtype=jnp.int32)
    first = jnp.where(lane < HALF, moved, image[:, :, :LANES])
    return tuple(jnp.concatenate([first[i], image[i, :, LANES:]], axis=1) for i in range(2))


def solution(mesh):
    placed = (
        P("depth", None, None, "lat"),
        P("depth", None, "lat"),
        P("depth", None),
        P("depth", None),
        P("depth", None),
        P("depth", None),
        P("depth"),
        P(),
    )
    return jax.shard_map(
        shards,
        mesh=mesh,
        in_specs=placed,
        out_specs=(P("depth", "lat"), P("depth", "lat")),
        check_vma=False,
    )
```
